32 devices in a mesh: clip: 4 (over x, core), seq: 2 (over y), tensor: 4 (over z).
Axes of the slice: x: 2, y: 2, z: 4, core: 2. Of those that a mesh axis runs over, the one named last changes fastest.
Arguments:
- clips_in: bfloat16 [16, 8, 4, 16, 384], P('clip', None, 'seq', 'tensor'), may hold values from -6 to 6
- cotangent: bfloat16 [16, 8, 2, 8, 768], P('clip', None, 'seq', 'tensor'), may hold values from -6 to 6
- resets: int32 [16], replicated, may hold values 0 or 1
- videos: int32 [16], replicated, may hold values from 0 to 3, never falling along the last dimension, each value on 1 to 8 neighbouring positions
- attend_gain_a: float32 [384], replicated, may hold values from 0.5 to 1.5
- project_a: bfloat16 [384, 1152], replicated, may hold values from -0.4375 to 0.4375
- pooling_a: float32 [2, 4, 384], replicated, may hold values from 0.2 to 0.6
- squeeze_a: float32 [2, 4, 384], replicated, may hold values from 0.1 to 0.5
- offsets_a: float32 [4, 31], replicated, may hold values from -4 to 4
- output_a: bfloat16 [384, 384], replicated, may hold values from -0.21875 to 0.21875
- mixer_gain_a: float32 [384], replicated, may hold values from 0.5 to 1.5
- expand_a: bfloat16 [384, 1536], P(None, 'tensor'), may hold values from -0.3125 to 0.3125
- reduce_a: bfloat16 [1536, 384], P('tensor'), may hold values from -0.15625 to 0.15625
- attend_gain_b: float32 [384], replicated, may hold values from 0.5 to 1.5
- project_b: bfloat16 [384, 2304], replicated, may hold values from -0.4375 to 0.4375
- pooling_b: float32 [3, 4, 768], replicated, may hold values from 0.2 to 0.6
- squeeze_b: float32 [2, 4, 768], replicated, may hold values from 0.1 to 0.5
- offsets_b: float32 [8, 31], replicated, may hold values from -4 to 4
- output_b: bfloat16 [768, 768], replicated, may hold values from -0.15625 to 0.15625
- shortcut_b: bfloat16 [384, 768], replicated, may hold values from -0.3125 to 0.3125
- mixer_gain_b: float32 [768], replicated, may hold values from 0.5 to 1.5
- expand_b: bfloat16 [768, 3072], P(None, 'tensor'), may hold values from -0.21875 to 0.21875
- reduce_b: bfloat16 [3072, 768], P('tensor'), may hold values from -0.109375 to 0.109375
Outputs:
- out_field: float32 [16, 8, 2, 8, 768], P('clip', None, 'seq', 'tensor')
- grad_input: float32 [16, 8, 4, 16, 384], P('clip', None, 'seq', 'tensor')
- grad_attend_gain_a: float32 [384], replicated
- grad_project_a: float32 [384, 1152], P('tensor')
- grad_pooling_a: float32 [2, 4, 384], replicated
- grad_squeeze_a: float32 [2, 4, 384], replicated
- grad_offsets_a: float32 [4, 31], replicated
- grad_output_a: float32 [384, 384], P('tensor')
- grad_mixer_gain_a: float32 [384], replicated
- grad_expand_a: float32 [384, 1536], P(None, 'tensor')
- grad_reduce_a: float32 [1536, 384], P('tensor')
- grad_attend_gain_b: float32 [384], replicated
- grad_project_b: float32 [384, 2304], P('tensor')
- grad_pooling_b: float32 [3, 4, 768], replicated
- grad_squeeze_b: float32 [2, 4, 768], replicated
- grad_offsets_b: float32 [8, 31], replicated
- grad_output_b: float32 [768, 768], P('tensor')
- grad_shortcut_b: float32 [384, 768], P('tensor')
- grad_mixer_gain_b: float32 [768], replicated
- grad_expand_b: float32 [768, 3072], P(None, 'tensor')
- grad_reduce_b: float32 [3072, 768], P('tensor')
The draws below stay inside these ranges and needn't reach their ends.
Inputs may be any that keep to these rules, and one draw needn't show every extreme that they name: `videos`: video ids never fall along the clips; a video has 1 to 8 clips in a row, one has exactly 8.
All inputs are finite; a program needn't handle non-finite values.
Results may differ from the reference program's by a relative error of at most 0.029.
Values may be sent and summed in bfloat16 or wider, within the bound.
No kernel may reach another device: no remote copies, remote signals or barrier semaphores. Data moves between devices by JAX's collectives and lax.ppermute only.
A program may use at most 128 MiB of HBM per device.

```python
import math
import jax
import jax.numpy as jnp
import numpy as np
from jax import lax

C1 = 384
HEADS1 = 4
C2 = 768
HEADS2 = 8
F1 = 1536
F2 = 3072
T_SIZE = 8
W = 16
CLIPS = 16
H = 4
REL = 31


def with_ends(drawn, rng, smallest, high):
    dims = drawn.shape
    place = [jax.random.randint(jax.random.fold_in(rng, axis), (), 0, dims[axis]) for axis in range(len(dims))]
    drawn = drawn.at[tuple(place)].set(smallest)
    longest = dims.index(max(dims))
    place[longest] = (place[longest] + 1) % dims[longest]
    return drawn.at[tuple(place)].set(high)


def levels(rng, dims, shards, low, high):
    factor_of = 1.0
    for dim, shards_of in shards:
        draws = jax.random.uniform(jax.random.fold_in(jax.random.fold_in(rng, 6), dim), (shards_of,), jnp.float32, low / len(shards), high / len(shards))
        factor_of = factor_of * jnp.repeat(jnp.exp(draws), dims[dim] // shards_of).reshape((-1,) + (1,) * (len(dims) - 1 - dim))
    return factor_of


def split_up(amount, total, bound, lean):
    weights = [(1 << 20) // math.isqrt(standing ** lean) + 1 for standing in range(2, amount + 1)]
    spare, counts = total - bound - (amount - 1), [1] * (amount - 1)
    while spare > 0:
        candidates = [i for i in range(amount - 1) if counts[i] < bound]
        pool, remaining = sum([weights[i] for i in candidates]), spare
        for i in candidates:
            extra = min(bound - counts[i], max(1, remaining * weights[i] // pool), spare)
            counts[i] = counts[i] + extra
            spare = spare - extra
    return np.array([bound] + counts)


def ragged(key, number_of, total, most, skew):
    if number_of == 2:
        one = jax.random.randint(key, (), max(1, total - most), min(most, total - 1) + 1)
        return jnp.stack([one, total - one])
    lengths = jnp.asarray(split_up(number_of, total, most, skew), jnp.int32)
    pairs = (number_of - 1) // 2
    giver, taker = lengths[1:1 + 2 * pairs:2], lengths[2:2 + 2 * pairs:2]
    slack = jnp.minimum(giver - 1, most - taker)
    shifted = jax.random.randint(jax.random.fold_in(key, 1), (pairs,), 0, 1 << 20) % (slack + 1)
    lengths = lengths.at[1:1 + 2 * pairs:2].set(giver - shifted).at[2:2 + 2 * pairs:2].set(taker + shifted)
    return lengths[jax.random.permutation(jax.random.fold_in(key, 2), number_of)]


def gaussian(key, dims, scale, reach, pieces=(), kind=jnp.bfloat16):
    level = levels(key, dims, pieces, -0.22, 0.18) if pieces else 1.0
    values = jax.random.normal(key, dims, jnp.float32) * scale * level
    return jnp.minimum(jnp.maximum(values, -reach), reach).astype(kind)


def setup_inputs(seed: int = 0) -> dict:
    seeds = jax.random.split(jax.random.key(seed), 24)
    return {
        "clips_in": gaussian(seeds[0], (CLIPS, T_SIZE, H, W, C1), 1.0, 6.0, ((0, 4), (2, 2), (3, 4))),
        "cotangent": gaussian(seeds[1], (CLIPS, T_SIZE, H // 2, W // 2, C2), 1.0, 6.0, ((0, 4), (2, 2), (3, 4))),
        "resets": with_ends((jax.random.randint(seeds[2], (CLIPS,), 0, 8) < 1).astype(jnp.int32), jax.random.fold_in(seeds[2], 1), 0, 1),
        "videos": jnp.searchsorted(jnp.cumsum(ragged(seeds[3], CLIPS // 4, CLIPS, 8, 0)), jnp.arange(CLIPS), side="right").astype(jnp.int32),
        "attend_gain_a": jnp.clip(1.0 + 0.1 * jax.random.normal(seeds[4], (C1,), jnp.float32), 0.5, 1.5),
        "project_a": gaussian(seeds[5], (C1, 3 * C1), (C1 // 2) ** -0.5, 0.4375),
        "pooling_a": jnp.clip(jax.random.uniform(seeds[6], (2, 4, C1), jnp.float32, 0.2, 0.6), 0.2, 0.6),
        "squeeze_a": jnp.clip(jax.random.uniform(seeds[7], (2, 4, C1), jnp.float32, 0.1, 0.5), 0.1, 0.5),
        "offsets_a": gaussian(seeds[8], (HEADS1, REL), 1.0, 4.0, (), jnp.float32),
        "output_a": gaussian(seeds[9], (C1, C1), (2 * C1) ** -0.5, 0.21875),
        "mixer_gain_a": jnp.clip(1.0 + 0.1 * jax.random.normal(seeds[10], (C1,), jnp.float32), 0.5, 1.5),
        "expand_a": gaussian(seeds[11], (C1, F1), C1 ** -0.5, 0.3125, ((1, 4),)),
        "reduce_a": gaussian(seeds[12], (F1, C1), F1 ** -0.5, 0.15625, ((0, 4),)),
        "attend_gain_b": jnp.clip(1.0 + 0.1 * jax.random.normal(seeds[13], (C1,), jnp.float32), 0.5, 1.5),
        "project_b": gaussian(seeds[14], (C1, 3 * C2), (C1 // 2) ** -0.5, 0.4375),
        "pooling_b": jnp.clip(jax.random.uniform(seeds[15], (3, 4, C2), jnp.float32, 0.2, 0.6), 0.2, 0.6),
        "squeeze_b": jnp.clip(jax.random.uniform(seeds[16], (2, 4, C2), jnp.float32, 0.1, 0.5), 0.1, 0.5),
        "offsets_b": gaussian(seeds[17], (HEADS2, REL), 1.0, 4.0, (), jnp.float32),
        "output_b": gaussian(seeds[18], (C2, C2), (2 * C2) ** -0.5, 0.15625),
        "shortcut_b": gaussian(seeds[19], (C1, C2), C1 ** -0.5, 0.3125),
        "mixer_gain_b": jnp.clip(1.0 + 0.1 * jax.random.normal(seeds[20], (C2,), jnp.float32), 0.5, 1.5),
        "expand_b": gaussian(seeds[21], (C2, F2), C2 ** -0.5, 0.21875, ((1, 4),)),
        "reduce_b": gaussian(seeds[22], (F2, C2), F2 ** -0.5, 0.109375, ((0, 4),)),
    }


HIGHEST = lax.Precision.HIGHEST
EPSILON = 1e-06
MASKED = -1000000000.0
LOG_FOUR = 1.3862943611198906

@jax.custom_vjp
def low(v):
    return lax.optimization_barrier(v.astype(jnp.bfloat16)).astype(jnp.float32)

@jax.custom_vjp
def low_back(v):
    return v

def low_keep(v):
    return (low(v), None)

def low_pass(kept, grad):
    return (grad,)

def back_keep(v):
    return (v, None)

def back_low(kept, grad):
    return (low(grad),)
low.defvjp(low_keep, low_pass)
low_back.defvjp(back_keep, back_low)

def widen(value):
    return value.astype(jnp.float32)

def matmul(left, right):
    return jnp.dot(left, right, precision=HIGHEST)

def layer_norm(field, gain):
    mean = lax.optimization_barrier(jnp.mean(field, axis=-1, keepdims=True))
    centered = field - mean
    inverse = lax.rsqrt(lax.optimization_barrier(jnp.mean(centered * centered, axis=-1, keepdims=True)) + EPSILON)
    return centered * inverse * gain

def pool_grid(field, weights):
    total = field[..., 0::2, 0::2, :] * weights[0]
    total = total + field[..., 0::2, 1::2, :] * weights[1]
    total = total + field[..., 1::2, 0::2, :] * weights[2]
    total = total + field[..., 1::2, 1::2, :] * weights[3]
    return total

def compress_time(field, weights):
    total = field[..., 0::4, :, :, :] * weights[0]
    total = total + field[..., 1::4, :, :, :] * weights[1]
    total = total + field[..., 2::4, :, :, :] * weights[2]
    total = total + field[..., 3::4, :, :, :] * weights[3]
    return total

def smooth_max(field):
    stacked = jnp.stack([field[..., 0::2, 0::2, :], field[..., 0::2, 1::2, :], field[..., 1::2, 0::2, :], field[..., 1::2, 1::2, :]], axis=0)
    highest = lax.optimization_barrier(jnp.max(stacked, axis=0))
    return highest + jnp.log(lax.optimization_barrier(jnp.sum(jnp.exp(stacked - highest), axis=0))) - LOG_FOUR

def gaussian_gate(values):
    return jax.nn.gelu(values, approximate=False)

def memory_valid(resets, videos, clip_ids):
    before = jnp.maximum(clip_ids - 1, 0)
    earlier = jnp.maximum(clip_ids - 2, 0)
    first = (clip_ids >= 1) & (videos[clip_ids] == videos[before]) & (resets[clip_ids] == 0)
    second = first & (clip_ids >= 2) & (videos[before] == videos[earlier]) & (resets[before] == 0)
    return (first, second)

def key_layout(count, per_frame, frames):
    index = jnp.arange(count, dtype=jnp.int32)
    current = frames * per_frame
    memory = frames // 4 * per_frame
    offset = index % (current + 2 * memory)
    first = offset - current
    second = first - memory
    times = jnp.where(offset < current, offset // per_frame, jnp.where(first < memory, 4 * (first // per_frame) - frames, 4 * (second // per_frame) - 2 * frames))
    kind = jnp.where(offset < current, 0, jnp.where(first < memory, 1, 2))
    return (times, kind)

def relative_onehot(times, frames, entries):
    index = jnp.arange(frames, dtype=jnp.int32)[:, None] - times[None, :] + frames - 1
    return (index[:, :, None] == jnp.arange(entries, dtype=jnp.int32)[None, None, :]).astype(jnp.float32)

def key_mask(kind, first_ok, second_ok):
    return (kind[None, :] == 0) | (kind[None, :] == 1) & first_ok[:, None] | (kind[None, :] == 2) & second_ok[:, None]

def attend_clip(query_clip, keys_clip, mask_clip, bias, heads):
    rows, width = query_clip.shape
    size = width // heads
    frames = bias.shape[1]
    query_heads = query_clip.reshape(rows, heads, size)
    key_heads = keys_clip[:, :width].reshape(-1, heads, size)
    value_heads = keys_clip[:, width:].reshape(-1, heads, size)
    scores = jnp.einsum('qhd,khd->hqk', query_heads, key_heads, precision=HIGHEST) * size ** (-0.5)
    scores = scores.reshape(heads, frames, rows // frames, -1) + bias[:, :, None, :]
    scores = low_back(scores)
    scores = jnp.where(mask_clip[None, None, None, :], scores, MASKED).reshape(heads, rows, -1)
    highest = lax.optimization_barrier(jnp.max(scores, axis=-1, keepdims=True))
    expd = jnp.exp(scores - highest)
    probs = low(expd / lax.optimization_barrier(jnp.sum(expd, axis=-1, keepdims=True)))
    mixed = low_back(jnp.einsum('hqk,khd->qhd', probs, value_heads, precision=HIGHEST))
    return mixed.reshape(rows, width) + query_clip

def block_forward(field, params, first_ok, second_ok, pooled_query):
    gain_in, in_weights, pool_weights, squeeze_weights, table, out_weights, skip_weights, gain_mid, up_weights, down_weights = params
    clips, frames, height, breadth, width_in = field.shape
    width = out_weights.shape[0]
    heads = table.shape[0]
    normed_r = low(layer_norm(field, gain_in))
    flat = normed_r.reshape(-1, width_in)
    projected = low_back(matmul(flat, in_weights)).reshape(clips, frames, height, breadth, 3 * width)
    if pooled_query:
        query = pool_grid(projected[..., :width], pool_weights[0])
    else:
        query = projected[..., :width]
    query_r = low(query)
    pair_weights = jnp.concatenate([pool_weights[-2], pool_weights[-1]], axis=-1)
    pair_squeeze = jnp.concatenate([squeeze_weights[0], squeeze_weights[1]], axis=-1)
    pooled = pool_grid(projected[..., width:], pair_weights)
    compact = compress_time(pooled, pair_squeeze)
    pooled_r = low(pooled).reshape(clips, -1, 2 * width)
    compact_r = low(compact).reshape(clips, -1, 2 * width)
    empty = jnp.zeros_like(compact_r[:1])
    first_memory = jnp.concatenate([empty, compact_r[:-1]], axis=0)
    second_memory = jnp.concatenate([empty, empty, compact_r[:-2]], axis=0)
    keys_all = jnp.concatenate([pooled_r, first_memory, second_memory], axis=1)
    per_frame = pooled.shape[2] * pooled.shape[3]
    times, kind = key_layout(keys_all.shape[1], per_frame, frames)
    onehot = relative_onehot(times, frames, table.shape[1])
    bias = jnp.einsum('hr,tkr->htk', table, onehot, precision=HIGHEST)
    mask = key_mask(kind, first_ok, second_ok)
    query_rows = query_r.reshape(clips, -1, width)

    def one_clip(items):
        return attend_clip(items[0], items[1], items[2], bias, heads)
    mixed = lax.map(jax.checkpoint(one_clip), (query_rows, keys_all, mask))
    branch = low_back(matmul(low(mixed).reshape(-1, width), out_weights))
    if pooled_query:
        skip_raw = low_back(matmul(flat, skip_weights)).reshape(clips, frames, height, breadth, width)
        base = smooth_max(skip_raw)
    else:
        base = field
    middle = base.reshape(-1, width) + branch
    normed2_r = low(layer_norm(middle, gain_mid))
    hidden_pre = low_back(matmul(normed2_r, up_weights))
    hidden_r = low(gaussian_gate(hidden_pre))
    mlp_out = low_back(matmul(hidden_r, down_weights))
    return (middle + mlp_out).reshape(base.shape)

def reference(clips_in, cotangent, resets, videos, attend_gain_a, project_a, pooling_a, squeeze_a, offsets_a, output_a, mixer_gain_a, expand_a, reduce_a, attend_gain_b, project_b, pooling_b, squeeze_b, offsets_b, output_b, shortcut_b, mixer_gain_b, expand_b, reduce_b):
    clip_ids = jnp.arange(CLIPS, dtype=jnp.int32)
    first_ok, second_ok = memory_valid(resets, videos, clip_ids)
    weights_a = (widen(attend_gain_a), widen(project_a), widen(pooling_a), widen(squeeze_a), widen(offsets_a), widen(output_a), None, widen(mixer_gain_a), widen(expand_a), widen(reduce_a))
    weights_b = (widen(attend_gain_b), widen(project_b), widen(pooling_b), widen(squeeze_b), widen(offsets_b), widen(output_b), widen(shortcut_b), widen(mixer_gain_b), widen(expand_b), widen(reduce_b))

    def forward(field, params_a, params_b):
        middle = block_forward(field, params_a, first_ok, second_ok, False)
        return block_forward(middle, params_b, first_ok, second_ok, True)
    result, pullback = jax.vjp(forward, widen(clips_in), weights_a, weights_b)
    grad_field, grads_a, grads_b = pullback(widen(cotangent))
    return (result, grad_field, grads_a[0], grads_a[1], grads_a[2], grads_a[3], grads_a[4], grads_a[5], grads_a[7], grads_a[8], grads_a[9], grads_b[0], grads_b[1], grads_b[2], grads_b[3], grads_b[4], grads_b[5], grads_b[6], grads_b[7], grads_b[8], grads_b[9])
```

```python
import functools

import jax
import jax.numpy as jnp
import numpy as np
from jax import lax
from jax.experimental import pallas as pl
from jax.experimental.pallas import tpu as pltpu
from jax.sharding import Mesh
from jax.sharding import PartitionSpec as P

F32 = jnp.float32
BF16 = jnp.bfloat16
HIGHEST = lax.Precision.HIGHEST
EPSILON = 1e-06
MASKED = -1000000000.0
LOG_FOUR = 1.3862943611198906
SIZE = 96
LANES = 384
INTERPRET = False
PLANE = ("chip", "core", "seq")
EVERY = ("chip", "core", "seq", "tensor")


def log2(n):
    return n.bit_length() - 1


def mm(left, right):
    return jnp.dot(left, right, preferred_element_type=F32)


def mm_tl(left, right):
    return lax.dot_general(left, right, (((0,), (0,)), ((), ())), preferred_element_type=F32)


def mm_tr(left, right):
    return lax.dot_general(left, right, (((1,), (1,)), ((), ())), preferred_element_type=F32)


def norm(field):
    mean = jnp.mean(field, axis=-1, keepdims=True)
    centered = field - mean
    inverse = lax.rsqrt(jnp.mean(centered * centered, axis=-1, keepdims=True) + EPSILON)
    return centered * inverse, inverse


def norm_back(grad, gain, normed, inverse):
    scaled = grad * gain
    field = inverse * (
        scaled
        - jnp.mean(scaled, axis=-1, keepdims=True)
        - normed * jnp.mean(scaled * normed, axis=-1, keepdims=True)
    )
    return field, jnp.sum(grad * normed, axis=0, keepdims=True)


def gelu(values):
    return 0.5 * values * (1.0 + lax.erf(values * 0.7071067811865476))


def gelu_both(values):
    half = 0.5 * (1.0 + lax.erf(values * 0.7071067811865476))
    slope = half + values * jnp.exp(-0.5 * values * values) * 0.3989422804014327
    return values * half, slope


def blocks(values, count):
    rows = values.shape[0] // count
    return [values[i * rows : (i + 1) * rows] for i in range(count)]


def pool(values, weights):
    parts = blocks(values, 4)
    total = parts[0] * weights[0:1]
    for p in range(1, 4):
        total = total + parts[p] * weights[p : p + 1]
    return total


class Plan:
    def __init__(self, seq, tensor, shape):
        clips, frames, rows, cols, _ = shape
        self.seq, self.tensor = seq, tensor
        assert clips == tensor and frames % seq == 0 and rows % 2 == 0 and cols % 2 == 0
        self.all_frames = frames
        self.frames = frames // seq
        self.rows, self.cols = rows, cols
        self.group = seq * tensor
        self.cells = self.group * rows * cols // 4
        self.pooled = self.frames * self.cells
        self.tokens = 4 * self.pooled
        self.local_squeeze = self.frames % 4 == 0
        self.memory = frames // 4 * self.cells
        self.own = seq * self.pooled
        self.keys = self.own + 2 * self.memory
        for n in (self.cells, self.pooled, self.memory, self.own, self.frames, seq):
            assert n == 1 << log2(n)

    def arrange(self):
        take = np.arange(self.tokens).reshape(
            self.group, self.frames, self.rows // 2, 2, self.cols // 2, 2
        )
        per = self.frames * self.rows * self.cols
        half = per // 4 * 2
        step = per + half
        x_rows = take // per * step + take % per
        x_rows = x_rows.transpose(3, 5, 1, 0, 2, 4).reshape(-1)
        cot = np.arange(self.pooled).reshape(self.group, self.frames, -1)
        low = cot // (per // 4) * step + per + cot % (per // 4) * 2
        low = low.transpose(1, 0, 2).reshape(-1)
        order = np.concatenate([x_rows, low, low + 1])
        return (order[:, None] == np.arange(self.group * step)[None, :]).astype(np.float32)


def clip_scalars(plan, resets, videos):
    s = lax.axis_index("seq")
    chip = lax.axis_index("chip") * lax.axis_size("core") + lax.axis_index("core")
    g = chip * plan.tensor + lax.axis_index("tensor")
    before = jnp.maximum(g - 1, 0)
    earlier = jnp.maximum(g - 2, 0)
    first = (g >= 1) & (videos[g] == videos[before]) & (resets[g] == 0)
    second = first & (g >= 2) & (videos[before] == videos[earlier]) & (resets[before] == 0)
    return s, first.astype(jnp.int32), second.astype(jnp.int32)


def key_facts(plan, s, first, second):
    k = lax.broadcasted_iota(jnp.int32, (1, plan.keys), 1)
    own_time = ((s ^ (k >> log2(plan.pooled))) << log2(plan.frames)) + (
        (k & (plan.pooled - 1)) >> log2(plan.cells)
    )
    m = k - plan.own
    late = (m >> log2(plan.memory)) > 0
    g = (m & (plan.memory - 1)) >> log2(plan.cells)
    if plan.local_squeeze:
        each = log2(plan.frames // 4)
        squeezed = ((s ^ (g >> each)) << each) + (g & (plan.frames // 4 - 1))
    else:
        squeezed = (s >> log2(4 // plan.frames)) ^ g
    kind = jnp.where(m < 0, 0, jnp.where(late, 2, 1))
    time = jnp.where(m < 0, own_time, 4 * squeezed - plan.all_frames * kind)
    counts = jnp.where(kind == 0, 1, jnp.where(kind == 1, first, second))
    return time, counts


def offset_onehot(plan, s, time, frame):
    index = s * plan.frames + frame - time + plan.all_frames - 1
    rows = lax.broadcasted_iota(jnp.int32, (128, plan.keys), 0)
    return jnp.where(rows == index, 1.0, 0.0).astype(F32)


def head_mask(width, head):
    lane = lax.broadcasted_iota(jnp.int32, (1, width), 1)
    inside = (lane >= head * SIZE) & (lane < (head + 1) * SIZE)
    return jnp.where(inside, 1.0, 0.0).astype(F32)


def attend(plan, query, keys, values, table, heads, probs_ref, scalars):
    s, first, second = scalars
    rows, width = query.shape
    places = rows // plan.pooled
    time, counts = key_facts(plan, s, first, second)
    biases = []
    for f in range(plan.frames):
        onehot = offset_onehot(plan, s, time, f)
        bias = jnp.dot(table, onehot, precision=HIGHEST, preferred_element_type=F32)
        biases.append(jnp.where(counts > 0, bias, MASKED))
    total = query.astype(F32)
    for h in range(heads):
        mask = head_mask(width, h)
        scores = mm_tr(query * mask.astype(BF16), keys) * SIZE ** (-0.5)
        bias = jnp.concatenate(
            [jnp.broadcast_to(b[h : h + 1], (plan.cells, plan.keys)) for b in biases] * places, axis=0
        )
        scores = scores + bias
        scores = jnp.exp(scores - jnp.max(scores, axis=-1, keepdims=True))
        probs = scores * (1.0 / jnp.sum(scores, axis=-1, keepdims=True))
        probs = probs.astype(BF16)
        probs_ref[h * rows : (h + 1) * rows] = probs
        total = total + mm(probs, values) * mask
    return total


def attend_back(plan, grad, query, keys, values, probs_ref, heads, bias_ref, table_ref, scalars):
    s, first, second = scalars
    rows, width = query.shape
    places = rows // plan.pooled
    grad_r = grad.astype(BF16)
    grad_query = grad
    grad_keys = jnp.zeros((plan.keys, width), F32)
    grad_values = jnp.zeros((plan.keys, width), F32)
    bias_ref[...] = jnp.zeros(bias_ref.shape, F32)
    for h in range(heads):
        mask = head_mask(width, h)
        mask_r = mask.astype(BF16)
        grad_head = grad_r * mask_r
        query_head = query * mask_r
        probs_r = probs_ref[h * rows : (h + 1) * rows]
        probs = probs_r.astype(F32)
        grad_probs = mm_tr(grad_head, values)
        weighted = probs * grad_probs
        grad_scores = weighted - probs * jnp.sum(weighted, axis=-1, keepdims=True)
        for f in range(plan.frames):
            part = grad_scores[f * plan.cells : (f + 1) * plan.cells]
            for p in range(1, places):
                at = p * plan.pooled + f * plan.cells
                part = part + grad_scores[at : at + plan.cells]
            bias_ref[f, h : h + 1, :] = jnp.sum(part, axis=0, keepdims=True)
        grad_scores_r = grad_scores.astype(BF16)
        grad_query = grad_query + mm(grad_scores_r, keys) * (mask * SIZE ** (-0.5))
        grad_keys = grad_keys + mm_tl(grad_scores_r, query_head)
        grad_values = grad_values + mm_tl(probs_r, grad_head)
    time, _ = key_facts(plan, s, first, second)
    table = jnp.zeros((8, 128), F32)
    for f in range(plan.frames):
        onehot = offset_onehot(plan, s, time, f)
        table = table + lax.dot_general(
            bias_ref[f], onehot, (((1,), (1,)), ((), ())), precision=HIGHEST, preferred_element_type=F32
        )
    table_ref[...] = table
    return grad_query, grad_keys * SIZE ** (-0.5), grad_values


def load_pairs(refs, width):
    pairs = jnp.concatenate([ref[...] for ref in refs], axis=0)
    return pairs[:, :width], pairs[:, width:]


def pool_pair(plan, raw, pool_ref, squeeze_ref, pair_ref):
    width = raw.shape[1] // 2
    for i in range(2):
        pooled = pool(raw[:, i * width : (i + 1) * width], pool_ref[pool_ref.shape[0] - 2 + i])
        pair_ref[: plan.pooled, i * width : (i + 1) * width] = pooled.astype(BF16)
        if plan.local_squeeze:
            weights = squeeze_ref[i]
            for g in range(plan.frames // 4):
                total = None
                for k in range(4):
                    at = (4 * g + k) * plan.cells
                    part = pooled[at : at + plan.cells] * weights[k : k + 1]
                    total = part if total is None else total + part
                at = plan.pooled + g * plan.cells
                pair_ref[at : at + plan.cells, i * width : (i + 1) * width] = total.astype(BF16)


def store_rows(ref, z, start, values):
    each, at = ref.shape[2], 0
    while at < values.shape[0]:
        who, off = divmod(start + at, each)
        n = min(each - off, values.shape[0] - at)
        ref[who, z, off : off + n, :] = values[at : at + n].astype(BF16)
        at += n


def store_columns(ref, tensor, start, values):
    rows = values.shape[0] // tensor
    for z in range(tensor):
        for c in range(values.shape[1] // LANES):
            part = values[z * rows : (z + 1) * rows, c * LANES : (c + 1) * LANES]
            store_rows(ref, z, start + c * rows, part)
    return start + values.shape[1] // LANES * rows


def smooth_max(raw):
    parts = blocks(raw, 4)
    highest = jnp.maximum(jnp.maximum(parts[0], parts[1]), jnp.maximum(parts[2], parts[3]))
    total = jnp.exp(parts[0] - highest)
    for p in range(1, 4):
        total = total + jnp.exp(parts[p] - highest)
    return highest + jnp.log(total) - LOG_FOUR


def smooth_max_back(raw, grad):
    parts = blocks(raw, 4)
    highest = jnp.maximum(jnp.maximum(parts[0], parts[1]), jnp.maximum(parts[2], parts[3]))
    parts = [jnp.exp(part - highest) for part in parts]
    total = parts[0] + parts[1] + parts[2] + parts[3]
    scaled = grad / total
    return jnp.concatenate([part * scaled for part in parts], axis=0)


def call(name, body, outs, vmem, smem=(), scratch=()):
    return pl.pallas_call(
        body,
        out_shape=[jax.ShapeDtypeStruct(shape, dtype) for shape, dtype in outs],
        in_specs=[pl.BlockSpec(memory_space=pltpu.SMEM)] * len(smem)
        + [pl.BlockSpec(memory_space=pltpu.VMEM)] * len(vmem),
        out_specs=[pl.BlockSpec(memory_space=pltpu.VMEM)] * len(outs),
        scratch_shapes=[pltpu.VMEM(shape, dtype) for shape, dtype in scratch],
        name=name,
        interpret=INTERPRET,
        compiler_params=pltpu.CompilerParams(vmem_limit_bytes=56 << 20),
    )(*smem, *vmem)


def enter_body(plan, arrived, order, gain, project, pools, squeeze, x_ref, cot_ref, n_ref, q_ref, pair_ref):
    rows = mm(order[...], arrived[...])
    x = rows[: plan.tokens]
    x_ref[...] = x.astype(BF16)
    width = cot_ref.shape[1] // 2
    cot_ref[:, :width] = rows[plan.tokens : plan.tokens + plan.pooled].astype(BF16)
    cot_ref[:, width:] = rows[plan.tokens + plan.pooled :].astype(BF16)
    n = (norm(x)[0] * gain[...]).astype(BF16)
    n_ref[...] = n
    raw = mm(n, project[...])
    q_ref[...] = raw[:, : x.shape[1]].astype(BF16)
    pool_pair(plan, raw[:, x.shape[1] :], pools, squeeze, pair_ref)


def pick_hidden(core, mine, theirs, expand, reduce, up_ref, down_ref):
    up_ref[0] = expand[...]
    down_ref[0] = reduce[...]

    @pl.when(core == 0)
    def _():
        for k in range(len(mine)):
            up_ref[k + 1] = mine[k][...]
            down_ref[k + 1] = theirs[k][...]

    @pl.when(core != 0)
    def _():
        for k in range(len(mine)):
            up_ref[k + 1] = theirs[k][...]
            down_ref[k + 1] = mine[k][...]


def first_body(plan, heads, resets, videos, *refs):
    refs = list(refs)

    def take(n):
        taken = refs[:n]
        del refs[:n]
        return taken

    x, query = take(2)
    pairs = take(plan.seq)
    memories = take(2)
    table, output, gain, expand, reduce = take(5)
    mine, theirs = take(plan.tensor - 1), take(plan.tensor - 1)
    gain_b, project_b, pool_b, squeeze_b, shortcut_b = take(5)
    or_ref, m_ref, l_ref, y_ref, probs_ref, nb_ref, qb_ref, pairb_ref, base_ref, up_ref, down_ref = refs
    width = x.shape[1]
    scalars = clip_scalars(plan, resets, videos)
    pick_hidden(lax.axis_index("core"), mine, theirs, expand, reduce, up_ref, down_ref)
    keys, values = load_pairs([ref.at[: plan.pooled] for ref in pairs] + memories, width)
    mixed = attend(plan, query[...], keys, values, table[...], heads, probs_ref, scalars)
    mixed_r = mixed.astype(BF16)
    or_ref[...] = mixed_r
    middle = x[...].astype(F32) + mm(mixed_r, output[...])
    m_ref[...] = middle
    l = (norm(middle)[0] * gain[...]).astype(BF16)
    l_ref[...] = l
    y = middle
    for k in range(plan.tensor):
        hidden = gelu(mm(l, up_ref[k])).astype(BF16)
        y = y + mm(hidden, down_ref[k])
    y_ref[...] = y
    n = (norm(y)[0] * gain_b[...]).astype(BF16)
    nb_ref[...] = n
    wide = base_ref.shape[1]
    raw = mm(n, project_b[...])
    qb_ref[...] = pool(raw[:, :wide], pool_b[0]).astype(BF16)
    pool_pair(plan, raw[:, wide:], pool_b, squeeze_b, pairb_ref)
    base_ref[...] = smooth_max(mm(n, shortcut_b[...]))


def second_body(plan, heads, resets, videos, *refs):
    refs = list(refs)
    query = refs.pop(0)
    pairs, refs = refs[: plan.seq], refs[plan.seq :]
    memories, refs = refs[:2], refs[2:]
    table, output, gain, base, cot, or_ref, m_ref, send_ref, probs_ref = refs
    width = query.shape[1]
    scalars = clip_scalars(plan, resets, videos)
    keys, values = load_pairs([ref.at[: plan.pooled] for ref in pairs] + memories, width)
    mixed_r = attend(plan, query[...], keys, values, table[...], heads, probs_ref, scalars).astype(BF16)
    or_ref[...] = mixed_r
    middle = base[...] + mm(mixed_r, output[...])
    m_ref[...] = middle
    send_ref[:, :width] = (norm(middle)[0] * gain[...]).astype(BF16)
    send_ref[:, width:] = cot[...]


def hidden_body(rows, up, down, send_ref, grads_ref):
    width = up.shape[0]
    l = rows[:, :width]
    grad = rows[:, width:]
    gate, slope = gelu_both(mm(l, up[...]))
    hidden = gate.astype(BF16)
    send_ref[:, :width] = mm(hidden, down[...]).astype(BF16)
    grad_pre = (slope * mm_tr(grad, down[...])).astype(BF16)
    send_ref[:, width:] = mm_tr(grad_pre, up[...]).astype(BF16)
    grad_up = mm_tl(l, grad_pre)
    grad_down = mm_tl(hidden, grad)
    at = 0
    for whole in (grad_up, grad_down):
        for c in range(whole.shape[1] // LANES):
            part = whole[:, c * LANES : (c + 1) * LANES]
            grads_ref[at : at + part.shape[0], :] = part.astype(BF16)
            at += part.shape[0]


def second_back_body(plan, heads, resets, videos, *refs):
    refs = list(refs)
    sums, cot, middle, gain, mixed, output, query, probs = refs[:8]
    pairs, refs = refs[8 : 8 + plan.seq], refs[8 + plan.seq :]
    memories, refs = refs[:2], refs[2:]
    out_ref, dm_ref, dgain_ref, doutput_ref, dq_ref, dtable_ref, gown_ref = refs[:7]
    gother, refs = refs[7 : 6 + plan.seq], refs[6 + plan.seq :]
    gm1_ref, gm2_ref, bias_ref = refs
    width = query.shape[1]
    total = sums[0].astype(F32)
    for z in range(1, plan.tensor):
        total = total + sums[z].astype(F32)
    m = middle[...]
    out_ref[...] = (m + total[:, :width]).astype(BF16)
    normed, inverse = norm(m)
    grad, dgain = norm_back(total[:, width:], gain[...], normed, inverse)
    dgain_ref[...] = dgain
    grad = cot[...].astype(F32) + grad
    dm_ref[...] = grad
    store_back(plan, heads, resets, videos, grad, mixed, output, query, probs, pairs, memories,
               doutput_ref, dq_ref, dtable_ref, gown_ref, gother, gm1_ref, gm2_ref, bias_ref)


def store_back(plan, heads, resets, videos, grad, mixed, output, query, probs, pairs, memories,
               doutput_ref, dq_ref, dtable_ref, gown_ref, gother, gm1_ref, gm2_ref, bias_ref):
    width = query.shape[1]
    scalars = clip_scalars(plan, resets, videos)
    grad_r = grad.astype(BF16)
    doutput_ref[...] = mm_tl(mixed[...], grad_r).astype(BF16)
    keys, values = load_pairs([ref.at[: plan.pooled] for ref in pairs] + list(memories), width)
    dq, dk, dv = attend_back(
        plan, mm_tr(grad_r, output[...]), query[...], keys, values, probs, heads, bias_ref, dtable_ref, scalars
    )
    dq_ref[...] = dq
    for i, part in enumerate((dk, dv)):
        lanes = slice(i * width, (i + 1) * width)
        gown_ref[:, lanes] = part[: plan.pooled]
        for o, ref in enumerate(gother):
            at = (o + 1) * plan.pooled
            ref[:, lanes] = part[at : at + plan.pooled].astype(BF16)
        gm1_ref[:, lanes] = part[plan.own : plan.own + plan.memory].astype(BF16)
        gm2_ref[:, lanes] = part[plan.own + plan.memory :].astype(BF16)


def pair_grads(plan, refs):
    own, received = refs[0], refs[1 : plan.seq]
    grad = own[...]
    for ref in received:
        grad = grad + ref[...].astype(F32)
    if not plan.local_squeeze:
        return grad, None
    parts = refs[plan.seq :]
    memory = parts[0][...].astype(F32)
    for ref in parts[1:]:
        memory = memory + ref[...].astype(F32)
    return grad, memory


def unpool(plan, raw, grad, memory, pool_ref, squeeze_ref, dpool_ref, dsqueeze_ref, first):
    width = raw.shape[1] // 2
    result = []
    for i in range(2):
        weights = pool_ref[first + i]
        lanes = slice(i * width, (i + 1) * width)
        part = grad[:, lanes]
        source = raw[:, lanes]
        if plan.local_squeeze:
            pooled = pool(source, weights)
            ws = squeeze_ref[i]
            pieces = []
            sums = [None] * 4
            for g in range(plan.frames // 4):
                dm = memory[g * plan.cells : (g + 1) * plan.cells, lanes]
                for k in range(4):
                    at = (4 * g + k) * plan.cells
                    pieces.append(part[at : at + plan.cells] + dm * ws[k : k + 1])
                    total = jnp.sum(dm * pooled[at : at + plan.cells], axis=0, keepdims=True)
                    sums[k] = total if sums[k] is None else sums[k] + total
            part = jnp.concatenate(pieces, axis=0)
            for k in range(4):
                dsqueeze_ref[i, k : k + 1, :] = sums[k]
        result.append(unpool_one(source, part, weights, dpool_ref, first + i))
    return result


def unpool_one(source, part, weights, dpool_ref, place):
    pieces = []
    for p, piece in enumerate(blocks(source, 4)):
        dpool_ref[place, p : p + 1, :] = jnp.sum(part * piece, axis=0, keepdims=True)
        pieces.append((part * weights[p : p + 1]).astype(BF16))
    return jnp.concatenate(pieces, axis=0)


def middle_back_body(plan, heads, resets, videos, *refs):
    refs = list(refs)

    def take(n):
        taken = refs[:n]
        del refs[:n]
        return taken

    pieces = 2 * plan.seq if plan.local_squeeze else plan.seq
    grads = take(pieces)
    dq, dm, doutput_b, n_ref, y_ref, gain_b, project_b, pool_b, squeeze_b, shortcut_b = take(10)
    m_ref, l_ref, gain, mixed, output, query, probs, expand, reduce = take(9)
    mine, theirs = take(plan.tensor - 1), take(plan.tensor - 1)
    pairs, memories = take(plan.seq), take(2)
    big_ref, dpool_ref, dsqueeze_ref, dgainb_ref, dgain_ref, dm_out, doutput_ref, dq_ref, dtable_ref = take(9)
    gown_ref = take(1)[0]
    gother = take(plan.seq - 1)
    gm1_ref, gm2_ref, up_ref, down_ref, bias_ref = refs
    tensor = plan.tensor
    pick_hidden(lax.axis_index("core"), mine, theirs, expand, reduce, up_ref, down_ref)
    wide = dm.shape[1]
    n = n_ref[...]
    grad, memory = pair_grads(plan, grads)
    at = 0
    grad_n = None
    raw = mm(n, project_b[...])
    parts = [unpool_one(raw[:, :wide], dq[...], pool_b[0], dpool_ref, 0)]
    parts += unpool(plan, raw[:, wide:], grad, memory, pool_b, squeeze_b, dpool_ref, dsqueeze_ref, 1)
    for i, part in enumerate(parts):
        at = store_columns(big_ref, tensor, at, mm_tl(n, part))
        back = mm_tr(part, project_b[:, i * wide : (i + 1) * wide])
        grad_n = back if grad_n is None else grad_n + back
    grad_z = smooth_max_back(mm(n, shortcut_b[...]), dm[...]).astype(BF16)
    at = store_columns(big_ref, tensor, at, mm_tl(n, grad_z))
    at = store_columns(big_ref, tensor, at, doutput_b[...])
    grad_n = grad_n + mm_tr(grad_z, shortcut_b[...])
    normed, inverse = norm(y_ref[...])
    grad_y, dgain = norm_back(grad_n, gain_b[...], normed, inverse)
    dgainb_ref[...] = dgain
    grad_r = grad_y.astype(BF16)
    l = l_ref[...]
    t = lax.axis_index("tensor")
    grad_l = None
    for k in range(tensor):
        gate, slope = gelu_both(mm(l, up_ref[k]))
        hidden = gate.astype(BF16)
        grad_pre = (slope * mm_tr(grad_r, down_ref[k])).astype(BF16)
        z = t ^ k
        store_rows(big_ref, z, at, mm_tl(l, grad_pre))
        store_rows(big_ref, z, at + l.shape[1], mm_tl(hidden, grad_r))
        back = mm_tr(grad_pre, up_ref[k])
        grad_l = back if grad_l is None else grad_l + back
    normed, inverse = norm(m_ref[...])
    grad, dgain = norm_back(grad_l, gain[...], normed, inverse)
    dgain_ref[...] = dgain
    grad = grad_y + grad
    dm_out[...] = grad
    store_back(plan, heads, resets, videos, grad, mixed, output, query, probs, pairs, memories,
               doutput_ref, dq_ref, dtable_ref, gown_ref, gother, gm1_ref, gm2_ref, bias_ref)


def leave_body(plan, *refs):
    refs = list(refs)
    pieces = 2 * plan.seq if plan.local_squeeze else plan.seq
    grads, refs = refs[:pieces], refs[pieces:]
    (dq, dm, doutput, n_ref, x_ref, gain, project, pools, squeeze, order, out,
     dgain_mid, dtable, dgain_b, dpool_b, dsqueeze_b, dmid_b, dtable_b) = refs[:18]
    refs = refs[18:]
    given = refs.pop(0) if not plan.local_squeeze else None
    send_ref, tail_ref, small_ref, dpool_ref, dsqueeze_ref, sum_ref = refs
    width = x_ref.shape[1]
    n = n_ref[...]
    grad, memory = pair_grads(plan, grads)
    raw = mm(n, project[:, width:])
    parts = [dq[...].astype(BF16)]
    parts += unpool(plan, raw, grad, memory, pools, squeeze, dpool_ref, dsqueeze_ref, 0)
    at = 0
    grad_n = None
    for i, part in enumerate(parts):
        at = store_columns(tail_ref, plan.tensor, at, mm_tl(n, part))
        back = mm_tr(part, project[:, i * width : (i + 1) * width])
        grad_n = back if grad_n is None else grad_n + back
    store_columns(tail_ref, plan.tensor, at, doutput[...])
    normed, inverse = norm(x_ref[...].astype(F32))
    grad_x, dgain = norm_back(grad_n, gain[...], normed, inverse)
    grad_x = (grad_x + dm[...]).astype(BF16)
    leaving = jnp.concatenate([grad_x, out[:, :width], out[:, width:]], axis=0)
    send_ref[...] = mm_tl(order[...], leaving).astype(BF16)
    sum_ref[...] = jnp.zeros(sum_ref.shape, F32)
    squeeze_a = dsqueeze_ref if given is None else given
    sum_ref[0:1, :] = dgain
    sum_ref[1:2, :] = dgain_mid[...]
    sum_ref[2:3, :] = dgain_b[...]
    for i in range(2):
        half = slice(i * width, (i + 1) * width)
        sum_ref[3 + i : 4 + i, :] = dmid_b[:, half]
        sum_ref[8 + 4 * i : 12 + 4 * i, :] = dpool_ref[i]
        sum_ref[16 + 4 * i : 20 + 4 * i, :] = squeeze_a[i]
        for j in range(3):
            sum_ref[24 + 16 * i + 4 * j : 28 + 16 * i + 4 * j, :] = dpool_b[j, :, half]
        for j in range(2):
            sum_ref[56 + 8 * i + 4 * j : 60 + 8 * i + 4 * j, :] = dsqueeze_b[j, :, half]
    sum_ref[72:80, :128] = dtable[...]
    sum_ref[80:88, :128] = dtable_b[...]
    store_rows(small_ref, 0, 0, sum_ref[...])


def all_pairs(axis, by):
    n = lax.axis_size(axis)
    return [(i, i ^ by) for i in range(n)]


def shift(values, by):
    chips, cores = lax.axis_size("chip"), lax.axis_size("core")
    seq, tensor = lax.axis_size("seq"), lax.axis_size("tensor")
    clips = chips * cores * tensor
    pairs = []
    for g in range(clips):
        if 0 <= g + by < clips:
            for s in range(seq):
                source = (g // tensor * seq + s) * tensor + g % tensor
                target = ((g + by) // tensor * seq + s) * tensor + (g + by) % tensor
                pairs.append((source, target))
    return lax.ppermute(values, EVERY, pairs)


def relative_weights(plan, squeeze):
    s = lax.axis_index("seq")
    order = jnp.arange(plan.all_frames)
    frame = ((s ^ (order // plan.frames)) * plan.frames + order % plan.frames) % 4
    pair = jnp.concatenate([squeeze[0], squeeze[1]], axis=-1)
    return pair[frame], frame


def share_pairs(plan, pair, squeeze):
    pairs = [pair] + [lax.ppermute(pair, "seq", all_pairs("seq", o)) for o in range(1, plan.seq)]
    if plan.local_squeeze:
        memory = jnp.concatenate([each[plan.pooled :] for each in pairs], axis=0)
    else:
        memory = squeeze_all(plan, pairs, squeeze)
    return pairs, (shift(memory, 1), shift(memory, 2))


def by_frame(plan, pairs):
    together = jnp.concatenate(pairs, axis=0).astype(F32)
    return together.reshape(plan.all_frames // 4, 4, plan.cells, -1)


def squeeze_all(plan, pairs, squeeze):
    weights = relative_weights(plan, squeeze)[0].reshape(plan.all_frames // 4, 4, 1, -1)
    total = jnp.sum(by_frame(plan, pairs) * weights, axis=1)
    return total.reshape(plan.memory, -1).astype(BF16)


def return_pairs(plan, grads, pairs, squeeze):
    own, others, first, second = grads
    memory = shift(first, -1).astype(F32) + shift(second, -2).astype(F32)
    if plan.local_squeeze:
        received = [lax.ppermute(each, "seq", all_pairs("seq", o + 1)) for o, each in enumerate(others)]
        parts = jnp.split(memory, plan.seq, axis=0)
        moved = [
            lax.ppermute(each.astype(BF16), "seq", all_pairs("seq", o + 1)) for o, each in enumerate(parts[1:])
        ]
        return [own] + received + [parts[0]] + moved, None
    weights, frame = relative_weights(plan, squeeze)
    weights = weights.reshape(plan.all_frames // 4, 4, 1, -1)
    memory = memory.reshape(plan.all_frames // 4, 1, plan.cells, -1)
    both = by_frame(plan, [own] + [each.astype(F32) for each in others]) + memory * weights
    both = jnp.split(both.reshape(plan.own, -1), plan.seq, axis=0)
    sums = jnp.sum(by_frame(plan, pairs) * memory, axis=2).reshape(plan.all_frames, -1)
    onehot = (frame[None, :] == jnp.arange(4)[:, None]).astype(F32)
    sums = jnp.dot(onehot, sums, precision=HIGHEST)
    width = sums.shape[1] // 2
    received = [
        lax.ppermute(each.astype(BF16), "seq", all_pairs("seq", o + 1)) for o, each in enumerate(both[1:])
    ]
    return [both[0]] + received, jnp.stack([sums[:, :width], sums[:, width:]])


def sum_first(values):
    return jnp.sum(values.astype(F32), axis=0).astype(BF16)


def spread(values, axes):
    return lax.all_to_all(values, axes, 0, 0, tiled=True)


def gather_plane(values):
    plane = lax.axis_size(PLANE)
    return spread(jnp.broadcast_to(values[None], (plane,) + values.shape), PLANE)


def padded(rows, parts):
    return -(-rows // (16 * parts)) * 16


def local(
    clips_in, cotangent, resets, videos,
    attend_gain_a, project_a, pooling_a, squeeze_a, offsets_a, output_a, mixer_gain_a, expand_a, reduce_a,
    attend_gain_b, project_b, pooling_b, squeeze_b, offsets_b, output_b, shortcut_b, mixer_gain_b, expand_b, reduce_b,
):
    seq, tensor, plane = lax.axis_size("seq"), lax.axis_size("tensor"), lax.axis_size(PLANE)
    plan = Plan(seq, tensor, clips_in.shape)
    width, wide = clips_in.shape[-1], cotangent.shape[-1]
    heads_a, heads_b = offsets_a.shape[0], offsets_b.shape[0]
    core = lax.axis_index("core")
    tokens, pooled, keys, memory = plan.tokens, plan.pooled, plan.keys, plan.memory
    half = jnp.where(core == 0, expand_a, reduce_a)
    mine = [lax.ppermute(half, "tensor", all_pairs("tensor", k)) for k in range(1, tensor)]
    theirs = [lax.ppermute(each, "core", all_pairs("core", 1)) for each in mine]

    order = jnp.asarray(plan.arrange(), BF16)
    home = ("tensor", "seq")
    leaving = jnp.concatenate(
        [clips_in.reshape(plan.group, -1, width), cotangent.reshape(plan.group, -1, width)], axis=1
    )
    arrived = spread(leaving, home).reshape(-1, width)
    row = lambda gain: gain.reshape(1, -1)
    table = lambda offsets: jnp.pad(offsets, ((0, 8 - offsets.shape[0]), (0, 128 - offsets.shape[1])))
    table_a, table_b = table(offsets_a), table(offsets_b)
    pair_rows = pooled + (plan.frames // 4 * plan.cells if plan.local_squeeze else 0)
    x, cot, n_a, q_a, pair_a = call(
        "enter",
        functools.partial(enter_body, plan),
        [((tokens, width), BF16), ((pooled, wide), BF16), ((tokens, width), BF16), ((tokens, width), BF16),
         ((pair_rows, 2 * width), BF16)],
        [arrived, order, row(attend_gain_a), project_a, pooling_a, squeeze_a],
    )
    pairs_a, memories_a = share_pairs(plan, pair_a, squeeze_a)
    hidden = [((tensor, width, expand_a.shape[1]), BF16), ((tensor, reduce_a.shape[0], width), BF16)]
    or_a, m_a, l_a, y_a, probs_a, n_b, q_b, pair_b, base = call(
        "first",
        functools.partial(first_body, plan, heads_a),
        [((tokens, width), BF16), ((tokens, width), F32), ((tokens, width), BF16), ((tokens, width), F32),
         ((heads_a * tokens, keys), BF16), ((tokens, width), BF16), ((pooled, wide), BF16),
         ((pair_rows, 2 * wide), BF16), ((pooled, wide), F32)],
        [x, q_a, *pairs_a, *memories_a, table_a, output_a, row(mixer_gain_a), expand_a, reduce_a, *mine, *theirs,
         row(attend_gain_b), project_b, pooling_b, squeeze_b, shortcut_b],
        [resets, videos],
        hidden,
    )
    pairs_b, memories_b = share_pairs(plan, pair_b, squeeze_b)
    or_b, m_b, rows_b, probs_b = call(
        "second",
        functools.partial(second_body, plan, heads_b),
        [((pooled, wide), BF16), ((pooled, wide), F32), ((pooled, 2 * wide), BF16),
         ((heads_b * pooled, keys), BF16)],
        [q_b, *pairs_b, *memories_b, table_b, output_b, row(mixer_gain_b), base, cot],
        [resets, videos],
    )
    rows_all = lax.all_gather(rows_b, "tensor", axis=0, tiled=True)
    hidden_rows = (expand_b.shape[1] // LANES) * wide + (wide // LANES) * reduce_b.shape[0]
    shares, grads_0 = call(
        "hidden",
        hidden_body,
        [((tensor * pooled, 2 * wide), BF16), ((hidden_rows, LANES), BF16)],
        [rows_all, expand_b, reduce_b],
    )
    sums = spread(shares, "tensor").reshape(tensor, pooled, 2 * wide)
    bias = lambda: [((plan.frames, 8, keys), F32)]
    key_grads = lambda w: (
        [((pooled, 2 * w), F32)] + [((pooled, 2 * w), BF16)] * (seq - 1) + [((memory, 2 * w), BF16)] * 2
    )
    out, dm_b, dmid_b, doutput_b, dq_b, dtable_b, *back = call(
        "second_back",
        functools.partial(second_back_body, plan, heads_b),
        [((pooled, wide), BF16), ((pooled, wide), F32), ((1, wide), F32), ((wide, wide), BF16), ((pooled, wide), F32),
         ((8, 128), F32), *key_grads(wide)],
        [sums, cot, m_b, row(mixer_gain_b), or_b, output_b, q_b, probs_b, *pairs_b, *memories_b],
        [resets, videos],
        bias(),
    )
    pieces, dsqueeze_given = return_pairs(plan, (back[0], back[1:seq], back[-2], back[-1]), pairs_b, squeeze_b)
    big_rows = padded((3 + 1) * wide // LANES * (width // tensor) + wide // LANES * (wide // tensor) + 2 * width, plane)
    big, dpool_b, dsqueeze_b, dgain_b, dmid_a, dm_a, doutput_a, dq_a, dtable_a, *back = call(
        "middle_back",
        functools.partial(middle_back_body, plan, heads_a),
        [((plane, tensor, big_rows, LANES), BF16), ((3, 4, wide), F32), ((2, 4, wide), F32), ((1, width), F32),
         ((1, width), F32), ((tokens, width), F32), ((width, width), BF16), ((tokens, width), F32), ((8, 128), F32),
         *key_grads(width)],
        [*pieces, dq_b, dm_b, doutput_b, n_b, y_a, row(attend_gain_b), project_b, pooling_b, squeeze_b, shortcut_b,
         m_a, l_a, row(mixer_gain_a), or_a, output_a, q_a, probs_a, expand_a, reduce_a, *mine, *theirs,
         *pairs_a, *memories_a],
        [resets, videos],
        hidden + bias(),
    )
    if dsqueeze_given is not None:
        dsqueeze_b = dsqueeze_given
    pieces, dsqueeze_given = return_pairs(plan, (back[0], back[1:seq], back[-2], back[-1]), pairs_a, squeeze_a)
    tail_rows, small_rows = padded(4 * (width // tensor), plane), padded(128, plane)
    leaving, tail, small = call(
        "leave",
        functools.partial(leave_body, plan),
        [(arrived.shape, BF16), ((plane, tensor, tail_rows, LANES), BF16), ((plane, 1, small_rows, LANES), BF16)],
        [*pieces, dq_a, dm_a, doutput_a, n_a, x, row(attend_gain_a), project_a, pooling_a, squeeze_a, order, out,
         dmid_a, dtable_a, dgain_b, dpool_b, dsqueeze_b, dmid_b, dtable_b]
        + ([] if dsqueeze_given is None else [dsqueeze_given]),
        (),
        [((2, 4, width), F32), ((2, 4, width), F32), ((128, LANES), F32)],
    )
    returned = spread(leaving.reshape(plan.group, -1, width), home)
    x_rows = plan.frames * plan.rows * plan.cols
    grad_input = returned[:, :x_rows].reshape(clips_in.shape).astype(F32)
    result = returned[:, x_rows:].reshape(cotangent.shape).astype(F32)

    hidden_each = padded(hidden_rows, plane)
    assert hidden_each * plane == hidden_rows
    grads_0 = sum_first(spread(grads_0.reshape(plane, hidden_each, LANES), PLANE))
    big = sum_first(spread(sum_first(spread(big, PLANE)), "tensor"))
    tail = jnp.concatenate(
        [tail.reshape(plane, tensor * tail_rows, LANES), small.reshape(plane, small_rows, LANES)], axis=1
    )
    tail = sum_first(spread(tail, PLANE))
    small = jnp.broadcast_to(tail[None, tensor * tail_rows :], (tensor, small_rows, LANES))
    tail = jnp.concatenate([tail[: tensor * tail_rows].reshape(tensor, tail_rows, LANES), small], axis=1)
    tail = sum_first(spread(tail.reshape(tensor, -1, LANES), "tensor").reshape(tensor, -1, LANES))
    whole = gather_plane(jnp.concatenate([grads_0, big, tail], axis=0)).astype(F32)
    at = 0
    groups = []
    for rows in (hidden_each, big_rows, tail_rows, small_rows):
        groups.append(whole[:, at : at + rows].reshape(plane * rows, LANES))
        at += rows
    hidden_g, big_g, tail_g, small_g = groups

    def columns(group, start, rows, count):
        part = group[start : start + rows * count].reshape(count, rows, LANES)
        return part.transpose(1, 0, 2).reshape(rows, count * LANES), start + rows * count

    grad_expand_b, at = columns(hidden_g, 0, wide, expand_b.shape[1] // LANES)
    grad_reduce_b, at = columns(hidden_g, at, reduce_b.shape[0], wide // LANES)
    share = width // tensor
    grad_project_b, at = columns(big_g, 0, share, 3 * wide // LANES)
    grad_shortcut_b, at = columns(big_g, at, share, wide // LANES)
    grad_output_b, at = columns(big_g, at, wide // tensor, wide // LANES)
    grad_expand_a, at = columns(big_g, at, width, 1)
    grad_reduce_a, at = columns(big_g, at, width, 1)
    grad_project_a, at = columns(tail_g, 0, share, 3)
    grad_output_a, at = columns(tail_g, at, share, 1)
    halves = lambda a, b, n: jnp.concatenate([small_g[a : a + n], small_g[b : b + n]], axis=1)
    entries = offsets_a.shape[1]
    return (
        result,
        grad_input,
        small_g[0],
        grad_project_a,
        small_g[8:16].reshape(2, 4, width),
        small_g[16:24].reshape(2, 4, width),
        small_g[72 : 72 + heads_a, :entries],
        grad_output_a,
        small_g[1],
        grad_expand_a,
        grad_reduce_a,
        small_g[2],
        grad_project_b,
        halves(24, 40, 12).reshape(3, 4, wide),
        halves(56, 64, 8).reshape(2, 4, wide),
        small_g[80 : 80 + heads_b, :entries],
        grad_output_b,
        grad_shortcut_b,
        halves(3, 4, 1).reshape(wide),
        grad_expand_b,
        grad_reduce_b,
    )


def solution(mesh):
    clip, seq, tensor = mesh.devices.shape
    split = Mesh(mesh.devices.reshape(clip // 2, 2, seq, tensor), EVERY)
    clips = ("chip", "core")
    field = P(clips, None, "seq", "tensor", None)
    up, down = P(None, "tensor"), P("tensor", None)
    block = (P(), P(), P(), P(), P(), P(), P(), up, down)
    block_b = (P(), P(), P(), P(), P(), P(), P(), P(), up, down)
    grads = (P(), down, P(), P(), P(), down, P(), up, down)
    grads_b = (P(), down, P(), P(), P(), down, down, P(), up, down)
    return jax.shard_map(
        local,
        mesh=split,
        in_specs=(field, field, P(), P()) + block + block_b,
        out_specs=(field, field) + grads + grads_b,
        check_vma=False,
    )
```

```python
import functools

import jax
import jax.numpy as jnp
import numpy as np
from jax import lax
from jax.experimental import pallas as pl
from jax.experimental.pallas import tpu as pltpu
from jax.sharding import Mesh
from jax.sharding import PartitionSpec as P

F32 = jnp.float32
BF16 = jnp.bfloat16
HIGHEST = lax.Precision.HIGHEST
EPSILON = 1e-06
MASKED = -1000000000.0
LOG_FOUR = 1.3862943611198906
SIZE = 96
LANES = 384
INTERPRET = False
PLANE = ("chip", "core", "far", "near")
EVERY = PLANE + ("tensor",)
ACROSS = ("chip", "far", "near")
FRAMES = ("far", "core")


def wide_row(gain):
    return gain[...].reshape(1, gain.shape[0])


def log2(n):
    return n.bit_length() - 1


def mm(left, right):
    return jnp.dot(left, right, preferred_element_type=F32)


def mm_tl(left, right):
    return lax.dot_general(left, right, (((0,), (0,)), ((), ())), preferred_element_type=F32)


def mm_tr(left, right):
    return lax.dot_general(left, right, (((1,), (1,)), ((), ())), preferred_element_type=F32)


def norm(field):
    mean = jnp.mean(field, axis=-1, keepdims=True)
    centered = field - mean
    inverse = lax.rsqrt(jnp.mean(centered * centered, axis=-1, keepdims=True) + EPSILON)
    return centered * inverse, inverse


def norm_back(grad, gain, normed, inverse):
    scaled = grad * gain
    field = inverse * (
        scaled
        - jnp.mean(scaled, axis=-1, keepdims=True)
        - normed * jnp.mean(scaled * normed, axis=-1, keepdims=True)
    )
    return field, jnp.sum(grad * normed, axis=0, keepdims=True)


def gelu(values):
    return 0.5 * values * (1.0 + lax.erf(values * 0.7071067811865476))


def gelu_both(values):
    half = 0.5 * (1.0 + lax.erf(values * 0.7071067811865476))
    slope = half + values * jnp.exp(-0.5 * values * values) * 0.3989422804014327
    return values * half, slope


def blocks(values, count):
    rows = values.shape[0] // count
    return [values[i * rows : (i + 1) * rows] for i in range(count)]


def pool(values, weights):
    parts = blocks(values, 4)
    total = parts[0] * weights[0:1]
    for p in range(1, 4):
        total = total + parts[p] * weights[p : p + 1]
    return total


class Plan:
    def __init__(self, seq, tensor, shape):
        clips, frames, rows, cols, _ = shape
        self.seq, self.tensor = seq, tensor
        assert clips == tensor and frames % seq == 0 and rows % 2 == 0 and cols % 2 == 0
        self.all_frames = frames
        self.frames = frames // seq
        self.rows, self.cols = rows, cols
        self.group = seq * tensor
        self.cells = self.group * rows * cols // 4
        self.pooled = self.frames * self.cells
        self.tokens = 4 * self.pooled
        self.local_squeeze = self.frames % 4 == 0
        self.memory = frames // 4 * self.cells
        self.own = seq * self.pooled
        self.sources = seq + 2 * (seq if self.local_squeeze else 1)
        self.returned = seq + (2 * seq if self.local_squeeze else 0)
        self.keys = self.own + 2 * self.memory
        for n in (self.cells, self.pooled, self.memory, self.own, self.frames, seq):
            assert n == 1 << log2(n)

    def arrange(self):
        take = np.arange(self.tokens).reshape(
            self.group, self.frames, self.rows // 2, 2, self.cols // 2, 2
        )
        per = self.frames * self.rows * self.cols
        half = per // 4 * 2
        step = per + half
        x_rows = take // per * step + take % per
        x_rows = x_rows.transpose(3, 5, 1, 0, 2, 4).reshape(-1)
        cot = np.arange(self.pooled).reshape(self.group, self.frames, -1)
        low = cot // (per // 4) * step + per + cot % (per // 4) * 2
        low = low.transpose(1, 0, 2).reshape(-1)
        order = np.concatenate([x_rows, low, low + 1])
        return (order[:, None] == np.arange(self.group * step)[None, :]).astype(np.float32)


def clip_scalars(plan, resets, videos):
    s = lax.axis_index("far") * lax.axis_size("core") + lax.axis_index("core")
    chip = lax.axis_index("chip") * lax.axis_size("near") + lax.axis_index("near")
    g = chip * plan.tensor + lax.axis_index("tensor")
    before = jnp.maximum(g - 1, 0)
    earlier = jnp.maximum(g - 2, 0)
    first = (g >= 1) & (videos[g] == videos[before]) & (resets[g] == 0)
    second = first & (g >= 2) & (videos[before] == videos[earlier]) & (resets[before] == 0)
    return s, first.astype(jnp.int32), second.astype(jnp.int32)


def key_facts(plan, s, first, second):
    k = lax.broadcasted_iota(jnp.int32, (1, plan.keys), 1)
    own_time = ((s ^ (k >> log2(plan.pooled))) << log2(plan.frames)) + (
        (k & (plan.pooled - 1)) >> log2(plan.cells)
    )
    m = k - plan.own
    late = (m >> log2(plan.memory)) > 0
    g = (m & (plan.memory - 1)) >> log2(plan.cells)
    if plan.local_squeeze:
        each = log2(plan.frames // 4)
        squeezed = ((s ^ (g >> each)) << each) + (g & (plan.frames // 4 - 1))
    else:
        squeezed = (s >> log2(4 // plan.frames)) ^ g
    kind = jnp.where(m < 0, 0, jnp.where(late, 2, 1))
    time = jnp.where(m < 0, own_time, 4 * squeezed - plan.all_frames * kind)
    counts = jnp.where(kind == 0, 1, jnp.where(kind == 1, first, second))
    return time, counts


def offset_onehot(plan, s, time, frame):
    index = s * plan.frames + frame - time + plan.all_frames - 1
    rows = lax.broadcasted_iota(jnp.int32, (128, plan.keys), 0)
    return jnp.where(rows == index, 1.0, 0.0).astype(F32)


def head_mask(width, head):
    lane = lax.broadcasted_iota(jnp.int32, (1, width), 1)
    inside = (lane >= head * SIZE) & (lane < (head + 1) * SIZE)
    return jnp.where(inside, 1.0, 0.0).astype(F32)


def attend(plan, query, keys, values, offsets, heads, probs_ref, table_ref, scalars):
    s, first, second = scalars
    rows, width = query.shape
    places = rows // plan.pooled
    time, counts = key_facts(plan, s, first, second)
    biases = []
    table_ref[...] = jnp.zeros(table_ref.shape, F32)
    table_ref[:heads, : offsets.shape[1]] = offsets[...]
    table = table_ref[...]
    for f in range(plan.frames):
        onehot = offset_onehot(plan, s, time, f)
        bias = jnp.dot(table, onehot, precision=HIGHEST, preferred_element_type=F32)
        biases.append(jnp.where(counts > 0, bias, MASKED))
    total = query.astype(F32)
    for h in range(heads):
        mask = head_mask(width, h)
        scores = mm_tr(query * mask.astype(BF16), keys) * SIZE ** (-0.5)
        bias = jnp.concatenate(
            [jnp.broadcast_to(b[h : h + 1], (plan.cells, plan.keys)) for b in biases] * places, axis=0
        )
        scores = scores + bias
        scores = jnp.exp(scores - jnp.max(scores, axis=-1, keepdims=True))
        probs = scores * (1.0 / jnp.sum(scores, axis=-1, keepdims=True))
        probs = probs.astype(BF16)
        probs_ref[h * rows : (h + 1) * rows] = probs
        total = total + mm(probs, values) * mask
    return total


def attend_back(plan, grad, query, keys, values, probs_ref, heads, bias_ref, table_ref, scalars):
    s, first, second = scalars
    rows, width = query.shape
    places = rows // plan.pooled
    grad_r = grad.astype(BF16)
    grad_query = grad
    grad_keys = jnp.zeros((plan.keys, width), F32)
    grad_values = jnp.zeros((plan.keys, width), F32)
    bias_ref[...] = jnp.zeros(bias_ref.shape, F32)
    for h in range(heads):
        mask = head_mask(width, h)
        mask_r = mask.astype(BF16)
        grad_head = grad_r * mask_r
        query_head = query * mask_r
        probs_r = probs_ref[h * rows : (h + 1) * rows]
        probs = probs_r.astype(F32)
        grad_probs = mm_tr(grad_head, values)
        weighted = probs * grad_probs
        grad_scores = weighted - probs * jnp.sum(weighted, axis=-1, keepdims=True)
        for f in range(plan.frames):
            part = grad_scores[f * plan.cells : (f + 1) * plan.cells]
            for p in range(1, places):
                at = p * plan.pooled + f * plan.cells
                part = part + grad_scores[at : at + plan.cells]
            bias_ref[f, h : h + 1, :] = jnp.sum(part, axis=0, keepdims=True)
        grad_scores_r = grad_scores.astype(BF16)
        grad_query = grad_query + mm(grad_scores_r, keys) * (mask * SIZE ** (-0.5))
        grad_keys = grad_keys + mm_tl(grad_scores_r, query_head)
        grad_values = grad_values + mm_tl(probs_r, grad_head)
    time, _ = key_facts(plan, s, first, second)
    table = jnp.zeros((8, 128), F32)
    for f in range(plan.frames):
        onehot = offset_onehot(plan, s, time, f)
        table = table + lax.dot_general(
            bias_ref[f], onehot, (((1,), (1,)), ((), ())), precision=HIGHEST, preferred_element_type=F32
        )
    table_ref[...] = table
    return grad_query, grad_keys * SIZE ** (-0.5), grad_values


def load_pairs(refs, width):
    pairs = jnp.concatenate([ref[...] for ref in refs], axis=0)
    return pairs[:, :width], pairs[:, width:]


def pool_pair(plan, raw, pool_ref, squeeze_ref, pair_ref, memory_ref=None):
    width = raw.shape[1] // 2
    for i in range(2):
        pooled = pool(raw[:, i * width : (i + 1) * width], pool_ref[pool_ref.shape[0] - 2 + i])
        pair_ref[:, i * width : (i + 1) * width] = pooled.astype(BF16)
        if memory_ref is not None:
            weights = squeeze_ref[i]
            for g in range(plan.frames // 4):
                total = None
                for k in range(4):
                    at = (4 * g + k) * plan.cells
                    part = pooled[at : at + plan.cells] * weights[k : k + 1]
                    total = part if total is None else total + part
                at = g * plan.cells
                memory_ref[at : at + plan.cells, i * width : (i + 1) * width] = total.astype(BF16)


def store_rows(stage, each, z, start, values, base=0):
    core = lax.axis_index("core")
    half, at = stage.shape[1], 0
    while at < values.shape[0]:
        who, off = divmod(start + at, each)
        n = min(each - off, values.shape[0] - at)
        part = values[at : at + n].astype(BF16)
        stage[(who // half) ^ core, who % half, z, base + off : base + off + n, :] = part
        at += n


def store_columns(stage, each, tensor, start, values):
    rows = values.shape[0] // tensor
    for z in range(tensor):
        for c in range(values.shape[1] // LANES):
            part = values[z * rows : (z + 1) * rows, c * LANES : (c + 1) * LANES]
            store_rows(stage, each, z, start + c * rows, part)
    return start + values.shape[1] // LANES * rows


def send_stage(stage, keep, give, sems):
    copies = [pltpu.make_async_copy(stage.at[i], (keep, give)[i], sems.at[i]) for i in range(2)]
    for copy in copies:
        copy.start()
    for copy in copies:
        copy.wait()


def smooth_max(raw):
    parts = blocks(raw, 4)
    highest = jnp.maximum(jnp.maximum(parts[0], parts[1]), jnp.maximum(parts[2], parts[3]))
    total = jnp.exp(parts[0] - highest)
    for p in range(1, 4):
        total = total + jnp.exp(parts[p] - highest)
    return highest + jnp.log(total) - LOG_FOUR


def smooth_max_back(raw, grad):
    parts = blocks(raw, 4)
    highest = jnp.maximum(jnp.maximum(parts[0], parts[1]), jnp.maximum(parts[2], parts[3]))
    parts = [jnp.exp(part - highest) for part in parts]
    total = parts[0] + parts[1] + parts[2] + parts[3]
    scaled = grad / total
    return jnp.concatenate([part * scaled for part in parts], axis=0)


def call(name, body, outs, vmem, smem=(), scratch=(), stage=None):
    scratch = [pltpu.VMEM(shape, dtype) for shape, dtype in scratch]
    spaces = [pltpu.VMEM] * len(outs)
    if stage is not None:
        outs = outs + [(stage[1:], BF16)] * 2
        spaces += [pl.ANY] * 2
        scratch += [pltpu.VMEM(stage, BF16), pltpu.SemaphoreType.DMA((2,))]
    return pl.pallas_call(
        body,
        out_shape=[jax.ShapeDtypeStruct(shape, dtype) for shape, dtype in outs],
        in_specs=[pl.BlockSpec(memory_space=pltpu.SMEM)] * len(smem)
        + [pl.BlockSpec(memory_space=pltpu.VMEM)] * len(vmem),
        out_specs=[pl.BlockSpec(memory_space=space) for space in spaces],
        scratch_shapes=scratch,
        name=name,
        interpret=INTERPRET,
        compiler_params=pltpu.CompilerParams(vmem_limit_bytes=56 << 20),
    )(*smem, *vmem)


def enter_body(plan, arrived, order, gain, project, pools, squeeze, x_ref, cot_ref, n_ref, q_ref, *pair):
    rows = mm(order[...], arrived[...])
    x = rows[: plan.tokens]
    x_ref[...] = x.astype(BF16)
    width = cot_ref.shape[1] // 2
    cot_ref[:, :width] = rows[plan.tokens : plan.tokens + plan.pooled].astype(BF16)
    cot_ref[:, width:] = rows[plan.tokens + plan.pooled :].astype(BF16)
    n = (norm(x)[0] * wide_row(gain)).astype(BF16)
    n_ref[...] = n
    raw = mm(n, project[...])
    q_ref[...] = raw[:, : x.shape[1]].astype(BF16)
    pool_pair(plan, raw[:, x.shape[1] :], pools, squeeze, *pair)


def pick_hidden(pieces, expand, reduce, up_ref, down_ref):
    up_ref[0] = expand[...]
    down_ref[0] = reduce[...]
    core, near = lax.axis_index("core"), lax.axis_index("near")
    rows = pieces[0].shape[0]

    def put(first, second):
        for i, piece in enumerate(pieces):
            k, n, c = i // 4 + 1, i // 2 % 2, i % 2
            at = pl.multiple_of((n ^ near) * rows, 16)
            (second if c else first)[k, pl.ds(at, rows), :] = piece[...]

    @pl.when(core == 0)
    def _():
        put(up_ref, down_ref)

    @pl.when(core != 0)
    def _():
        put(down_ref, up_ref)


def first_body(plan, heads, resets, videos, *refs):
    x, query = refs[:2]
    pairs, refs = refs[2 : 2 + plan.sources], refs[2 + plan.sources :]
    table, output, gain, or_ref, m_ref, l_ref, probs_ref, table_ref = refs
    scalars = clip_scalars(plan, resets, videos)
    keys, values = load_pairs(pairs, x.shape[1])
    mixed_r = attend(plan, query[...], keys, values, table, heads, probs_ref, table_ref, scalars).astype(BF16)
    or_ref[...] = mixed_r
    middle = x[...].astype(F32) + mm(mixed_r, output[...])
    m_ref[...] = middle
    l_ref[...] = (norm(middle)[0] * wide_row(gain)).astype(BF16)


def between_body(plan, m_ref, l_ref, expand, reduce, *refs):
    weights, refs = refs[: 4 * plan.tensor - 4], refs[4 * plan.tensor - 4 :]
    gain_b, project_b, pool_b, squeeze_b, shortcut_b, y_ref, nb_ref, qb_ref, base_ref = refs[:9]
    pair, up_ref, down_ref = refs[9:-2], refs[-2], refs[-1]
    pick_hidden(weights, expand, reduce, up_ref, down_ref)
    l = l_ref[...]
    y = m_ref[...]
    for k in range(plan.tensor):
        hidden = gelu(mm(l, up_ref[k])).astype(BF16)
        y = y + mm(hidden, down_ref[k])
    y_ref[...] = y
    n = (norm(y)[0] * wide_row(gain_b)).astype(BF16)
    nb_ref[...] = n
    wide = base_ref.shape[1]
    raw = mm(n, project_b[...])
    qb_ref[...] = pool(raw[:, :wide], pool_b[0]).astype(BF16)
    pool_pair(plan, raw[:, wide:], pool_b, squeeze_b, *pair)
    base_ref[...] = smooth_max(mm(n, shortcut_b[...]))


def second_body(plan, heads, resets, videos, *refs):
    query, pairs, refs = refs[0], refs[1 : 1 + plan.sources], refs[1 + plan.sources :]
    table, output, gain, base, cot, or_ref, m_ref, send_ref, probs_ref, table_ref = refs
    width = query.shape[1]
    scalars = clip_scalars(plan, resets, videos)
    keys, values = load_pairs(pairs, width)
    mixed_r = attend(plan, query[...], keys, values, table, heads, probs_ref, table_ref, scalars).astype(BF16)
    or_ref[...] = mixed_r
    middle = base[...] + mm(mixed_r, output[...])
    m_ref[...] = middle
    send_ref[:, :width] = (norm(middle)[0] * wide_row(gain)).astype(BF16)
    send_ref[:, width:] = cot[...]


def hidden_body(each, rows, up, down, send_ref, keep, give, stage, sems):
    width = up.shape[0]
    l = rows[:, :width]
    grad = rows[:, width:]
    gate, slope = gelu_both(mm(l, up[...]))
    hidden = gate.astype(BF16)
    send_ref[:, :width] = mm(hidden, down[...]).astype(BF16)
    grad_pre = (slope * mm_tr(grad, down[...])).astype(BF16)
    send_ref[:, width:] = mm_tr(grad_pre, up[...]).astype(BF16)
    grad_up = mm_tl(l, grad_pre)
    grad_down = mm_tl(hidden, grad)
    at = 0
    for whole in (grad_up, grad_down):
        for c in range(whole.shape[1] // LANES):
            part = whole[:, c * LANES : (c + 1) * LANES]
            store_rows(stage, each, 0, at, part)
            at += part.shape[0]
    send_stage(stage, keep, give, sems)


def second_back_body(plan, heads, resets, videos, *refs):
    refs = list(refs)
    sums, cot, middle, gain, mixed, output, query, probs = refs[:8]
    pairs, refs = refs[8 : 8 + plan.sources], refs[8 + plan.sources :]
    out_ref, dm_ref, dgain_ref = refs[:3]
    refs = refs[3:]
    width = query.shape[1]
    total = sums[0].astype(F32)
    for z in range(1, plan.tensor):
        total = total + sums[z].astype(F32)
    m = middle[...]
    out_ref[...] = (m + total[:, :width]).astype(BF16)
    normed, inverse = norm(m)
    grad, dgain = norm_back(total[:, width:], wide_row(gain), normed, inverse)
    dgain_ref[...] = dgain
    grad = cot[...].astype(F32) + grad
    dm_ref[...] = grad
    store_back(plan, heads, resets, videos, grad, mixed, output, query, probs, pairs, *refs)


def store_back(plan, heads, resets, videos, grad, mixed, output, query, probs, pairs, doutput_ref, dq_ref, dtable_ref,
               *refs):
    width = query.shape[1]
    scalars = clip_scalars(plan, resets, videos)
    grad_r = grad.astype(BF16)
    doutput_ref[...] = mm_tl(mixed[...], grad_r).astype(BF16)
    grads, bias_ref = refs[:-1], refs[-1]
    keys, values = load_pairs(pairs, width)
    dq, dk, dv = attend_back(
        plan, mm_tr(grad_r, output[...]), query[...], keys, values, probs, heads, bias_ref, dtable_ref, scalars
    )
    dq_ref[...] = dq
    for i, part in enumerate((dk, dv)):
        lanes = slice(i * width, (i + 1) * width)
        at = 0
        for ref in grads:
            ref[:, lanes] = part[at : at + ref.shape[0]].astype(ref.dtype)
            at += ref.shape[0]


def pair_grads(plan, refs):
    own, received = refs[0], refs[1 : plan.seq]
    grad = own[...]
    for ref in received:
        grad = grad + ref[...].astype(F32)
    if not plan.local_squeeze:
        return grad, None
    memory = None
    size = plan.memory // plan.seq
    for i, ref in enumerate(refs[plan.seq :]):
        o = i % plan.seq
        part = ref[o * size : (o + 1) * size, :].astype(F32)
        memory = part if memory is None else memory + part
    return grad, memory


def unpool(plan, raw, grad, memory, pool_ref, squeeze_ref, dpool_ref, dsqueeze_ref, first):
    width = raw.shape[1] // 2
    result = []
    for i in range(2):
        weights = pool_ref[first + i]
        lanes = slice(i * width, (i + 1) * width)
        part = grad[:, lanes]
        source = raw[:, lanes]
        if plan.local_squeeze:
            pooled = pool(source, weights)
            ws = squeeze_ref[i]
            pieces = []
            sums = [None] * 4
            for g in range(plan.frames // 4):
                dm = memory[g * plan.cells : (g + 1) * plan.cells, lanes]
                for k in range(4):
                    at = (4 * g + k) * plan.cells
                    pieces.append(part[at : at + plan.cells] + dm * ws[k : k + 1])
                    total = jnp.sum(dm * pooled[at : at + plan.cells], axis=0, keepdims=True)
                    sums[k] = total if sums[k] is None else sums[k] + total
            part = jnp.concatenate(pieces, axis=0)
            for k in range(4):
                dsqueeze_ref[i, k : k + 1, :] = sums[k]
        result.append(unpool_one(source, part, weights, dpool_ref, first + i))
    return result


def unpool_one(source, part, weights, dpool_ref, place):
    pieces = []
    for p, piece in enumerate(blocks(source, 4)):
        dpool_ref[place, p : p + 1, :] = jnp.sum(part * piece, axis=0, keepdims=True)
        pieces.append((part * weights[p : p + 1]).astype(BF16))
    return jnp.concatenate(pieces, axis=0)


def cross_body(plan, each, *refs):
    pieces = plan.returned
    grads = refs[:pieces]
    (dq, dm, doutput_b, n_ref, y_ref, gain_b, project_b, pool_b, squeeze_b, shortcut_b,
     dy_ref, dpool_ref, dsqueeze_ref, dgain_ref, keep, give, stage, sems) = refs[pieces:]
    tensor = plan.tensor
    wide = dm.shape[1]
    n = n_ref[...]
    grad, memory = pair_grads(plan, grads)
    raw = mm(n, project_b[...])
    parts = [unpool_one(raw[:, :wide], dq[...], pool_b[0], dpool_ref, 0)]
    parts += unpool(plan, raw[:, wide:], grad, memory, pool_b, squeeze_b, dpool_ref, dsqueeze_ref, 1)
    at = 0
    grad_n = None
    for i, part in enumerate(parts):
        at = store_columns(stage, each, tensor, at, mm_tl(n, part))
        back = mm_tr(part, project_b[:, i * wide : (i + 1) * wide])
        grad_n = back if grad_n is None else grad_n + back
    grad_z = smooth_max_back(mm(n, shortcut_b[...]), dm[...]).astype(BF16)
    at = store_columns(stage, each, tensor, at, mm_tl(n, grad_z))
    store_columns(stage, each, tensor, at, doutput_b[...])
    grad_n = grad_n + mm_tr(grad_z, shortcut_b[...])
    normed, inverse = norm(y_ref[...])
    grad_y, dgain = norm_back(grad_n, wide_row(gain_b), normed, inverse)
    dgain_ref[...] = dgain
    dy_ref[...] = grad_y
    send_stage(stage, keep, give, sems)


def first_back_body(plan, each, heads, resets, videos, *refs):
    refs = list(refs)

    def take(n):
        taken = refs[:n]
        del refs[:n]
        return taken

    dy_ref, m_ref, l_ref, gain, mixed, output, query, probs, expand, reduce = take(10)
    weights = take(4 * plan.tensor - 4)
    pairs = take(plan.sources)
    dgain_ref, dm_out = take(2)
    refs, (keep, give, up_ref, down_ref, bias_ref, stage, sems) = refs[:-7], refs[-7:]
    tensor = plan.tensor
    pick_hidden(weights, expand, reduce, up_ref, down_ref)
    grad_y = dy_ref[...]
    grad_r = grad_y.astype(BF16)
    l = l_ref[...]
    t = lax.axis_index("tensor")
    grad_l = None
    for k in range(tensor):
        gate, slope = gelu_both(mm(l, up_ref[k]))
        hidden = gate.astype(BF16)
        grad_pre = (slope * mm_tr(grad_r, down_ref[k])).astype(BF16)
        z = t ^ k
        store_rows(stage, each, z, 0, mm_tl(l, grad_pre))
        store_rows(stage, each, z, l.shape[1], mm_tl(hidden, grad_r))
        back = mm_tr(grad_pre, up_ref[k])
        grad_l = back if grad_l is None else grad_l + back
    normed, inverse = norm(m_ref[...])
    grad, dgain = norm_back(grad_l, wide_row(gain), normed, inverse)
    dgain_ref[...] = dgain
    grad = grad_y + grad
    dm_out[...] = grad
    store_back(plan, heads, resets, videos, grad, mixed, output, query, probs, pairs, *refs, bias_ref)
    send_stage(stage, keep, give, sems)


def store_tail(stage, each, tensor, start, values):
    rows = values.shape[0] // tensor
    for z in range(tensor):
        for c in range(values.shape[1] // LANES):
            part = values[z * rows : (z + 1) * rows, c * LANES : (c + 1) * LANES]
            store_rows(stage, each, 0, start + c * rows, part, z * each)
    return start + values.shape[1] // LANES * rows


def load_rows(whole, each, start, count, base=0):
    half = whole.shape[1]
    parts, at = [], 0
    while at < count:
        who, off = divmod(start + at, each)
        n = min(each - off, count - at)
        parts.append(whole[who // half, who % half, base + off : base + off + n, :].astype(F32))
        at += n
    return parts


def across_index():
    index = 0
    for axis in ACROSS:
        index = index * lax.axis_size(axis) + lax.axis_index(axis)
    return index


def unpack_columns(whole, each, base, start, out):
    rows = out.shape[0]
    for c in range(out.shape[1] // LANES):
        at = 0
        for part in load_rows(whole, each, start + c * rows, rows, base):
            out[at : at + part.shape[0], c * LANES : (c + 1) * LANES] = part
            at += part.shape[0]
    return start + out.shape[1] // LANES * rows


def unpack_body(groups, *refs):
    core, across = lax.axis_index("core"), across_index()
    half = refs[-1].shape[1]
    pieces, refs = refs[: 2 * half], refs[2 * half :]
    count = sum(n for _, n in groups)
    outs, small, whole = refs[:count], refs[count:-1], refs[-1]
    sums, small = (small[-1], small[:-1]) if small else (None, small)
    for i, ref in enumerate(pieces):
        whole[(i // half) ^ core, (i % half) ^ across] = ref[...]
    base, first = 0, 0
    for each, n in groups:
        at = 0
        for out in outs[first : first + n]:
            at = unpack_columns(whole, each, base, at, out)
        base, first = base + each, first + n
    if sums is None:
        return
    at = 0
    for part in load_rows(whole, whole.shape[2] - base, 0, sums.shape[0], base):
        sums[at : at + part.shape[0]] = part
        at += part.shape[0]
    gain_a, pool_a, squeeze_a, table_a, mid_a, gain_b, pool_b, squeeze_b, table_b, mid_b = small
    for i, ref in enumerate((gain_a, mid_a, gain_b)):
        ref[...] = sums[i]
    for i in range(2):
        half = slice(i * LANES, (i + 1) * LANES)
        mid_b[half] = sums[3 + i]
        pool_a[i] = sums[8 + 4 * i : 12 + 4 * i, :]
        squeeze_a[i] = sums[16 + 4 * i : 20 + 4 * i, :]
        for j in range(3):
            pool_b[j, :, half] = sums[24 + 16 * i + 4 * j : 28 + 16 * i + 4 * j, :]
        for j in range(2):
            squeeze_b[j, :, half] = sums[56 + 8 * i + 4 * j : 60 + 8 * i + 4 * j, :]
    for ref, at in ((table_a, 72), (table_b, 80)):
        ref[...] = sums[at : at + ref.shape[0], : ref.shape[1]]


def leave_body(plan, each, small_each, *refs):
    refs = list(refs)
    pieces = plan.returned
    grads, refs = refs[:pieces], refs[pieces:]
    (dq, dm, doutput, n_ref, x_ref, gain, project, pools, squeeze, order, out,
     dgain_mid, dtable, dgain_b, dpool_b, dsqueeze_b, dmid_b, dtable_b) = refs[:18]
    refs = refs[18:]
    given = refs.pop(0) if not plan.local_squeeze else None
    send_ref, keep, give, dpool_ref, dsqueeze_ref, sum_ref, stage, sems = refs
    tensor = plan.tensor
    width = x_ref.shape[1]
    n = n_ref[...]
    grad, memory = pair_grads(plan, grads)
    raw = mm(n, project[:, width:])
    parts = [dq[...].astype(BF16)]
    parts += unpool(plan, raw, grad, memory, pools, squeeze, dpool_ref, dsqueeze_ref, 0)
    at = 0
    grad_n = None
    for i, part in enumerate(parts):
        at = store_tail(stage, each, tensor, at, mm_tl(n, part))
        back = mm_tr(part, project[:, i * width : (i + 1) * width])
        grad_n = back if grad_n is None else grad_n + back
    store_tail(stage, each, tensor, at, doutput[...])
    normed, inverse = norm(x_ref[...].astype(F32))
    grad_x, dgain = norm_back(grad_n, wide_row(gain), normed, inverse)
    grad_x = (grad_x + dm[...]).astype(BF16)
    leaving = jnp.concatenate([grad_x, out[:, :width], out[:, width:]], axis=0)
    send_ref[...] = mm_tl(order[...], leaving).astype(BF16)
    sum_ref[...] = jnp.zeros(sum_ref.shape, F32)
    squeeze_a = dsqueeze_ref if given is None else given
    sum_ref[0:1, :] = dgain
    sum_ref[1:2, :] = dgain_mid[...]
    sum_ref[2:3, :] = dgain_b[...]
    for i in range(2):
        half = slice(i * width, (i + 1) * width)
        sum_ref[3 + i : 4 + i, :] = dmid_b[:, half]
        sum_ref[8 + 4 * i : 12 + 4 * i, :] = dpool_ref[i]
        sum_ref[16 + 4 * i : 20 + 4 * i, :] = squeeze_a[i]
        for j in range(3):
            sum_ref[24 + 16 * i + 4 * j : 28 + 16 * i + 4 * j, :] = dpool_b[j, :, half]
        for j in range(2):
            sum_ref[56 + 8 * i + 4 * j : 60 + 8 * i + 4 * j, :] = dsqueeze_b[j, :, half]
    sum_ref[72:80, :128] = dtable[...]
    sum_ref[80:88, :128] = dtable_b[...]
    store_rows(stage, small_each, 0, 0, sum_ref[...], tensor * each)
    send_stage(stage, keep, give, sems)


def exchange(values, axes, by):
    axes = (axes,) if isinstance(axes, str) else axes
    order = [axis for axis in EVERY if axis in axes]
    sizes = [lax.axis_size(axis) for axis in axes]
    into = [axes.index(axis) for axis in order]
    place = np.arange(np.prod(sizes)).reshape(sizes).transpose(into).reshape(-1)
    where = np.argsort(place)
    return lax.ppermute(values, tuple(order), [(i, int(where[p ^ by])) for i, p in enumerate(place)])


def to_core(values):
    return exchange(values, "core", 1)


def swap(values):
    cores, near = lax.axis_size("core"), lax.axis_size("near")
    assert cores == near
    pairs = [(i * near + j, j * near + i) for i in range(cores) for j in range(near)]
    return lax.ppermute(values, ("core", "near"), pairs)


def shift(values, by):
    chips, cores, far, near, tensor = (lax.axis_size(axis) for axis in EVERY)
    clips = chips * near * tensor

    def place(g, core, f):
        chip, n = divmod(g // tensor, near)
        return (((chip * cores + core) * far + f) * near + n) * tensor + g % tensor

    pairs = [
        (place(g, core, f), place(g + by, core, f))
        for g in range(clips)
        for core in range(cores)
        for f in range(far)
        if 0 <= g + by < clips
    ]
    return lax.ppermute(values, EVERY, pairs)


def relative_weights(plan, squeeze):
    s = lax.axis_index(FRAMES)
    order = jnp.arange(plan.all_frames)
    frame = ((s ^ (order // plan.frames)) * plan.frames + order % plan.frames) % 4
    pair = jnp.concatenate([squeeze[0], squeeze[1]], axis=-1)
    return pair[frame], frame


def share_pairs(plan, pair, squeeze):
    pairs = [pair[0]] + [exchange(pair[0], FRAMES, o) for o in range(1, plan.seq)]
    if plan.local_squeeze:
        memories = [shift(pair[1], by) for by in (1, 2)]
        return pairs + [exchange(each, FRAMES, o) if o else each for each in memories for o in range(plan.seq)]
    memory = squeeze_all(plan, pairs, squeeze)
    return pairs + [shift(memory, 1), shift(memory, 2)]


def by_frame(plan, pairs):
    together = jnp.concatenate([each.astype(F32) for each in pairs], axis=0)
    return together.reshape(plan.all_frames // 4, 4, plan.cells, -1)


def squeeze_all(plan, pairs, squeeze):
    weights = relative_weights(plan, squeeze)[0].reshape(plan.all_frames // 4, 4, 1, -1)
    total = jnp.sum(by_frame(plan, pairs) * weights, axis=1)
    return total.reshape(plan.memory, -1).astype(BF16)


def return_pairs(plan, grads, pairs, squeeze):
    own, others, memories = grads[0], grads[1 : plan.seq], grads[plan.seq :]
    memories = [shift(memories[0], -1), shift(memories[1], -2)]
    if plan.local_squeeze:
        received = [exchange(each, FRAMES, o + 1) for o, each in enumerate(others)]
        memories = [exchange(each, FRAMES, o) if o else each for each in memories for o in range(plan.seq)]
        return [own] + received + memories, None
    memory = memories[0].astype(F32) + memories[1].astype(F32)
    weights, frame = relative_weights(plan, squeeze)
    weights = weights.reshape(plan.all_frames // 4, 4, 1, -1)
    memory = memory.reshape(plan.all_frames // 4, 1, plan.cells, -1)
    both = by_frame(plan, [own, *others]) + memory * weights
    both = jnp.split(both.reshape(plan.own, -1), plan.seq, axis=0)
    sums = jnp.sum(by_frame(plan, pairs[: plan.seq]) * memory, axis=2).reshape(plan.all_frames, -1)
    onehot = (frame[None, :] == jnp.arange(4)[:, None]).astype(F32)
    sums = jnp.dot(onehot, sums, precision=HIGHEST)
    width = sums.shape[1] // 2
    received = [
        exchange(each.astype(BF16), FRAMES, o + 1) for o, each in enumerate(both[1:])
    ]
    return [both[0]] + received, jnp.stack([sums[:, :width], sums[:, width:]])


def sum_first(values):
    return jnp.sum(values.astype(F32), axis=0).astype(BF16)


def spread(values, axes):
    return lax.all_to_all(values, axes, 0, 0, tiled=True)


def after(value, *others):
    return lax.optimization_barrier((value, others))[0]


def sum_cores(keep, give):
    return (keep.astype(F32) + to_core(give).astype(F32)).astype(BF16)


def gather_plane(values):
    mine = [exchange(values, ACROSS, k) if k else values for k in range(lax.axis_size(ACROSS))]
    return mine + [to_core(each) for each in mine]


def padded(rows, parts):
    return -(-rows // (16 * parts)) * 16


def local(
    clips_in, cotangent, resets, videos,
    attend_gain_a, project_a, pooling_a, squeeze_a, offsets_a, output_a, mixer_gain_a, expand_a, reduce_a,
    attend_gain_b, project_b, pooling_b, squeeze_b, offsets_b, output_b, shortcut_b, mixer_gain_b, expand_b, reduce_b,
):
    seq, tensor, plane = lax.axis_size(FRAMES), lax.axis_size("tensor"), lax.axis_size(PLANE)
    plan = Plan(seq, tensor, clips_in.shape)
    width, wide = clips_in.shape[-1], cotangent.shape[-1]
    heads_a, heads_b = offsets_a.shape[0], offsets_b.shape[0]
    core = lax.axis_index("core")
    tokens, pooled, keys, memory = plan.tokens, plan.pooled, plan.keys, plan.memory
    order = jnp.asarray(plan.arrange(), BF16)
    home = ("tensor",) + FRAMES
    leaving = jnp.concatenate(
        [clips_in.reshape(plan.group, -1, width), cotangent.reshape(plan.group, -1, width)], axis=1
    )
    arrived = spread(swap(leaving), home)
    half = jnp.where(core == 0, expand_a, reduce_a)
    half, arrived = lax.optimization_barrier((half, arrived))
    arrived = arrived.reshape(-1, width)
    quarter = half.reshape(2, -1, half.shape[1])[lax.axis_index("near")]
    mine = [exchange(quarter, "tensor", k) for k in range(1, tensor)]
    pair = lambda w: [((pooled, 2 * w), BF16)] + [((memory // seq, 2 * w), BF16)] * plan.local_squeeze
    x, cot, n_a, q_a, *pair_a = call(
        "enter",
        functools.partial(enter_body, plan),
        [((tokens, width), BF16), ((pooled, wide), BF16), ((tokens, width), BF16), ((tokens, width), BF16),
         *pair(width)],
        [arrived, order, attend_gain_a, project_a, pooling_a, squeeze_a],
    )
    pairs_a = share_pairs(plan, pair_a, squeeze_a)
    hidden = [((tensor, width, expand_a.shape[1]), BF16), ((tensor, reduce_a.shape[0], width), BF16)]
    or_a, m_a, l_a, probs_a = call(
        "first",
        functools.partial(first_body, plan, heads_a),
        [((tokens, width), BF16), ((tokens, width), F32), ((tokens, width), BF16), ((heads_a * tokens, keys), BF16)],
        [x, q_a, *pairs_a, offsets_a, output_a, mixer_gain_a],
        [resets, videos],
        [((8, 128), F32)],
    )
    mine, pairs_a = lax.optimization_barrier((mine, pairs_a))
    weights = []
    for each in mine:
        other = exchange(each, "near", 1)
        weights += [each, to_core(each), other, to_core(other)]
    y_a, n_b, q_b, base, *pair_b = call(
        "between",
        functools.partial(between_body, plan),
        [((tokens, width), F32), ((tokens, width), BF16), ((pooled, wide), BF16), ((pooled, wide), F32), *pair(wide)],
        [m_a, l_a, expand_a, reduce_a, *weights, attend_gain_b, project_b, pooling_b, squeeze_b, shortcut_b],
        (),
        hidden,
    )
    pairs_b = share_pairs(plan, pair_b, squeeze_b)
    or_b, m_b, rows_b, probs_b = call(
        "second",
        functools.partial(second_body, plan, heads_b),
        [((pooled, wide), BF16), ((pooled, wide), F32), ((pooled, 2 * wide), BF16),
         ((heads_b * pooled, keys), BF16)],
        [q_b, *pairs_b, offsets_b, output_b, mixer_gain_b, base, cot],
        [resets, videos],
        [((8, 128), F32)],
    )
    rows_all = lax.all_gather(rows_b, "tensor", axis=0, tiled=True)
    hidden_rows = (expand_b.shape[1] // LANES) * wide + (wide // LANES) * reduce_b.shape[0]
    half_plane = plane // 2
    hidden_each = padded(hidden_rows, plane)
    shares, keep, give = call(
        "hidden",
        functools.partial(hidden_body, hidden_each),
        [((tensor * pooled, 2 * wide), BF16)],
        [rows_all, expand_b, reduce_b],
        stage=(2, half_plane, 1, hidden_each, LANES),
    )
    sums = spread(shares, "tensor")
    early = spread(after(sum_cores(keep, give), sums), ACROSS)
    sums = sums.reshape(tensor, pooled, 2 * wide)
    bias = lambda: [((plan.frames, 8, keys), F32)]
    key_grads = lambda w: (
        [((pooled, 2 * w), F32)] + [((pooled, 2 * w), BF16)] * (seq - 1) + [((memory, 2 * w), BF16)] * 2
    )
    out, dm_b, dmid_b, doutput_b, dq_b, dtable_b, *back = call(
        "second_back",
        functools.partial(second_back_body, plan, heads_b),
        [((pooled, wide), BF16), ((pooled, wide), F32), ((1, wide), F32), ((wide, wide), BF16), ((pooled, wide), F32),
         ((8, 128), F32), *key_grads(wide)],
        [sums, cot, m_b, mixer_gain_b, or_b, output_b, q_b, probs_b, *pairs_b],
        [resets, videos],
        bias(),
    )
    pieces, dsqueeze_given = return_pairs(plan, back, pairs_b, squeeze_b)
    dq_b = after(dq_b, early)
    early = gather_plane(sum_first(early)[0])
    share = width // tensor
    cross_each = padded((3 + 1) * wide // LANES * share + wide // LANES * (wide // tensor), plane)
    dy_a, dpool_b, dsqueeze_b, dgain_b, keep, give = call(
        "cross",
        functools.partial(cross_body, plan, cross_each),
        [((tokens, width), F32), ((3, 4, wide), F32), ((2, 4, wide), F32), ((1, width), F32)],
        [*pieces, dq_b, dm_b, doutput_b, n_b, y_a, attend_gain_b, project_b, pooling_b, squeeze_b, shortcut_b],
        stage=(2, half_plane, tensor, cross_each, LANES),
    )
    cross = spread(sum_cores(keep, give), ACROSS)
    first_each = padded(2 * width, plane)
    dmid_a, dm_a, doutput_a, dq_a, dtable_a, *back, keep, give = call(
        "first_back",
        functools.partial(first_back_body, plan, first_each, heads_a),
        [((1, width), F32), ((tokens, width), F32), ((width, width), BF16), ((tokens, width), F32), ((8, 128), F32),
         *key_grads(width)],
        [dy_a, m_a, l_a, mixer_gain_a, or_a, output_a, q_a, probs_a, expand_a, reduce_a, *weights,
         *pairs_a],
        [resets, videos],
        hidden + bias(),
        stage=(2, half_plane, tensor, first_each, LANES),
    )
    first = spread(after(sum_cores(keep, give), cross), ACROSS)
    grad_expand_b, grad_reduce_b = call(
        "unpack_early",
        functools.partial(unpack_body, [(hidden_each, 2)]),
        [(expand_b.shape, F32), (reduce_b.shape, F32)],
        early,
        (),
        [((2, half_plane, hidden_each, LANES), BF16)],
    )
    if dsqueeze_given is not None:
        dsqueeze_b = dsqueeze_given
    pieces, dsqueeze_given = return_pairs(plan, back, pairs_a, squeeze_a)
    tail_each, small_each = padded(4 * share, plane), padded(128, plane)
    leaving, keep, give = call(
        "leave",
        functools.partial(leave_body, plan, tail_each, small_each),
        [(arrived.shape, BF16)],
        [*pieces, dq_a, dm_a, doutput_a, n_a, x, attend_gain_a, project_a, pooling_a, squeeze_a, order, out,
         dmid_a, dtable_a, dgain_b, dpool_b, dsqueeze_b, dmid_b, dtable_b]
        + ([] if dsqueeze_given is None else [dsqueeze_given]),
        (),
        [((2, 4, width), F32), ((2, 4, width), F32), ((128, LANES), F32)],
        stage=(2, half_plane, 1, tensor * tail_each + small_each, LANES),
    )
    last = spread(after(sum_cores(keep, give), first), ACROSS)
    cross, first = sum_first(cross), sum_first(first)
    last = sum_first(last)[0]
    small = jnp.broadcast_to(last[None, tensor * tail_each :], (tensor, small_each, LANES))
    last = last[: tensor * tail_each].reshape(tensor, tail_each, LANES)
    last = spread(jnp.concatenate([cross, first, last, small], axis=1), "tensor")
    leaving = after(leaving, last)
    late = gather_plane(sum_first(last))
    returned = swap(spread(leaving.reshape(plan.group, -1, width), home))
    x_rows = plan.frames * plan.rows * plan.cols
    grad_input = returned[:, :x_rows].reshape(clips_in.shape).astype(F32)
    result = returned[:, x_rows:].reshape(cotangent.shape).astype(F32)
    column = lambda rows, columns: ((rows, columns), F32)
    (
        grad_project_b, grad_shortcut_b, grad_output_b, grad_expand_a, grad_reduce_a, grad_project_a, grad_output_a,
        *small,
    ) = call(
        "unpack",
        functools.partial(unpack_body, [(cross_each, 3), (first_each, 2), (tail_each, 2)]),
        [
            column(share, 3 * wide), column(share, wide), column(wide // tensor, wide), (expand_a.shape, F32),
            (reduce_a.shape, F32), column(share, 3 * width), column(share, width),
            ((width,), F32), (pooling_a.shape, F32), (squeeze_a.shape, F32), (offsets_a.shape, F32), ((width,), F32),
            ((width,), F32), (pooling_b.shape, F32), (squeeze_b.shape, F32), (offsets_b.shape, F32), ((wide,), F32),
        ],
        late,
        (),
        [((128, LANES), F32), ((2, half_plane, cross_each + first_each + tail_each + small_each, LANES), BF16)],
    )
    return (
        result,
        grad_input,
        small[0],
        grad_project_a,
        small[1],
        small[2],
        small[3],
        grad_output_a,
        small[4],
        grad_expand_a,
        grad_reduce_a,
        small[5],
        grad_project_b,
        small[6],
        small[7],
        small[8],
        grad_output_b,
        grad_shortcut_b,
        small[9],
        grad_expand_b,
        grad_reduce_b,
    )


def solution(mesh):
    clip, seq, tensor = mesh.devices.shape
    split = Mesh(mesh.devices.reshape(clip // 2, 2, seq // 2, 2, tensor), EVERY)
    field = P(("chip", "core"), None, ("far", "near"), "tensor", None)
    up, down = P(None, "tensor"), P("tensor", None)
    block = (P(), P(), P(), P(), P(), P(), P(), up, down)
    block_b = (P(), P(), P(), P(), P(), P(), P(), P(), up, down)
    grads = (P(), down, P(), P(), P(), down, P(), up, down)
    grads_b = (P(), down, P(), P(), P(), down, down, P(), up, down)
    return jax.shard_map(
        local,
        mesh=split,
        in_specs=(field, field, P(), P()) + block + block_b,
        out_specs=(field, field) + grads + grads_b,
        check_vma=False,
    )
```

```python
import functools

import jax
import jax.numpy as jnp
import numpy as np
from jax import lax
from jax.experimental import pallas as pl
from jax.experimental.pallas import tpu as pltpu
from jax.sharding import Mesh
from jax.sharding import PartitionSpec as P

F32 = jnp.float32
BF16 = jnp.bfloat16
HIGHEST = lax.Precision.HIGHEST
EPSILON = 1e-06
MASKED = -1000000000.0
LOG_FOUR = 1.3862943611198906
SIZE = 96
LANES = 384
INTERPRET = False
PLANE = ("chip", "core", "far", "near")
EVERY = PLANE + ("tensor",)
ACROSS = ("chip", "far", "near")
FRAMES = ("far", "core")
FEW = 8
COSTS = {
    "enter": 3, "first": 4, "between": 6, "second": 7, "hidden": 4, "hidden_rest": 5, "second_back": 9, "cross": 8,
    "first_back": 10, "leave": 5, "exit": 2,
}


def wide_row(gain):
    return gain[...].reshape(1, gain.shape[0])


def log2(n):
    return n.bit_length() - 1


def mm(left, right):
    return jnp.dot(left, right, preferred_element_type=F32)


def mm_tl(left, right):
    return lax.dot_general(left, right, (((0,), (0,)), ((), ())), preferred_element_type=F32)


def mm_tr(left, right):
    return lax.dot_general(left, right, (((1,), (1,)), ((), ())), preferred_element_type=F32)


def norm(field):
    mean = jnp.mean(field, axis=-1, keepdims=True)
    centered = field - mean
    inverse = lax.rsqrt(jnp.mean(centered * centered, axis=-1, keepdims=True) + EPSILON)
    return centered * inverse, inverse


def norm_back(grad, gain, normed, inverse):
    scaled = grad * gain
    field = inverse * (
        scaled
        - jnp.mean(scaled, axis=-1, keepdims=True)
        - normed * jnp.mean(scaled * normed, axis=-1, keepdims=True)
    )
    return field, jnp.sum(grad * normed, axis=0, keepdims=True)


def gelu(values):
    return 0.5 * values * (1.0 + lax.erf(values * 0.7071067811865476))


def gelu_both(values):
    half = 0.5 * (1.0 + lax.erf(values * 0.7071067811865476))
    slope = half + values * jnp.exp(-0.5 * values * values) * 0.3989422804014327
    return values * half, slope


def blocks(values, count):
    rows = values.shape[0] // count
    return [values[i * rows : (i + 1) * rows] for i in range(count)]


def pool(values, weights):
    parts = blocks(values, 4)
    total = parts[0] * weights[0:1]
    for p in range(1, 4):
        total = total + parts[p] * weights[p : p + 1]
    return total


class Plan:
    def __init__(self, seq, tensor, shape):
        clips, frames, rows, cols, _ = shape
        self.seq, self.tensor = seq, tensor
        assert clips == tensor and frames % seq == 0 and rows % 2 == 0 and cols % 2 == 0
        self.all_frames = frames
        self.frames = frames // seq
        self.rows, self.cols = rows, cols
        self.group = seq * tensor
        self.cells = self.group * rows * cols // 4
        self.pooled = self.frames * self.cells
        self.tokens = 4 * self.pooled
        self.local_squeeze = self.frames % 4 == 0
        self.memory = frames // 4 * self.cells
        self.own = seq * self.pooled
        self.sources = seq + 2 * (seq if self.local_squeeze else 1)
        self.returned = seq + (2 * seq if self.local_squeeze else 0)
        self.keys = self.own + 2 * self.memory
        for n in (self.cells, self.pooled, self.memory, self.own, self.frames, seq):
            assert n == 1 << log2(n)

    def arrange(self):
        take = np.arange(self.tokens).reshape(
            self.group, self.frames, self.rows // 2, 2, self.cols // 2, 2
        )
        per = self.frames * self.rows * self.cols
        half = per // 4 * 2
        step = per + half
        x_rows = take // per * step + take % per
        x_rows = x_rows.transpose(3, 5, 1, 0, 2, 4).reshape(-1)
        cot = np.arange(self.pooled).reshape(self.group, self.frames, -1)
        low = cot // (per // 4) * step + per + cot % (per // 4) * 2
        low = low.transpose(1, 0, 2).reshape(-1)
        order = np.concatenate([x_rows, low, low + 1])
        return (order[:, None] == np.arange(self.group * step)[None, :]).astype(np.float32)


def clip_scalars(plan, resets, videos):
    s = lax.axis_index("far") * lax.axis_size("core") + lax.axis_index("core")
    chip = lax.axis_index("chip") * lax.axis_size("near") + lax.axis_index("near")
    g = chip * plan.tensor + lax.axis_index("tensor")
    before = jnp.maximum(g - 1, 0)
    earlier = jnp.maximum(g - 2, 0)
    first = (g >= 1) & (videos[g] == videos[before]) & (resets[g] == 0)
    second = first & (g >= 2) & (videos[before] == videos[earlier]) & (resets[before] == 0)
    return s, first.astype(jnp.int32), second.astype(jnp.int32)


def key_facts(plan, s, first, second):
    k = lax.broadcasted_iota(jnp.int32, (1, plan.keys), 1)
    own_time = ((s ^ (k >> log2(plan.pooled))) << log2(plan.frames)) + (
        (k & (plan.pooled - 1)) >> log2(plan.cells)
    )
    m = k - plan.own
    late = (m >> log2(plan.memory)) > 0
    g = (m & (plan.memory - 1)) >> log2(plan.cells)
    if plan.local_squeeze:
        each = log2(plan.frames // 4)
        squeezed = ((s ^ (g >> each)) << each) + (g & (plan.frames // 4 - 1))
    else:
        squeezed = (s >> log2(4 // plan.frames)) ^ g
    kind = jnp.where(m < 0, 0, jnp.where(late, 2, 1))
    time = jnp.where(m < 0, own_time, 4 * squeezed - plan.all_frames * kind)
    counts = jnp.where(kind == 0, 1, jnp.where(kind == 1, first, second))
    return time, counts


def offset_onehot(plan, s, time, frame):
    index = s * plan.frames + frame - time + plan.all_frames - 1
    rows = lax.broadcasted_iota(jnp.int32, (128, plan.keys), 0)
    return jnp.where(rows == index, 1.0, 0.0).astype(F32)


def head_mask(width, head):
    lane = lax.broadcasted_iota(jnp.int32, (1, width), 1)
    inside = (lane >= head * SIZE) & (lane < (head + 1) * SIZE)
    return jnp.where(inside, 1.0, 0.0).astype(F32)


def attend(plan, query, keys, values, offsets, heads, probs_ref, table_ref, scalars):
    s, first, second = scalars
    rows, width = query.shape
    places = rows // plan.pooled
    time, counts = key_facts(plan, s, first, second)
    biases = []
    table_ref[...] = jnp.zeros(table_ref.shape, F32)
    table_ref[:heads, : offsets.shape[1]] = offsets[...]
    table = table_ref[...]
    for f in range(plan.frames):
        onehot = offset_onehot(plan, s, time, f)
        bias = jnp.dot(table, onehot, precision=HIGHEST, preferred_element_type=F32)
        biases.append(jnp.where(counts > 0, bias, MASKED))
    total = query.astype(F32)
    for h in range(heads):
        mask = head_mask(width, h)
        scores = mm_tr(query * mask.astype(BF16), keys) * SIZE ** (-0.5)
        bias = jnp.concatenate(
            [jnp.broadcast_to(b[h : h + 1], (plan.cells, plan.keys)) for b in biases] * places, axis=0
        )
        scores = scores + bias
        scores = jnp.exp(scores - jnp.max(scores, axis=-1, keepdims=True))
        probs = scores * (1.0 / jnp.sum(scores, axis=-1, keepdims=True))
        probs = probs.astype(BF16)
        probs_ref[h * rows : (h + 1) * rows] = probs
        total = total + mm(probs, values) * mask
    return total


def attend_back(plan, grad, query, keys, values, probs_ref, heads, bias_ref, table_ref, scalars):
    s, first, second = scalars
    rows, width = query.shape
    places = rows // plan.pooled
    grad_r = grad.astype(BF16)
    grad_query = grad
    grad_keys = jnp.zeros((plan.keys, width), F32)
    grad_values = jnp.zeros((plan.keys, width), F32)
    bias_ref[...] = jnp.zeros(bias_ref.shape, F32)
    for h in range(heads):
        mask = head_mask(width, h)
        mask_r = mask.astype(BF16)
        grad_head = grad_r * mask_r
        query_head = query * mask_r
        probs_r = probs_ref[h * rows : (h + 1) * rows]
        probs = probs_r.astype(F32)
        grad_probs = mm_tr(grad_head, values)
        weighted = probs * grad_probs
        grad_scores = weighted - probs * jnp.sum(weighted, axis=-1, keepdims=True)
        for f in range(plan.frames):
            part = grad_scores[f * plan.cells : (f + 1) * plan.cells]
            for p in range(1, places):
                at = p * plan.pooled + f * plan.cells
                part = part + grad_scores[at : at + plan.cells]
            bias_ref[f, h : h + 1, :] = jnp.sum(part, axis=0, keepdims=True)
        grad_scores_r = grad_scores.astype(BF16)
        grad_query = grad_query + mm(grad_scores_r, keys) * (mask * SIZE ** (-0.5))
        grad_keys = grad_keys + mm_tl(grad_scores_r, query_head)
        grad_values = grad_values + mm_tl(probs_r, grad_head)
    time, _ = key_facts(plan, s, first, second)
    table = jnp.zeros((8, 128), F32)
    for f in range(plan.frames):
        onehot = offset_onehot(plan, s, time, f)
        table = table + lax.dot_general(
            bias_ref[f], onehot, (((1,), (1,)), ((), ())), precision=HIGHEST, preferred_element_type=F32
        )
    table_ref[...] = table
    return grad_query, grad_keys * SIZE ** (-0.5), grad_values


def load_pairs(refs, width):
    pairs = jnp.concatenate([ref[...] for ref in refs], axis=0)
    return pairs[:, :width], pairs[:, width:]


def pool_pair(plan, raw, pool_ref, squeeze_ref, pair_ref, memory_ref=None):
    width = raw.shape[1] // 2
    for i in range(2):
        pooled = pool(raw[:, i * width : (i + 1) * width], pool_ref[pool_ref.shape[0] - 2 + i])
        pair_ref[:, i * width : (i + 1) * width] = pooled.astype(BF16)
        if memory_ref is not None:
            weights = squeeze_ref[i]
            for g in range(plan.frames // 4):
                total = None
                for k in range(4):
                    at = (4 * g + k) * plan.cells
                    part = pooled[at : at + plan.cells] * weights[k : k + 1]
                    total = part if total is None else total + part
                at = g * plan.cells
                memory_ref[at : at + plan.cells, i * width : (i + 1) * width] = total.astype(BF16)


def store_rows(stage, each, z, start, values, base=0):
    core = lax.axis_index("core")
    half, at = stage.shape[1], 0
    while at < values.shape[0]:
        who, off = divmod(start + at, each)
        n = min(each - off, values.shape[0] - at)
        part = values[at : at + n].astype(BF16)
        rows = pl.ds(base + off if isinstance(base, int) else pl.multiple_of(base + off, 16), n)
        stage[(who // half) ^ core, who % half, z, rows, :] = part
        at += n


def store_columns(stage, each, tensor, start, values):
    rows = values.shape[0] // tensor
    t = lax.axis_index("tensor")
    for z in range(tensor):
        for c in range(values.shape[1] // LANES):
            part = values[z * rows : (z + 1) * rows, c * LANES : (c + 1) * LANES]
            store_rows(stage, each, z ^ t, start + c * rows, part)
    return start + values.shape[1] // LANES * rows


def send_stage(stage, keep, give, sems):
    copies = [pltpu.make_async_copy(stage.at[i], (keep, give)[i], sems.at[i]) for i in range(2)]
    for copy in copies:
        copy.start()
    for copy in copies:
        copy.wait()


def smooth_max(raw):
    parts = blocks(raw, 4)
    highest = jnp.maximum(jnp.maximum(parts[0], parts[1]), jnp.maximum(parts[2], parts[3]))
    total = jnp.exp(parts[0] - highest)
    for p in range(1, 4):
        total = total + jnp.exp(parts[p] - highest)
    return highest + jnp.log(total) - LOG_FOUR


def smooth_max_back(raw, grad):
    parts = blocks(raw, 4)
    highest = jnp.maximum(jnp.maximum(parts[0], parts[1]), jnp.maximum(parts[2], parts[3]))
    parts = [jnp.exp(part - highest) for part in parts]
    total = parts[0] + parts[1] + parts[2] + parts[3]
    scaled = grad / total
    return jnp.concatenate([part * scaled for part in parts], axis=0)


def call(name, body, outs, vmem, smem=(), scratch=(), stage=None):
    moved = COSTS.get(name, 4) * 3_000_000
    scratch = [pltpu.VMEM(shape, dtype) for shape, dtype in scratch]
    spaces = [pltpu.VMEM] * len(outs)
    if stage is not None:
        outs = outs + [(stage[1:], BF16)] * 2
        spaces += [pl.ANY] * 2
        scratch += [pltpu.VMEM(stage, BF16), pltpu.SemaphoreType.DMA((2,))]
    return pl.pallas_call(
        body,
        out_shape=[jax.ShapeDtypeStruct(shape, dtype) for shape, dtype in outs],
        in_specs=[pl.BlockSpec(memory_space=pltpu.SMEM)] * len(smem)
        + [pl.BlockSpec(memory_space=pltpu.VMEM)] * len(vmem),
        out_specs=[pl.BlockSpec(memory_space=space) for space in spaces],
        scratch_shapes=scratch,
        name=name,
        interpret=INTERPRET,
        cost_estimate=pl.CostEstimate(flops=0, bytes_accessed=moved, transcendentals=0),
        compiler_params=pltpu.CompilerParams(vmem_limit_bytes=56 << 20),
    )(*smem, *vmem)


def enter_body(plan, arrived, order, gain, project, pools, squeeze, x_ref, cot_ref, n_ref, q_ref, *pair):
    rows = mm(order[...], arrived[...])
    x = rows[: plan.tokens]
    x_ref[...] = x.astype(BF16)
    width = cot_ref.shape[1] // 2
    cot_ref[:, :width] = rows[plan.tokens : plan.tokens + plan.pooled].astype(BF16)
    cot_ref[:, width:] = rows[plan.tokens + plan.pooled :].astype(BF16)
    n = (norm(x)[0] * wide_row(gain)).astype(BF16)
    n_ref[...] = n
    raw = mm(n, project[...])
    q_ref[...] = raw[:, : x.shape[1]].astype(BF16)
    pool_pair(plan, raw[:, x.shape[1] :], pools, squeeze, *pair)


def pick_hidden(tensor, expand, reduce, weights, up_ref, down_ref):
    up_ref[0] = expand[...]
    down_ref[0] = reduce[...]
    core, near = lax.axis_index("core"), lax.axis_index("near")
    rows = weights[0].shape[0] // (tensor - 1)

    def put(first, second):
        for i, piece in enumerate(weights):
            at = pl.multiple_of(((i % 2) ^ near) * rows, 16)
            for k in range(1, tensor):
                part = piece[(k - 1) * rows : k * rows, :]
                (second if i // 2 else first)[k, pl.ds(at, rows), :] = part

    @pl.when(core == 0)
    def _():
        put(up_ref, down_ref)

    @pl.when(core != 0)
    def _():
        put(down_ref, up_ref)


def first_body(plan, heads, resets, videos, *refs):
    x, query = refs[:2]
    pairs, refs = refs[2 : 2 + plan.sources], refs[2 + plan.sources :]
    table, output, gain, or_ref, m_ref, l_ref, probs_ref, table_ref = refs
    scalars = clip_scalars(plan, resets, videos)
    keys, values = load_pairs(pairs, x.shape[1])
    mixed_r = attend(plan, query[...], keys, values, table, heads, probs_ref, table_ref, scalars).astype(BF16)
    or_ref[...] = mixed_r
    middle = x[...].astype(F32) + mm(mixed_r, output[...])
    m_ref[...] = middle
    l_ref[...] = (norm(middle)[0] * wide_row(gain)).astype(BF16)


def between_body(plan, m_ref, l_ref, expand, reduce, *refs):
    weights, refs = refs[:4], refs[4:]
    gain_b, project_b, pool_b, squeeze_b, shortcut_b, y_ref, nb_ref, qb_ref, base_ref = refs[:9]
    pair, up_ref, down_ref = refs[9:-2], refs[-2], refs[-1]
    pick_hidden(plan.tensor, expand, reduce, weights, up_ref, down_ref)
    l = l_ref[...]
    y = m_ref[...]
    for k in range(plan.tensor):
        hidden = gelu(mm(l, up_ref[k])).astype(BF16)
        y = y + mm(hidden, down_ref[k])
    y_ref[...] = y
    n = (norm(y)[0] * wide_row(gain_b)).astype(BF16)
    nb_ref[...] = n
    wide = base_ref.shape[1]
    raw = mm(n, project_b[...])
    qb_ref[...] = pool(raw[:, :wide], pool_b[0]).astype(BF16)
    pool_pair(plan, raw[:, wide:], pool_b, squeeze_b, *pair)
    base_ref[...] = smooth_max(mm(n, shortcut_b[...]))


def second_body(plan, heads, resets, videos, *refs):
    query, pairs, refs = refs[0], refs[1 : 1 + plan.sources], refs[1 + plan.sources :]
    table, output, gain, base, or_ref, m_ref, l_ref, probs_ref, table_ref = refs
    width = query.shape[1]
    scalars = clip_scalars(plan, resets, videos)
    keys, values = load_pairs(pairs, width)
    mixed_r = attend(plan, query[...], keys, values, table, heads, probs_ref, table_ref, scalars).astype(BF16)
    or_ref[...] = mixed_r
    middle = base[...] + mm(mixed_r, output[...])
    m_ref[...] = middle
    l_ref[...] = (norm(middle)[0] * wide_row(gain)).astype(BF16)


def hidden_body(tensor, up, down, *refs):
    rows, grads, refs = refs[:tensor], refs[tensor : 2 * tensor], refs[2 * tensor :]
    sends, (hidden_ref, grad_pre_ref) = refs[:tensor], refs[tensor:]
    l = jnp.concatenate([ref[...] for ref in rows], axis=0)
    grad = jnp.concatenate([ref[...] for ref in grads], axis=0)
    gate, slope = gelu_both(mm(l, up[...]))
    hidden_ref[...] = gate.astype(BF16)
    grad_pre = (slope * mm_tr(grad, down[...])).astype(BF16)
    grad_pre_ref[...] = grad_pre
    for ref, part in zip(sends, blocks(mm_tr(grad_pre, up[...]), tensor)):
        ref[...] = part.astype(BF16)


def hidden_rest_body(tensor, each, down, hidden_ref, grad_pre_ref, *refs):
    rows, grads, refs = refs[:tensor], refs[tensor : 2 * tensor], refs[2 * tensor :]
    sends, (keep, give, stage, sems) = refs[:tensor], refs[tensor:]
    hidden, grad_pre = hidden_ref[...], grad_pre_ref[...]
    l = jnp.concatenate([ref[...] for ref in rows], axis=0)
    grad = jnp.concatenate([ref[...] for ref in grads], axis=0)
    at = 0
    for whole in (mm_tl(l, grad_pre), mm_tl(hidden, grad)):
        for c in range(whole.shape[1] // LANES):
            part = whole[:, c * LANES : (c + 1) * LANES]
            store_rows(stage, each, 0, at, part)
            at += part.shape[0]
    for ref, part in zip(sends, blocks(mm(hidden, down[...]), tensor)):
        ref[...] = part.astype(BF16)
    send_stage(stage, keep, give, sems)


def sum_refs(refs):
    total = refs[0][...].astype(F32)
    for ref in refs[1:]:
        total = total + ref[...].astype(F32)
    return total


def second_back_body(plan, heads, resets, videos, *refs):
    refs = list(refs)
    sums, refs = refs[: plan.tensor], refs[plan.tensor :]
    cot, middle, gain, mixed, output, query, probs = refs[:7]
    pairs, refs = refs[7 : 7 + plan.sources], refs[7 + plan.sources :]
    dm_ref, dgain_ref = refs[:2]
    refs = refs[2:]
    normed, inverse = norm(middle[...])
    grad, dgain = norm_back(sum_refs(sums), wide_row(gain), normed, inverse)
    dgain_ref[...] = dgain
    grad = cot[...].astype(F32) + grad
    dm_ref[...] = grad
    store_back(plan, heads, resets, videos, grad, mixed, output, query, probs, pairs, *refs)


def store_back(plan, heads, resets, videos, grad, mixed, output, query, probs, pairs, doutput_ref, dq_ref, dtable_ref,
               *refs):
    width = query.shape[1]
    scalars = clip_scalars(plan, resets, videos)
    grad_r = grad.astype(BF16)
    doutput_ref[...] = mm_tl(mixed[...], grad_r).astype(BF16)
    grads, bias_ref = refs[:-1], refs[-1]
    keys, values = load_pairs(pairs, width)
    dq, dk, dv = attend_back(
        plan, mm_tr(grad_r, output[...]), query[...], keys, values, probs, heads, bias_ref, dtable_ref, scalars
    )
    dq_ref[...] = dq
    for i, part in enumerate((dk, dv)):
        lanes = slice(i * width, (i + 1) * width)
        at = 0
        for ref in grads:
            ref[:, lanes] = part[at : at + ref.shape[0]].astype(ref.dtype)
            at += ref.shape[0]


def pair_grads(plan, refs):
    own, received = refs[0], refs[1 : plan.seq]
    grad = own[...]
    for ref in received:
        grad = grad + ref[...].astype(F32)
    if not plan.local_squeeze:
        return grad, None
    memory = None
    size = plan.memory // plan.seq
    for i, ref in enumerate(refs[plan.seq :]):
        o = i % plan.seq
        part = ref[o * size : (o + 1) * size, :].astype(F32)
        memory = part if memory is None else memory + part
    return grad, memory


def unpool(plan, raw, grad, memory, pool_ref, squeeze_ref, dpool_ref, dsqueeze_ref, first):
    width = raw.shape[1] // 2
    result = []
    for i in range(2):
        weights = pool_ref[first + i]
        lanes = slice(i * width, (i + 1) * width)
        part = grad[:, lanes]
        source = raw[:, lanes]
        if plan.local_squeeze:
            pooled = pool(source, weights)
            ws = squeeze_ref[i]
            pieces = []
            sums = [None] * 4
            for g in range(plan.frames // 4):
                dm = memory[g * plan.cells : (g + 1) * plan.cells, lanes]
                for k in range(4):
                    at = (4 * g + k) * plan.cells
                    pieces.append(part[at : at + plan.cells] + dm * ws[k : k + 1])
                    total = jnp.sum(dm * pooled[at : at + plan.cells], axis=0, keepdims=True)
                    sums[k] = total if sums[k] is None else sums[k] + total
            part = jnp.concatenate(pieces, axis=0)
            for k in range(4):
                dsqueeze_ref[i, k : k + 1, :] = sums[k]
        result.append(unpool_one(source, part, weights, dpool_ref, first + i))
    return result


def unpool_one(source, part, weights, dpool_ref, place):
    pieces = []
    for p, piece in enumerate(blocks(source, 4)):
        dpool_ref[place, p : p + 1, :] = jnp.sum(part * piece, axis=0, keepdims=True)
        pieces.append((part * weights[p : p + 1]).astype(BF16))
    return jnp.concatenate(pieces, axis=0)


def cross_body(plan, each, *refs):
    pieces = plan.returned
    grads = refs[:pieces]
    (dq, dm, doutput_b, n_ref, y_ref, gain_b, project_b, pool_b, squeeze_b, shortcut_b,
     dy_ref, dpool_ref, dsqueeze_ref, dgain_ref, keep, give, stage, sems) = refs[pieces:]
    tensor = plan.tensor
    wide = dm.shape[1]
    n = n_ref[...]
    grad, memory = pair_grads(plan, grads)
    raw = mm(n, project_b[...])
    parts = [unpool_one(raw[:, :wide], dq[...], pool_b[0], dpool_ref, 0)]
    parts += unpool(plan, raw[:, wide:], grad, memory, pool_b, squeeze_b, dpool_ref, dsqueeze_ref, 1)
    at = 0
    grad_n = None
    for i, part in enumerate(parts):
        at = store_columns(stage, each, tensor, at, mm_tl(n, part))
        back = mm_tr(part, project_b[:, i * wide : (i + 1) * wide])
        grad_n = back if grad_n is None else grad_n + back
    grad_z = smooth_max_back(mm(n, shortcut_b[...]), dm[...]).astype(BF16)
    at = store_columns(stage, each, tensor, at, mm_tl(n, grad_z))
    store_columns(stage, each, tensor, at, doutput_b[...])
    grad_n = grad_n + mm_tr(grad_z, shortcut_b[...])
    normed, inverse = norm(y_ref[...])
    grad_y, dgain = norm_back(grad_n, wide_row(gain_b), normed, inverse)
    dgain_ref[...] = dgain
    dy_ref[...] = grad_y
    send_stage(stage, keep, give, sems)


def first_back_body(plan, each, heads, resets, videos, *refs):
    refs = list(refs)

    def take(n):
        taken = refs[:n]
        del refs[:n]
        return taken

    dy_ref, m_ref, l_ref, gain, mixed, output, query, probs, expand, reduce = take(10)
    weights = take(4)
    pairs = take(plan.sources)
    dgain_ref, dm_out = take(2)
    refs, (keep, give, up_ref, down_ref, bias_ref, stage, sems) = refs[:-7], refs[-7:]
    tensor = plan.tensor
    pick_hidden(tensor, expand, reduce, weights, up_ref, down_ref)
    grad_y = dy_ref[...]
    grad_r = grad_y.astype(BF16)
    l = l_ref[...]
    grad_l = None
    for k in range(tensor):
        gate, slope = gelu_both(mm(l, up_ref[k]))
        hidden = gate.astype(BF16)
        grad_pre = (slope * mm_tr(grad_r, down_ref[k])).astype(BF16)
        store_rows(stage, each, k, 0, mm_tl(l, grad_pre))
        store_rows(stage, each, k, l.shape[1], mm_tl(hidden, grad_r))
        back = mm_tr(grad_pre, up_ref[k])
        grad_l = back if grad_l is None else grad_l + back
    normed, inverse = norm(m_ref[...])
    grad, dgain = norm_back(grad_l, wide_row(gain), normed, inverse)
    dgain_ref[...] = dgain
    grad = grad_y + grad
    dm_out[...] = grad
    store_back(plan, heads, resets, videos, grad, mixed, output, query, probs, pairs, *refs, bias_ref)
    send_stage(stage, keep, give, sems)


def store_tail(stage, each, tensor, start, values):
    rows = values.shape[0] // tensor
    t = lax.axis_index("tensor")
    for z in range(tensor):
        for c in range(values.shape[1] // LANES):
            part = values[z * rows : (z + 1) * rows, c * LANES : (c + 1) * LANES]
            store_rows(stage, each, 0, start + c * rows, part, (z ^ t) * each)
    return start + values.shape[1] // LANES * rows


def load_rows(whole, each, start, count, base=0):
    half = whole.shape[1]
    parts, at = [], 0
    while at < count:
        who, off = divmod(start + at, each)
        n = min(each - off, count - at)
        parts.append(whole[who // half, who % half, base + off : base + off + n, :].astype(F32))
        at += n
    return parts


def across_index():
    index = 0
    for axis in ACROSS:
        index = index * lax.axis_size(axis) + lax.axis_index(axis)
    return index


def unpack_columns(whole, each, base, start, out):
    rows = out.shape[0]
    for c in range(out.shape[1] // LANES):
        at = 0
        for part in load_rows(whole, each, start + c * rows, rows, base):
            out[at : at + part.shape[0], c * LANES : (c + 1) * LANES] = part
            at += part.shape[0]
    return start + out.shape[1] // LANES * rows


def unpack_body(groups, *refs):
    core, across = lax.axis_index("core"), across_index()
    pieces, refs = refs[:2], refs[2:]
    count = sum(n for _, n in groups)
    outs, small, whole = refs[:count], refs[count:-1], refs[-1]
    sums, small = (small[-1], small[:-1]) if small else (None, small)
    for i, ref in enumerate(pieces):
        for k in range(ref.shape[0]):
            whole[i ^ core, k ^ across] = ref[k]
    base, first = 0, 0
    for each, n in groups:
        at = 0
        for out in outs[first : first + n]:
            at = unpack_columns(whole, each, base, at, out)
        base, first = base + each, first + n
    if sums is None:
        return
    at = 0
    for part in load_rows(whole, whole.shape[2] - base, 0, sums.shape[0], base):
        sums[at : at + part.shape[0]] = part
        at += part.shape[0]
    gain_a, pool_a, squeeze_a, table_a, mid_a, gain_b, pool_b, squeeze_b, table_b, mid_b = small
    for i, ref in enumerate((gain_a, mid_a, gain_b)):
        ref[...] = sums[i]
    for i in range(2):
        half = slice(i * LANES, (i + 1) * LANES)
        mid_b[half] = sums[3 + i]
        pool_a[i] = sums[8 + 4 * i : 12 + 4 * i, :]
        squeeze_a[i] = sums[16 + 4 * i : 20 + 4 * i, :]
        for j in range(3):
            pool_b[j, :, half] = sums[24 + 16 * i + 4 * j : 28 + 16 * i + 4 * j, :]
        for j in range(2):
            squeeze_b[j, :, half] = sums[56 + 8 * i + 4 * j : 60 + 8 * i + 4 * j, :]
    for ref, at in ((table_a, 72), (table_b, 80)):
        ref[...] = sums[at : at + ref.shape[0], : ref.shape[1]]


def leave_body(plan, each, small_each, *refs):
    refs = list(refs)
    pieces = plan.returned
    grads, refs = refs[:pieces], refs[pieces:]
    (dq, dm, doutput, n_ref, x_ref, gain, project, pools, squeeze,
     dgain_mid, dtable, dgain_b, dpool_b, dsqueeze_b, dmid_b, dtable_b) = refs[:16]
    refs = refs[16:]
    given = refs.pop(0) if not plan.local_squeeze else None
    grad_ref, keep, give, dpool_ref, dsqueeze_ref, sum_ref, stage, sems = refs
    tensor = plan.tensor
    width = x_ref.shape[1]
    n = n_ref[...]
    grad, memory = pair_grads(plan, grads)
    raw = mm(n, project[:, width:])
    parts = [dq[...].astype(BF16)]
    parts += unpool(plan, raw, grad, memory, pools, squeeze, dpool_ref, dsqueeze_ref, 0)
    at = 0
    grad_n = None
    for i, part in enumerate(parts):
        at = store_tail(stage, each, tensor, at, mm_tl(n, part))
        back = mm_tr(part, project[:, i * width : (i + 1) * width])
        grad_n = back if grad_n is None else grad_n + back
    store_tail(stage, each, tensor, at, doutput[...])
    normed, inverse = norm(x_ref[...].astype(F32))
    grad_x, dgain = norm_back(grad_n, wide_row(gain), normed, inverse)
    grad_ref[...] = (grad_x + dm[...]).astype(BF16)
    sum_ref[...] = jnp.zeros(sum_ref.shape, F32)
    squeeze_a = dsqueeze_ref if given is None else given
    sum_ref[0:1, :] = dgain
    sum_ref[1:2, :] = dgain_mid[...]
    sum_ref[2:3, :] = dgain_b[...]
    for i in range(2):
        half = slice(i * width, (i + 1) * width)
        sum_ref[3 + i : 4 + i, :] = dmid_b[:, half]
        sum_ref[8 + 4 * i : 12 + 4 * i, :] = dpool_ref[i]
        sum_ref[16 + 4 * i : 20 + 4 * i, :] = squeeze_a[i]
        for j in range(3):
            sum_ref[24 + 16 * i + 4 * j : 28 + 16 * i + 4 * j, :] = dpool_b[j, :, half]
        for j in range(2):
            sum_ref[56 + 8 * i + 4 * j : 60 + 8 * i + 4 * j, :] = dsqueeze_b[j, :, half]
    sum_ref[72:80, :128] = dtable[...]
    sum_ref[80:88, :128] = dtable_b[...]
    store_rows(stage, small_each, 0, 0, sum_ref[...], tensor * each)
    send_stage(stage, keep, give, sems)


def exit_body(order, grad_x, middle_b, *refs):
    outs, send_ref = refs[:-1], refs[-1]
    width = grad_x.shape[1]
    out = (middle_b[...] + sum_refs(outs)).astype(BF16)
    leaving = jnp.concatenate([grad_x[...], out[:, :width], out[:, width:]], axis=0)
    send_ref[...] = mm_tl(order[...], leaving).astype(BF16)


def exchange(values, axes, by):
    axes = (axes,) if isinstance(axes, str) else axes
    order = [axis for axis in EVERY if axis in axes]
    sizes = [lax.axis_size(axis) for axis in axes]
    into = [axes.index(axis) for axis in order]
    place = np.arange(np.prod(sizes)).reshape(sizes).transpose(into).reshape(-1)
    where = np.argsort(place)
    return lax.ppermute(values, tuple(order), [(i, int(where[p ^ by])) for i, p in enumerate(place)])


def to_core(values):
    return exchange(values, "core", 1)


def swap(values):
    cores, near = lax.axis_size("core"), lax.axis_size("near")
    assert cores == near
    pairs = [(i * near + j, j * near + i) for i in range(cores) for j in range(near)]
    return lax.ppermute(values, ("core", "near"), pairs)


def shift(values, by):
    chips, cores, far, near, tensor = (lax.axis_size(axis) for axis in EVERY)
    clips = chips * near * tensor

    def place(g, core, f):
        chip, n = divmod(g // tensor, near)
        return (((chip * cores + core) * far + f) * near + n) * tensor + g % tensor

    pairs = [
        (place(g, core, f), place(g + by, core, f))
        for g in range(clips)
        for core in range(cores)
        for f in range(far)
        if 0 <= g + by < clips
    ]
    return lax.ppermute(values, EVERY, pairs)


def relative_weights(plan, squeeze):
    s = lax.axis_index(FRAMES)
    order = jnp.arange(plan.all_frames)
    frame = ((s ^ (order // plan.frames)) * plan.frames + order % plan.frames) % 4
    pair = jnp.concatenate([squeeze[0], squeeze[1]], axis=-1)
    return pair[frame], frame


def share_pairs(plan, pair, squeeze):
    pairs = [pair[0]] + [exchange(pair[0], FRAMES, o) for o in range(1, plan.seq)]
    if plan.local_squeeze:
        memories = [shift(pair[1], by) for by in (1, 2)]
        return pairs + [exchange(each, FRAMES, o) if o else each for each in memories for o in range(plan.seq)]
    memory = squeeze_all(plan, pairs, squeeze)
    return pairs + [shift(memory, 1), shift(memory, 2)]


def by_frame(plan, pairs):
    together = jnp.concatenate([each.astype(F32) for each in pairs], axis=0)
    return together.reshape(plan.all_frames // 4, 4, plan.cells, -1)


def squeeze_all(plan, pairs, squeeze):
    weights = relative_weights(plan, squeeze)[0].reshape(plan.all_frames // 4, 4, 1, -1)
    total = jnp.sum(by_frame(plan, pairs) * weights, axis=1)
    return total.reshape(plan.memory, -1).astype(BF16)


def return_pairs(plan, grads, pairs, squeeze):
    own, others, memories = grads[0], grads[1 : plan.seq], grads[plan.seq :]
    memories = [shift(memories[0], -1), shift(memories[1], -2)]
    if plan.local_squeeze:
        received = [exchange(each, FRAMES, o + 1) for o, each in enumerate(others)]
        memories = [exchange(each, FRAMES, o) if o else each for each in memories for o in range(plan.seq)]
        return [own] + received + memories, None
    memory = memories[0].astype(F32) + memories[1].astype(F32)
    weights, frame = relative_weights(plan, squeeze)
    weights = weights.reshape(plan.all_frames // 4, 4, 1, -1)
    memory = memory.reshape(plan.all_frames // 4, 1, plan.cells, -1)
    both = by_frame(plan, [own, *others]) + memory * weights
    both = jnp.split(both.reshape(plan.own, -1), plan.seq, axis=0)
    sums = jnp.sum(by_frame(plan, pairs[: plan.seq]) * memory, axis=2).reshape(plan.all_frames, -1)
    onehot = (frame[None, :] == jnp.arange(4)[:, None]).astype(F32)
    sums = jnp.dot(onehot, sums, precision=HIGHEST)
    width = sums.shape[1] // 2
    received = [
        exchange(each.astype(BF16), FRAMES, o + 1) for o, each in enumerate(both[1:])
    ]
    return [both[0]] + received, jnp.stack([sums[:, :width], sums[:, width:]])


def add_all(parts):
    total = parts[0].astype(F32)
    for part in parts[1:]:
        total = total + part.astype(F32)
    return total.astype(BF16)


def sum_first(values):
    return add_all([values[k] for k in range(values.shape[0])])


def everyone(values, axis):
    return [values[0]] + [exchange(values[k], axis, k) for k in range(1, lax.axis_size(axis))]


def spread(values, axes):
    return lax.all_to_all(values, axes, 0, 0, tiled=True)


def after(value, *others):
    return lax.optimization_barrier((value, others))[0]


def sum_pair(keep, other):
    return (keep.astype(F32) + other.astype(F32)).astype(BF16)


def sum_cores(keep, give):
    return sum_pair(keep, to_core(give))


def scatter(values):
    count = lax.axis_size(ACROSS)
    if count > FEW:
        values = spread(values, ACROSS)
        return [values[k] for k in range(count)]
    parts = [lax.dynamic_index_in_dim(values, across_index() ^ k, keepdims=False) for k in range(count)]
    return [exchange(part, ACROSS, k) if k else part for k, part in enumerate(parts)]


def gather_across(values):
    return jnp.stack([exchange(values, ACROSS, k) if k else values for k in range(lax.axis_size(ACROSS))])


def gather_plane(values):
    values = gather_across(values)
    return [values, to_core(values)]


def halve(values, axis):
    for bit in range(log2(lax.axis_size(axis))):
        values = values.reshape(-1, 2, *values.shape[1:])
        values = sum_pair(values[:, 0], exchange(values[:, 1], axis, 1 << bit))
    return values[0]


def both_cores(values):
    return [values, to_core(values)]


def padded(rows, parts):
    return -(-rows // (16 * parts)) * 16


def local(
    clips_in, cotangent, resets, videos,
    attend_gain_a, project_a, pooling_a, squeeze_a, offsets_a, output_a, mixer_gain_a, expand_a, reduce_a,
    attend_gain_b, project_b, pooling_b, squeeze_b, offsets_b, output_b, shortcut_b, mixer_gain_b, expand_b, reduce_b,
):
    seq, tensor, plane = lax.axis_size(FRAMES), lax.axis_size("tensor"), lax.axis_size(PLANE)
    plan = Plan(seq, tensor, clips_in.shape)
    width, wide = clips_in.shape[-1], cotangent.shape[-1]
    heads_a, heads_b = offsets_a.shape[0], offsets_b.shape[0]
    core = lax.axis_index("core")
    tokens, pooled, keys, memory = plan.tokens, plan.pooled, plan.keys, plan.memory
    order = jnp.asarray(plan.arrange(), BF16)
    home = ("tensor",) + FRAMES
    leaving = jnp.concatenate(
        [clips_in.reshape(plan.group, -1, width), cotangent.reshape(plan.group, -1, width)], axis=1
    )
    arrived = spread(swap(leaving), home)
    half = jnp.where(core == 0, expand_a, reduce_a)
    quarter = half.reshape(2, -1, half.shape[1])[lax.axis_index("near")]
    quarter, arrived = lax.optimization_barrier((quarter, arrived))
    mine = [exchange(quarter, "tensor", k) for k in range(1, tensor)]
    arrived = arrived.reshape(-1, width)
    pair = lambda w: [((pooled, 2 * w), BF16)] + [((memory // seq, 2 * w), BF16)] * plan.local_squeeze
    x, cot, n_a, q_a, *pair_a = call(
        "enter",
        functools.partial(enter_body, plan),
        [((tokens, width), BF16), ((pooled, wide), BF16), ((tokens, width), BF16), ((tokens, width), BF16),
         *pair(width)],
        [arrived, order, attend_gain_a, project_a, pooling_a, squeeze_a],
    )
    pairs_a = share_pairs(plan, pair_a, squeeze_a)
    hidden = [((tensor, width, expand_a.shape[1]), BF16), ((tensor, reduce_a.shape[0], width), BF16)]
    mine, pairs_a[1] = lax.optimization_barrier((mine, pairs_a[1]))
    mine = jnp.concatenate(mine, axis=0)
    weights = [mine, exchange(mine, "near", 1)]
    weights, cots, pairs_a = lax.optimization_barrier((weights, cot, pairs_a))
    weights = weights + [to_core(each) for each in weights]
    cots = [cot] + [exchange(cots, "tensor", k) for k in range(1, tensor)]
    or_a, m_a, l_a, probs_a = call(
        "first",
        functools.partial(first_body, plan, heads_a),
        [((tokens, width), BF16), ((tokens, width), F32), ((tokens, width), BF16), ((heads_a * tokens, keys), BF16)],
        [x, q_a, *pairs_a, offsets_a, output_a, mixer_gain_a],
        [resets, videos],
        [((8, 128), F32)],
    )
    m_a, cots = lax.optimization_barrier((m_a, cots))
    y_a, n_b, q_b, base, *pair_b = call(
        "between",
        functools.partial(between_body, plan),
        [((tokens, width), F32), ((tokens, width), BF16), ((pooled, wide), BF16), ((pooled, wide), F32), *pair(wide)],
        [m_a, l_a, expand_a, reduce_a, *weights, attend_gain_b, project_b, pooling_b, squeeze_b, shortcut_b],
        (),
        hidden,
    )
    pairs_b = share_pairs(plan, pair_b, squeeze_b)
    or_b, m_b, l_b, probs_b = call(
        "second",
        functools.partial(second_body, plan, heads_b),
        [((pooled, wide), BF16), ((pooled, wide), F32), ((pooled, wide), BF16), ((heads_b * pooled, keys), BF16)],
        [q_b, *pairs_b, offsets_b, output_b, mixer_gain_b, base],
        [resets, videos],
        [((8, 128), F32)],
    )
    rows_b = [exchange(l_b, "tensor", k) if k else l_b for k in range(tensor)]
    hidden_rows = (expand_b.shape[1] // LANES) * wide + (wide // LANES) * reduce_b.shape[0]
    half_plane = plane // 2
    hidden_each = padded(hidden_rows, plane)
    units = ((tensor * pooled, expand_b.shape[1]), BF16)
    *shares, hidden_b, grad_pre_b = call(
        "hidden",
        functools.partial(hidden_body, tensor),
        [((pooled, wide), BF16)] * tensor + [units, units],
        [expand_b, reduce_b, *rows_b, *cots],
    )
    sums = everyone(shares, "tensor")
    bias = lambda: [((plan.frames, 8, keys), F32)]
    key_grads = lambda w: (
        [((pooled, 2 * w), F32)] + [((pooled, 2 * w), BF16)] * (seq - 1) + [((memory, 2 * w), BF16)] * 2
    )
    dm_b, dmid_b, doutput_b, dq_b, dtable_b, *back = call(
        "second_back",
        functools.partial(second_back_body, plan, heads_b),
        [((pooled, wide), F32), ((1, wide), F32), ((wide, wide), BF16), ((pooled, wide), F32),
         ((8, 128), F32), *key_grads(wide)],
        [*sums, cot, m_b, mixer_gain_b, or_b, output_b, q_b, probs_b, *pairs_b],
        [resets, videos],
        bias(),
    )
    pieces, dsqueeze_given = return_pairs(plan, back, pairs_b, squeeze_b)
    share = width // tensor
    cross_each = padded((3 + 1) * wide // LANES * share + wide // LANES * (wide // tensor), plane)
    dy_a, dpool_b, dsqueeze_b, dgain_b, keep, give = call(
        "cross",
        functools.partial(cross_body, plan, cross_each),
        [((tokens, width), F32), ((3, 4, wide), F32), ((2, 4, wide), F32), ((1, width), F32)],
        [*pieces, dq_b, dm_b, doutput_b, n_b, y_a, attend_gain_b, project_b, pooling_b, squeeze_b, shortcut_b],
        stage=(2, half_plane, tensor, cross_each, LANES),
    )
    cross = (keep, give)
    hidden_b = after(hidden_b, dgain_b)
    *out_shares, keep, give = call(
        "hidden_rest",
        functools.partial(hidden_rest_body, tensor, hidden_each),
        [((pooled, wide), BF16)] * tensor,
        [reduce_b, hidden_b, grad_pre_b, *rows_b, *cots],
        stage=(2, half_plane, 1, hidden_each, LANES),
    )
    early = (keep, give)
    early, cross = sum_cores(*early), sum_cores(*cross)
    early = [part.reshape(half_plane, -1, LANES) for part in (early, cross)]
    early, dy_a = lax.optimization_barrier((jnp.concatenate(early, axis=1), dy_a))
    early = spread(early, ACROSS)
    first_each = padded(2 * width, plane)
    dmid_a, dm_a, doutput_a, dq_a, dtable_a, *back, keep, give = call(
        "first_back",
        functools.partial(first_back_body, plan, first_each, heads_a),
        [((1, width), F32), ((tokens, width), F32), ((width, width), BF16), ((tokens, width), F32), ((8, 128), F32),
         *key_grads(width)],
        [dy_a, m_a, l_a, mixer_gain_a, or_a, output_a, q_a, probs_a, expand_a, reduce_a, *weights,
         *pairs_a],
        [resets, videos],
        hidden + bias(),
        stage=(2, half_plane, tensor, first_each, LANES),
    )
    if dsqueeze_given is not None:
        dsqueeze_b = dsqueeze_given
    pieces, dsqueeze_given = return_pairs(plan, back, pairs_a, squeeze_a)
    out_sums = everyone(out_shares, "tensor")
    early, dq_a, out_sums = lax.optimization_barrier((early, dq_a, out_sums))
    first = sum_cores(keep, give)
    tail_each, small_each = padded(4 * share, plane), padded(128, plane)
    grad_x, keep, give = call(
        "leave",
        functools.partial(leave_body, plan, tail_each, small_each),
        [((tokens, width), BF16)],
        [*pieces, dq_a, dm_a, doutput_a, n_a, x, attend_gain_a, project_a, pooling_a, squeeze_a, dmid_a, dtable_a,
         dgain_b, dpool_b, dsqueeze_b, dmid_b, dtable_b]
        + ([] if dsqueeze_given is None else [dsqueeze_given]),
        (),
        [((2, 4, width), F32), ((2, 4, width), F32), ((128, LANES), F32)],
        stage=(2, half_plane, 1, tensor * tail_each + small_each, LANES),
    )
    last = sum_cores(keep, give)
    last = jnp.concatenate([first.reshape(half_plane, -1, LANES), last[:, 0]], axis=1)
    leaving, = call("exit", exit_body, [(arrived.shape, BF16)], [order, after(grad_x, last), m_b, *out_sums])
    last = spread(last, ACROSS)
    early = sum_first(early)
    cross = halve(early[hidden_each:].reshape(tensor, cross_each, LANES), "tensor")
    early = gather_across(jnp.concatenate([early[:hidden_each], cross], axis=0))
    last, cross, leaving = lax.optimization_barrier((last, cross, leaving))
    last = sum_first(last)
    first_rows = tensor * first_each
    first = last[:first_rows].reshape(tensor, first_each, LANES)
    small = jnp.broadcast_to(last[None, first_rows + tensor * tail_each :], (tensor, small_each, LANES))
    last = last[first_rows : first_rows + tensor * tail_each].reshape(tensor, tail_each, LANES)
    last = jnp.concatenate([first, last, small], axis=1)
    leaving = after(leaving, last)
    last = gather_across(halve(last, "tensor"))
    returned = swap(spread(leaving.reshape(plan.group, -1, width), home))
    x_rows = plan.frames * plan.rows * plan.cols
    grad_input = returned[:, :x_rows].reshape(clips_in.shape).astype(F32)
    result = returned[:, x_rows:].reshape(cotangent.shape).astype(F32)
    early, last, grad_input, result = lax.optimization_barrier((early, last, grad_input, result))
    early, last = both_cores(early), both_cores(last)
    column = lambda rows, columns: ((rows, columns), F32)
    grad_expand_b, grad_reduce_b, grad_project_b, grad_shortcut_b, grad_output_b = call(
        "unpack_early",
        functools.partial(unpack_body, [(hidden_each, 2), (cross_each, 3)]),
        [
            (expand_b.shape, F32), (reduce_b.shape, F32),
            column(share, 3 * wide), column(share, wide), column(wide // tensor, wide),
        ],
        early,
        (),
        [((2, half_plane, hidden_each + cross_each, LANES), BF16)],
    )
    grad_expand_a, grad_reduce_a, grad_project_a, grad_output_a, *small = call(
        "unpack_last",
        functools.partial(unpack_body, [(first_each, 2), (tail_each, 2)]),
        [
            (expand_a.shape, F32), (reduce_a.shape, F32), column(share, 3 * width), column(share, width),
            ((width,), F32), (pooling_a.shape, F32), (squeeze_a.shape, F32), (offsets_a.shape, F32), ((width,), F32),
            ((width,), F32), (pooling_b.shape, F32), (squeeze_b.shape, F32), (offsets_b.shape, F32), ((wide,), F32),
        ],
        last,
        (),
        [((128, LANES), F32), ((2, half_plane, first_each + tail_each + small_each, LANES), BF16)],
    )
    return (
        result,
        grad_input,
        small[0],
        grad_project_a,
        small[1],
        small[2],
        small[3],
        grad_output_a,
        small[4],
        grad_expand_a,
        grad_reduce_a,
        small[5],
        grad_project_b,
        small[6],
        small[7],
        small[8],
        grad_output_b,
        grad_shortcut_b,
        small[9],
        grad_expand_b,
        grad_reduce_b,
    )


def solution(mesh):
    clip, seq, tensor = mesh.devices.shape
    split = Mesh(mesh.devices.reshape(clip // 2, 2, seq // 2, 2, tensor), EVERY)
    field = P(("chip", "core"), None, ("far", "near"), "tensor", None)
    up, down = P(None, "tensor"), P("tensor", None)
    block = (P(), P(), P(), P(), P(), P(), P(), up, down)
    block_b = (P(), P(), P(), P(), P(), P(), P(), P(), up, down)
    grads = (P(), down, P(), P(), P(), down, P(), up, down)
    grads_b = (P(), down, P(), P(), P(), down, down, P(), up, down)
    return jax.shard_map(
        local,
        mesh=split,
        in_specs=(field, field, P(), P()) + block + block_b,
        out_specs=(field, field) + grads + grads_b,
        check_vma=False,
    )
```

```python
import functools

import jax
import jax.numpy as jnp
import numpy as np
from jax import lax
from jax.experimental import pallas as pl
from jax.experimental.pallas import tpu as pltpu
from jax.sharding import Mesh
from jax.sharding import PartitionSpec as P

F32 = jnp.float32
BF16 = jnp.bfloat16
HIGHEST = lax.Precision.HIGHEST
EPSILON = 1e-06
MASKED = -1000000000.0
LOG_FOUR = 1.3862943611198906
SIZE = 96
LANES = 384
INTERPRET = False
PLANE = ("chip", "core", "far", "near")
EVERY = PLANE + ("tensor",)
ACROSS = ("chip", "far", "near")
FRAMES = ("far", "core")
FEW = 8
COSTS = {
    "enter": 3, "first": 4, "between": 6, "second": 7, "hidden": 4, "hidden_rest": 5, "second_back": 9, "cross": 8,
    "first_back": 10, "leave": 5, "exit": 2,
}


def wide_row(gain):
    return gain[...].reshape(1, gain.shape[0])


def log2(n):
    return n.bit_length() - 1


def mm(left, right):
    return jnp.dot(left, right, preferred_element_type=F32)


def mm_tl(left, right):
    return lax.dot_general(left, right, (((0,), (0,)), ((), ())), preferred_element_type=F32)


def mm_tr(left, right):
    return lax.dot_general(left, right, (((1,), (1,)), ((), ())), preferred_element_type=F32)


def norm(field):
    mean = jnp.mean(field, axis=-1, keepdims=True)
    centered = field - mean
    inverse = lax.rsqrt(jnp.mean(centered * centered, axis=-1, keepdims=True) + EPSILON)
    return centered * inverse, inverse


def norm_back(grad, gain, normed, inverse):
    scaled = grad * gain
    field = inverse * (
        scaled
        - jnp.mean(scaled, axis=-1, keepdims=True)
        - normed * jnp.mean(scaled * normed, axis=-1, keepdims=True)
    )
    return field, jnp.sum(grad * normed, axis=0, keepdims=True)


def gelu(values):
    return 0.5 * values * (1.0 + lax.erf(values * 0.7071067811865476))


def gelu_both(values):
    half = 0.5 * (1.0 + lax.erf(values * 0.7071067811865476))
    slope = half + values * jnp.exp(-0.5 * values * values) * 0.3989422804014327
    return values * half, slope


def blocks(values, count):
    rows = values.shape[0] // count
    return [values[i * rows : (i + 1) * rows] for i in range(count)]


def pool(values, weights):
    parts = blocks(values, 4)
    total = parts[0] * weights[0:1]
    for p in range(1, 4):
        total = total + parts[p] * weights[p : p + 1]
    return total


class Plan:
    def __init__(self, seq, tensor, shape):
        clips, frames, rows, cols, _ = shape
        self.seq, self.tensor = seq, tensor
        assert clips == tensor and frames % seq == 0 and rows % 2 == 0 and cols % 2 == 0
        self.all_frames = frames
        self.frames = frames // seq
        self.rows, self.cols = rows, cols
        self.group = seq * tensor
        self.cells = self.group * rows * cols // 4
        self.pooled = self.frames * self.cells
        self.tokens = 4 * self.pooled
        self.local_squeeze = self.frames % 4 == 0
        self.memory = frames // 4 * self.cells
        self.own = seq * self.pooled
        self.sources = seq + 2 * (seq if self.local_squeeze else 1)
        self.returned = seq + (2 * seq if self.local_squeeze else 0)
        self.keys = self.own + 2 * self.memory
        for n in (self.cells, self.pooled, self.memory, self.own, self.frames, seq):
            assert n == 1 << log2(n)

    def arrange(self):
        take = np.arange(self.tokens).reshape(
            self.group, self.frames, self.rows // 2, 2, self.cols // 2, 2
        )
        per = self.frames * self.rows * self.cols
        half = per // 4 * 2
        step = per + half
        x_rows = take // per * step + take % per
        x_rows = x_rows.transpose(3, 5, 1, 0, 2, 4).reshape(-1)
        cot = np.arange(self.pooled).reshape(self.group, self.frames, -1)
        low = cot // (per // 4) * step + per + cot % (per // 4) * 2
        low = low.transpose(1, 0, 2).reshape(-1)
        order = np.concatenate([x_rows, low, low + 1])
        return (order[:, None] == np.arange(self.group * step)[None, :]).astype(np.float32)


def clip_scalars(plan, resets, videos):
    s = lax.axis_index("far") * lax.axis_size("core") + lax.axis_index("core")
    chip = lax.axis_index("chip") * lax.axis_size("near") + lax.axis_index("near")
    g = chip * plan.tensor + lax.axis_index("tensor")
    before = jnp.maximum(g - 1, 0)
    earlier = jnp.maximum(g - 2, 0)
    first = (g >= 1) & (videos[g] == videos[before]) & (resets[g] == 0)
    second = first & (g >= 2) & (videos[before] == videos[earlier]) & (resets[before] == 0)
    return s, first.astype(jnp.int32), second.astype(jnp.int32)


def key_facts(plan, s, first, second):
    k = lax.broadcasted_iota(jnp.int32, (1, plan.keys), 1)
    own_time = ((s ^ (k >> log2(plan.pooled))) << log2(plan.frames)) + (
        (k & (plan.pooled - 1)) >> log2(plan.cells)
    )
    m = k - plan.own
    late = (m >> log2(plan.memory)) > 0
    g = (m & (plan.memory - 1)) >> log2(plan.cells)
    if plan.local_squeeze:
        each = log2(plan.frames // 4)
        squeezed = ((s ^ (g >> each)) << each) + (g & (plan.frames // 4 - 1))
    else:
        squeezed = (s >> log2(4 // plan.frames)) ^ g
    kind = jnp.where(m < 0, 0, jnp.where(late, 2, 1))
    time = jnp.where(m < 0, own_time, 4 * squeezed - plan.all_frames * kind)
    counts = jnp.where(kind == 0, 1, jnp.where(kind == 1, first, second))
    return time, counts


def offset_onehot(plan, s, time, frame):
    index = s * plan.frames + frame - time + plan.all_frames - 1
    rows = lax.broadcasted_iota(jnp.int32, (128, plan.keys), 0)
    return jnp.where(rows == index, 1.0, 0.0).astype(F32)


def head_mask(width, head):
    lane = lax.broadcasted_iota(jnp.int32, (1, width), 1)
    inside = (lane >= head * SIZE) & (lane < (head + 1) * SIZE)
    return jnp.where(inside, 1.0, 0.0).astype(F32)


def attend(plan, query, keys, values, offsets, heads, probs_ref, table_ref, scalars):
    s, first, second = scalars
    rows, width = query.shape
    places = rows // plan.pooled
    time, counts = key_facts(plan, s, first, second)
    biases = []
    table_ref[...] = jnp.zeros(table_ref.shape, F32)
    table_ref[:heads, : offsets.shape[1]] = offsets[...]
    table = table_ref[...]
    for f in range(plan.frames):
        onehot = offset_onehot(plan, s, time, f)
        bias = jnp.dot(table, onehot, precision=HIGHEST, preferred_element_type=F32)
        biases.append(jnp.where(counts > 0, bias, MASKED))
    total = query.astype(F32)
    for h in range(heads):
        mask = head_mask(width, h)
        scores = mm_tr(query * mask.astype(BF16), keys) * SIZE ** (-0.5)
        bias = jnp.concatenate(
            [jnp.broadcast_to(b[h : h + 1], (plan.cells, plan.keys)) for b in biases] * places, axis=0
        )
        scores = scores + bias
        scores = jnp.exp(scores - jnp.max(scores, axis=-1, keepdims=True))
        probs = scores * (1.0 / jnp.sum(scores, axis=-1, keepdims=True))
        probs = probs.astype(BF16)
        probs_ref[h * rows : (h + 1) * rows] = probs
        total = total + mm(probs, values) * mask
    return total


def attend_back(plan, grad, query, keys, values, probs_ref, heads, bias_ref, table_ref, scalars):
    s, first, second = scalars
    rows, width = query.shape
    places = rows // plan.pooled
    grad_r = grad.astype(BF16)
    grad_query = grad
    grad_keys = jnp.zeros((plan.keys, width), F32)
    grad_values = jnp.zeros((plan.keys, width), F32)
    bias_ref[...] = jnp.zeros(bias_ref.shape, F32)
    for h in range(heads):
        mask = head_mask(width, h)
        mask_r = mask.astype(BF16)
        grad_head = grad_r * mask_r
        query_head = query * mask_r
        probs_r = probs_ref[h * rows : (h + 1) * rows]
        probs = probs_r.astype(F32)
        grad_probs = mm_tr(grad_head, values)
        weighted = probs * grad_probs
        grad_scores = weighted - probs * jnp.sum(weighted, axis=-1, keepdims=True)
        for f in range(plan.frames):
            part = grad_scores[f * plan.cells : (f + 1) * plan.cells]
            for p in range(1, places):
                at = p * plan.pooled + f * plan.cells
                part = part + grad_scores[at : at + plan.cells]
            bias_ref[f, h : h + 1, :] = jnp.sum(part, axis=0, keepdims=True)
        grad_scores_r = grad_scores.astype(BF16)
        grad_query = grad_query + mm(grad_scores_r, keys) * (mask * SIZE ** (-0.5))
        grad_keys = grad_keys + mm_tl(grad_scores_r, query_head)
        grad_values = grad_values + mm_tl(probs_r, grad_head)
    time, _ = key_facts(plan, s, first, second)
    table = jnp.zeros((8, 128), F32)
    for f in range(plan.frames):
        onehot = offset_onehot(plan, s, time, f)
        table = table + lax.dot_general(
            bias_ref[f], onehot, (((1,), (1,)), ((), ())), precision=HIGHEST, preferred_element_type=F32
        )
    table_ref[...] = table
    return grad_query, grad_keys * SIZE ** (-0.5), grad_values


def load_pairs(refs, width):
    pairs = jnp.concatenate([ref[...] for ref in refs], axis=0)
    return pairs[:, :width], pairs[:, width:]


def pool_pair(plan, raw, pool_ref, squeeze_ref, pair_ref, memory_ref=None):
    width = raw.shape[1] // 2
    for i in range(2):
        pooled = pool(raw[:, i * width : (i + 1) * width], pool_ref[pool_ref.shape[0] - 2 + i])
        pair_ref[:, i * width : (i + 1) * width] = pooled.astype(BF16)
        if memory_ref is not None:
            weights = squeeze_ref[i]
            for g in range(plan.frames // 4):
                total = None
                for k in range(4):
                    at = (4 * g + k) * plan.cells
                    part = pooled[at : at + plan.cells] * weights[k : k + 1]
                    total = part if total is None else total + part
                at = g * plan.cells
                memory_ref[at : at + plan.cells, i * width : (i + 1) * width] = total.astype(BF16)


def store_rows(stage, each, z, start, values, base=0):
    core = lax.axis_index("core")
    half, at = stage.shape[1], 0
    while at < values.shape[0]:
        who, off = divmod(start + at, each)
        n = min(each - off, values.shape[0] - at)
        part = values[at : at + n].astype(BF16)
        rows = pl.ds(base + off if isinstance(base, int) else pl.multiple_of(base + off, 16), n)
        stage[(who // half) ^ core, who % half, z, rows, :] = part
        at += n


def store_columns(stage, each, tensor, start, values):
    rows = values.shape[0] // tensor
    t = lax.axis_index("tensor")
    for z in range(tensor):
        for c in range(values.shape[1] // LANES):
            part = values[z * rows : (z + 1) * rows, c * LANES : (c + 1) * LANES]
            store_rows(stage, each, z ^ t, start + c * rows, part)
    return start + values.shape[1] // LANES * rows


def send_stage(stage, keep, give, sems):
    copies = [pltpu.make_async_copy(stage.at[i], (keep, give)[i], sems.at[i]) for i in range(2)]
    for copy in copies:
        copy.start()
    for copy in copies:
        copy.wait()


def smooth_max(raw):
    parts = blocks(raw, 4)
    highest = jnp.maximum(jnp.maximum(parts[0], parts[1]), jnp.maximum(parts[2], parts[3]))
    total = jnp.exp(parts[0] - highest)
    for p in range(1, 4):
        total = total + jnp.exp(parts[p] - highest)
    return highest + jnp.log(total) - LOG_FOUR


def smooth_max_back(raw, grad):
    parts = blocks(raw, 4)
    highest = jnp.maximum(jnp.maximum(parts[0], parts[1]), jnp.maximum(parts[2], parts[3]))
    parts = [jnp.exp(part - highest) for part in parts]
    total = parts[0] + parts[1] + parts[2] + parts[3]
    scaled = grad / total
    return jnp.concatenate([part * scaled for part in parts], axis=0)


def call(name, body, outs, vmem, smem=(), scratch=(), stage=None):
    moved = COSTS.get(name, 4) * 3_000_000
    scratch = [pltpu.VMEM(shape, dtype) for shape, dtype in scratch]
    spaces = [pltpu.VMEM] * len(outs)
    if stage is not None:
        outs = outs + [(stage[1:], BF16)] * 2
        spaces += [pl.ANY] * 2
        scratch += [pltpu.VMEM(stage, BF16), pltpu.SemaphoreType.DMA((2,))]
    return pl.pallas_call(
        body,
        out_shape=[jax.ShapeDtypeStruct(shape, dtype) for shape, dtype in outs],
        in_specs=[pl.BlockSpec(memory_space=pltpu.SMEM)] * len(smem)
        + [pl.BlockSpec(memory_space=pltpu.VMEM)] * len(vmem),
        out_specs=[pl.BlockSpec(memory_space=space) for space in spaces],
        scratch_shapes=scratch,
        name=name,
        interpret=INTERPRET,
        cost_estimate=pl.CostEstimate(flops=0, bytes_accessed=moved, transcendentals=0),
        compiler_params=pltpu.CompilerParams(vmem_limit_bytes=56 << 20),
    )(*smem, *vmem)


def enter_body(plan, arrived, order, gain, project, pools, squeeze, x_ref, cot_ref, n_ref, q_ref, *pair):
    rows = mm(order[...], arrived[...])
    x = rows[: plan.tokens]
    x_ref[...] = x.astype(BF16)
    width = cot_ref.shape[1] // 2
    cot_ref[:, :width] = rows[plan.tokens : plan.tokens + plan.pooled].astype(BF16)
    cot_ref[:, width:] = rows[plan.tokens + plan.pooled :].astype(BF16)
    n = (norm(x)[0] * wide_row(gain)).astype(BF16)
    n_ref[...] = n
    raw = mm(n, project[...])
    q_ref[...] = raw[:, : x.shape[1]].astype(BF16)
    pool_pair(plan, raw[:, x.shape[1] :], pools, squeeze, *pair)


def pick_hidden(tensor, expand, reduce, weights, up_ref, down_ref):
    up_ref[0] = expand[...]
    down_ref[0] = reduce[...]
    core, near = lax.axis_index("core"), lax.axis_index("near")
    rows = weights[0].shape[0] // (tensor - 1)

    def put(first, second):
        for i, piece in enumerate(weights):
            at = pl.multiple_of(((i % 2) ^ near) * rows, 16)
            for k in range(1, tensor):
                part = piece[(k - 1) * rows : k * rows, :]
                (second if i // 2 else first)[k, pl.ds(at, rows), :] = part

    @pl.when(core == 0)
    def _():
        put(up_ref, down_ref)

    @pl.when(core != 0)
    def _():
        put(down_ref, up_ref)


def first_body(plan, heads, resets, videos, *refs):
    x, query = refs[:2]
    pairs, refs = refs[2 : 2 + plan.sources], refs[2 + plan.sources :]
    table, output, gain, or_ref, m_ref, l_ref, probs_ref, table_ref = refs
    scalars = clip_scalars(plan, resets, videos)
    keys, values = load_pairs(pairs, x.shape[1])
    mixed_r = attend(plan, query[...], keys, values, table, heads, probs_ref, table_ref, scalars).astype(BF16)
    or_ref[...] = mixed_r
    middle = x[...].astype(F32) + mm(mixed_r, output[...])
    m_ref[...] = middle
    l_ref[...] = (norm(middle)[0] * wide_row(gain)).astype(BF16)


def between_body(plan, m_ref, l_ref, expand, reduce, *refs):
    weights, refs = refs[:4], refs[4:]
    gain_b, project_b, pool_b, squeeze_b, shortcut_b, y_ref, nb_ref, qb_ref, base_ref = refs[:9]
    pair, up_ref, down_ref = refs[9:-2], refs[-2], refs[-1]
    pick_hidden(plan.tensor, expand, reduce, weights, up_ref, down_ref)
    l = l_ref[...]
    y = m_ref[...]
    for k in range(plan.tensor):
        hidden = gelu(mm(l, up_ref[k])).astype(BF16)
        y = y + mm(hidden, down_ref[k])
    y_ref[...] = y
    n = (norm(y)[0] * wide_row(gain_b)).astype(BF16)
    nb_ref[...] = n
    wide = base_ref.shape[1]
    raw = mm(n, project_b[...])
    qb_ref[...] = pool(raw[:, :wide], pool_b[0]).astype(BF16)
    pool_pair(plan, raw[:, wide:], pool_b, squeeze_b, *pair)
    base_ref[...] = smooth_max(mm(n, shortcut_b[...]))


def second_body(plan, heads, resets, videos, *refs):
    query, pairs, refs = refs[0], refs[1 : 1 + plan.sources], refs[1 + plan.sources :]
    table, output, gain, base, or_ref, m_ref, l_ref, probs_ref, table_ref = refs
    width = query.shape[1]
    scalars = clip_scalars(plan, resets, videos)
    keys, values = load_pairs(pairs, width)
    mixed_r = attend(plan, query[...], keys, values, table, heads, probs_ref, table_ref, scalars).astype(BF16)
    or_ref[...] = mixed_r
    middle = base[...] + mm(mixed_r, output[...])
    m_ref[...] = middle
    l_ref[...] = (norm(middle)[0] * wide_row(gain)).astype(BF16)


def hidden_body(tensor, up, down, *refs):
    rows, grads, refs = refs[:tensor], refs[tensor : 2 * tensor], refs[2 * tensor :]
    sends, (hidden_ref, grad_pre_ref) = refs[:tensor], refs[tensor:]
    l = jnp.concatenate([ref[...] for ref in rows], axis=0)
    grad = jnp.concatenate([ref[...] for ref in grads], axis=0)
    gate, slope = gelu_both(mm(l, up[...]))
    hidden_ref[...] = gate.astype(BF16)
    grad_pre = (slope * mm_tr(grad, down[...])).astype(BF16)
    grad_pre_ref[...] = grad_pre
    for ref, part in zip(sends, blocks(mm_tr(grad_pre, up[...]), tensor)):
        ref[...] = part.astype(BF16)


def hidden_rest_body(tensor, each, down, hidden_ref, grad_pre_ref, *refs):
    rows, grads, refs = refs[:tensor], refs[tensor : 2 * tensor], refs[2 * tensor :]
    sends, (keep, give, stage, sems) = refs[:tensor], refs[tensor:]
    hidden, grad_pre = hidden_ref[...], grad_pre_ref[...]
    l = jnp.concatenate([ref[...] for ref in rows], axis=0)
    grad = jnp.concatenate([ref[...] for ref in grads], axis=0)
    at = 0
    for whole in (mm_tl(l, grad_pre), mm_tl(hidden, grad)):
        for c in range(whole.shape[1] // LANES):
            part = whole[:, c * LANES : (c + 1) * LANES]
            store_rows(stage, each, 0, at, part)
            at += part.shape[0]
    for ref, part in zip(sends, blocks(mm(hidden, down[...]), tensor)):
        ref[...] = part.astype(BF16)
    send_stage(stage, keep, give, sems)


def sum_refs(refs):
    total = refs[0][...].astype(F32)
    for ref in refs[1:]:
        total = total + ref[...].astype(F32)
    return total


def second_back_body(plan, heads, resets, videos, *refs):
    refs = list(refs)
    sums, refs = refs[: plan.tensor], refs[plan.tensor :]
    cot, middle, gain, mixed, output, query, probs = refs[:7]
    pairs, refs = refs[7 : 7 + plan.sources], refs[7 + plan.sources :]
    dm_ref, dgain_ref = refs[:2]
    refs = refs[2:]
    normed, inverse = norm(middle[...])
    grad, dgain = norm_back(sum_refs(sums), wide_row(gain), normed, inverse)
    dgain_ref[...] = dgain
    grad = cot[...].astype(F32) + grad
    dm_ref[...] = grad
    store_back(plan, heads, resets, videos, grad, mixed, output, query, probs, pairs, *refs)


def store_back(plan, heads, resets, videos, grad, mixed, output, query, probs, pairs, doutput_ref, dq_ref, dtable_ref,
               *refs):
    width = query.shape[1]
    scalars = clip_scalars(plan, resets, videos)
    grad_r = grad.astype(BF16)
    doutput_ref[...] = mm_tl(mixed[...], grad_r).astype(BF16)
    grads, bias_ref = refs[:-1], refs[-1]
    keys, values = load_pairs(pairs, width)
    dq, dk, dv = attend_back(
        plan, mm_tr(grad_r, output[...]), query[...], keys, values, probs, heads, bias_ref, dtable_ref, scalars
    )
    dq_ref[...] = dq
    for i, part in enumerate((dk, dv)):
        lanes = slice(i * width, (i + 1) * width)
        at = 0
        for ref in grads:
            ref[:, lanes] = part[at : at + ref.shape[0]].astype(ref.dtype)
            at += ref.shape[0]


def pair_grads(plan, refs):
    own, received = refs[0], refs[1 : plan.seq]
    grad = own[...]
    for ref in received:
        grad = grad + ref[...].astype(F32)
    if not plan.local_squeeze:
        return grad, None
    memory = None
    size = plan.memory // plan.seq
    for i, ref in enumerate(refs[plan.seq :]):
        o = i % plan.seq
        part = ref[o * size : (o + 1) * size, :].astype(F32)
        memory = part if memory is None else memory + part
    return grad, memory


def unpool(plan, raw, grad, memory, pool_ref, squeeze_ref, dpool_ref, dsqueeze_ref, first):
    width = raw.shape[1] // 2
    result = []
    for i in range(2):
        weights = pool_ref[first + i]
        lanes = slice(i * width, (i + 1) * width)
        part = grad[:, lanes]
        source = raw[:, lanes]
        if plan.local_squeeze:
            pooled = pool(source, weights)
            ws = squeeze_ref[i]
            pieces = []
            sums = [None] * 4
            for g in range(plan.frames // 4):
                dm = memory[g * plan.cells : (g + 1) * plan.cells, lanes]
                for k in range(4):
                    at = (4 * g + k) * plan.cells
                    pieces.append(part[at : at + plan.cells] + dm * ws[k : k + 1])
                    total = jnp.sum(dm * pooled[at : at + plan.cells], axis=0, keepdims=True)
                    sums[k] = total if sums[k] is None else sums[k] + total
            part = jnp.concatenate(pieces, axis=0)
            for k in range(4):
                dsqueeze_ref[i, k : k + 1, :] = sums[k]
        result.append(unpool_one(source, part, weights, dpool_ref, first + i))
    return result


def unpool_one(source, part, weights, dpool_ref, place):
    pieces = []
    for p, piece in enumerate(blocks(source, 4)):
        dpool_ref[place, p : p + 1, :] = jnp.sum(part * piece, axis=0, keepdims=True)
        pieces.append((part * weights[p : p + 1]).astype(BF16))
    return jnp.concatenate(pieces, axis=0)


def cross_body(plan, each, *refs):
    pieces = plan.returned
    grads = refs[:pieces]
    (dq, dm, doutput_b, n_ref, y_ref, gain_b, project_b, pool_b, squeeze_b, shortcut_b,
     dy_ref, dpool_ref, dsqueeze_ref, dgain_ref, keep, give, stage, sems) = refs[pieces:]
    tensor = plan.tensor
    wide = dm.shape[1]
    n = n_ref[...]
    grad, memory = pair_grads(plan, grads)
    raw = mm(n, project_b[...])
    parts = [unpool_one(raw[:, :wide], dq[...], pool_b[0], dpool_ref, 0)]
    parts += unpool(plan, raw[:, wide:], grad, memory, pool_b, squeeze_b, dpool_ref, dsqueeze_ref, 1)
    at = 0
    grad_n = None
    for i, part in enumerate(parts):
        at = store_columns(stage, each, tensor, at, mm_tl(n, part))
        back = mm_tr(part, project_b[:, i * wide : (i + 1) * wide])
        grad_n = back if grad_n is None else grad_n + back
    grad_z = smooth_max_back(mm(n, shortcut_b[...]), dm[...]).astype(BF16)
    at = store_columns(stage, each, tensor, at, mm_tl(n, grad_z))
    store_columns(stage, each, tensor, at, doutput_b[...])
    grad_n = grad_n + mm_tr(grad_z, shortcut_b[...])
    normed, inverse = norm(y_ref[...])
    grad_y, dgain = norm_back(grad_n, wide_row(gain_b), normed, inverse)
    dgain_ref[...] = dgain
    dy_ref[...] = grad_y
    send_stage(stage, keep, give, sems)


def first_back_body(plan, each, heads, resets, videos, *refs):
    refs = list(refs)

    def take(n):
        taken = refs[:n]
        del refs[:n]
        return taken

    dy_ref, m_ref, l_ref, gain, mixed, output, query, probs, expand, reduce = take(10)
    weights = take(4)
    pairs = take(plan.sources)
    dgain_ref, dm_out = take(2)
    refs, (keep, give, up_ref, down_ref, bias_ref, stage, sems) = refs[:-7], refs[-7:]
    tensor = plan.tensor
    pick_hidden(tensor, expand, reduce, weights, up_ref, down_ref)
    grad_y = dy_ref[...]
    grad_r = grad_y.astype(BF16)
    l = l_ref[...]
    grad_l = None
    for k in range(tensor):
        gate, slope = gelu_both(mm(l, up_ref[k]))
        hidden = gate.astype(BF16)
        grad_pre = (slope * mm_tr(grad_r, down_ref[k])).astype(BF16)
        store_rows(stage, each, k, 0, mm_tl(l, grad_pre))
        store_rows(stage, each, k, l.shape[1], mm_tl(hidden, grad_r))
        back = mm_tr(grad_pre, up_ref[k])
        grad_l = back if grad_l is None else grad_l + back
    normed, inverse = norm(m_ref[...])
    grad, dgain = norm_back(grad_l, wide_row(gain), normed, inverse)
    dgain_ref[...] = dgain
    grad = grad_y + grad
    dm_out[...] = grad
    store_back(plan, heads, resets, videos, grad, mixed, output, query, probs, pairs, *refs, bias_ref)
    send_stage(stage, keep, give, sems)


def store_tail(stage, each, tensor, start, values):
    rows = values.shape[0] // tensor
    t = lax.axis_index("tensor")
    for z in range(tensor):
        for c in range(values.shape[1] // LANES):
            part = values[z * rows : (z + 1) * rows, c * LANES : (c + 1) * LANES]
            store_rows(stage, each, 0, start + c * rows, part, (z ^ t) * each)
    return start + values.shape[1] // LANES * rows


def load_rows(whole, each, start, count, base=0):
    half = whole.shape[1]
    parts, at = [], 0
    while at < count:
        who, off = divmod(start + at, each)
        n = min(each - off, count - at)
        parts.append(whole[who // half, who % half, base + off : base + off + n, :].astype(F32))
        at += n
    return parts


def across_index():
    index = 0
    for axis in ACROSS:
        index = index * lax.axis_size(axis) + lax.axis_index(axis)
    return index


def unpack_columns(whole, each, base, start, out):
    rows = out.shape[0]
    for c in range(out.shape[1] // LANES):
        at = 0
        for part in load_rows(whole, each, start + c * rows, rows, base):
            out[at : at + part.shape[0], c * LANES : (c + 1) * LANES] = part
            at += part.shape[0]
    return start + out.shape[1] // LANES * rows


def unpack_body(groups, *refs):
    core, across = lax.axis_index("core"), across_index()
    pieces, refs = refs[:2], refs[2:]
    count = sum(n for _, n in groups)
    outs, small, whole = refs[:count], refs[count:-1], refs[-1]
    sums, small = (small[-1], small[:-1]) if small else (None, small)
    for i, ref in enumerate(pieces):
        for k in range(ref.shape[0]):
            whole[i ^ core, k ^ across] = ref[k]
    base, first = 0, 0
    for each, n in groups:
        at = 0
        for out in outs[first : first + n]:
            at = unpack_columns(whole, each, base, at, out)
        base, first = base + each, first + n
    if sums is None:
        return
    at = 0
    for part in load_rows(whole, whole.shape[2] - base, 0, sums.shape[0], base):
        sums[at : at + part.shape[0]] = part
        at += part.shape[0]
    gain_a, pool_a, squeeze_a, table_a, mid_a, gain_b, pool_b, squeeze_b, table_b, mid_b = small
    for i, ref in enumerate((gain_a, mid_a, gain_b)):
        ref[...] = sums[i]
    for i in range(2):
        half = slice(i * LANES, (i + 1) * LANES)
        mid_b[half] = sums[3 + i]
        pool_a[i] = sums[8 + 4 * i : 12 + 4 * i, :]
        squeeze_a[i] = sums[16 + 4 * i : 20 + 4 * i, :]
        for j in range(3):
            pool_b[j, :, half] = sums[24 + 16 * i + 4 * j : 28 + 16 * i + 4 * j, :]
        for j in range(2):
            squeeze_b[j, :, half] = sums[56 + 8 * i + 4 * j : 60 + 8 * i + 4 * j, :]
    for ref, at in ((table_a, 72), (table_b, 80)):
        ref[...] = sums[at : at + ref.shape[0], : ref.shape[1]]


def leave_body(plan, each, small_each, *refs):
    refs = list(refs)
    pieces = plan.returned
    grads, refs = refs[:pieces], refs[pieces:]
    (dq, dm, doutput, n_ref, x_ref, gain, project, pools, squeeze,
     dgain_mid, dtable, dgain_b, dpool_b, dsqueeze_b, dmid_b, dtable_b) = refs[:16]
    refs = refs[16:]
    given = refs.pop(0) if not plan.local_squeeze else None
    grad_ref, keep, give, dpool_ref, dsqueeze_ref, sum_ref, stage, sems = refs
    tensor = plan.tensor
    width = x_ref.shape[1]
    n = n_ref[...]
    grad, memory = pair_grads(plan, grads)
    raw = mm(n, project[:, width:])
    parts = [dq[...].astype(BF16)]
    parts += unpool(plan, raw, grad, memory, pools, squeeze, dpool_ref, dsqueeze_ref, 0)
    at = 0
    grad_n = None
    for i, part in enumerate(parts):
        at = store_tail(stage, each, tensor, at, mm_tl(n, part))
        back = mm_tr(part, project[:, i * width : (i + 1) * width])
        grad_n = back if grad_n is None else grad_n + back
    store_tail(stage, each, tensor, at, doutput[...])
    normed, inverse = norm(x_ref[...].astype(F32))
    grad_x, dgain = norm_back(grad_n, wide_row(gain), normed, inverse)
    grad_ref[...] = (grad_x + dm[...]).astype(BF16)
    sum_ref[...] = jnp.zeros(sum_ref.shape, F32)
    squeeze_a = dsqueeze_ref if given is None else given
    sum_ref[0:1, :] = dgain
    sum_ref[1:2, :] = dgain_mid[...]
    sum_ref[2:3, :] = dgain_b[...]
    for i in range(2):
        half = slice(i * width, (i + 1) * width)
        sum_ref[3 + i : 4 + i, :] = dmid_b[:, half]
        sum_ref[8 + 4 * i : 12 + 4 * i, :] = dpool_ref[i]
        sum_ref[16 + 4 * i : 20 + 4 * i, :] = squeeze_a[i]
        for j in range(3):
            sum_ref[24 + 16 * i + 4 * j : 28 + 16 * i + 4 * j, :] = dpool_b[j, :, half]
        for j in range(2):
            sum_ref[56 + 8 * i + 4 * j : 60 + 8 * i + 4 * j, :] = dsqueeze_b[j, :, half]
    sum_ref[72:80, :128] = dtable[...]
    sum_ref[80:88, :128] = dtable_b[...]
    store_rows(stage, small_each, 0, 0, sum_ref[...], tensor * each)
    send_stage(stage, keep, give, sems)


def exit_body(order, grad_x, middle_b, *refs):
    outs, send_ref = refs[:-1], refs[-1]
    width = grad_x.shape[1]
    out = (middle_b[...] + sum_refs(outs)).astype(BF16)
    leaving = jnp.concatenate([grad_x[...], out[:, :width], out[:, width:]], axis=0)
    send_ref[...] = mm_tl(order[...], leaving).astype(BF16)


def exchange(values, axes, by):
    axes = (axes,) if isinstance(axes, str) else axes
    order = [axis for axis in EVERY if axis in axes]
    sizes = [lax.axis_size(axis) for axis in axes]
    into = [axes.index(axis) for axis in order]
    place = np.arange(np.prod(sizes)).reshape(sizes).transpose(into).reshape(-1)
    where = np.argsort(place)
    return lax.ppermute(values, tuple(order), [(i, int(where[p ^ by])) for i, p in enumerate(place)])


def to_core(values):
    return exchange(values, "core", 1)


def swap(values):
    cores, near = lax.axis_size("core"), lax.axis_size("near")
    assert cores == near
    pairs = [(i * near + j, j * near + i) for i in range(cores) for j in range(near)]
    return lax.ppermute(values, ("core", "near"), pairs)


def shift(values, by):
    chips, cores, far, near, tensor = (lax.axis_size(axis) for axis in EVERY)
    clips = chips * near * tensor

    def place(g, core, f):
        chip, n = divmod(g // tensor, near)
        return (((chip * cores + core) * far + f) * near + n) * tensor + g % tensor

    pairs = [
        (place(g, core, f), place(g + by, core, f))
        for g in range(clips)
        for core in range(cores)
        for f in range(far)
        if 0 <= g + by < clips
    ]
    return lax.ppermute(values, EVERY, pairs)


def relative_weights(plan, squeeze):
    s = lax.axis_index(FRAMES)
    order = jnp.arange(plan.all_frames)
    frame = ((s ^ (order // plan.frames)) * plan.frames + order % plan.frames) % 4
    pair = jnp.concatenate([squeeze[0], squeeze[1]], axis=-1)
    return pair[frame], frame


def share_pairs(plan, pair, squeeze):
    pairs = [pair[0]] + [exchange(pair[0], FRAMES, o) for o in range(1, plan.seq)]
    if plan.local_squeeze:
        memories = [shift(pair[1], by) for by in (1, 2)]
        return pairs + [exchange(each, FRAMES, o) if o else each for each in memories for o in range(plan.seq)]
    memory = squeeze_all(plan, pairs, squeeze)
    return pairs + [shift(memory, 1), shift(memory, 2)]


def by_frame(plan, pairs):
    together = jnp.concatenate([each.astype(F32) for each in pairs], axis=0)
    return together.reshape(plan.all_frames // 4, 4, plan.cells, -1)


def squeeze_all(plan, pairs, squeeze):
    weights = relative_weights(plan, squeeze)[0].reshape(plan.all_frames // 4, 4, 1, -1)
    total = jnp.sum(by_frame(plan, pairs) * weights, axis=1)
    return total.reshape(plan.memory, -1).astype(BF16)


def return_pairs(plan, grads, pairs, squeeze):
    own, others, memories = grads[0], grads[1 : plan.seq], grads[plan.seq :]
    memories = [shift(memories[0], -1), shift(memories[1], -2)]
    if plan.local_squeeze:
        received = [exchange(each, FRAMES, o + 1) for o, each in enumerate(others)]
        memories = [exchange(each, FRAMES, o) if o else each for each in memories for o in range(plan.seq)]
        return [own] + received + memories, None
    memory = memories[0].astype(F32) + memories[1].astype(F32)
    weights, frame = relative_weights(plan, squeeze)
    weights = weights.reshape(plan.all_frames // 4, 4, 1, -1)
    memory = memory.reshape(plan.all_frames // 4, 1, plan.cells, -1)
    both = by_frame(plan, [own, *others]) + memory * weights
    both = jnp.split(both.reshape(plan.own, -1), plan.seq, axis=0)
    sums = jnp.sum(by_frame(plan, pairs[: plan.seq]) * memory, axis=2).reshape(plan.all_frames, -1)
    onehot = (frame[None, :] == jnp.arange(4)[:, None]).astype(F32)
    sums = jnp.dot(onehot, sums, precision=HIGHEST)
    width = sums.shape[1] // 2
    received = [
        exchange(each.astype(BF16), FRAMES, o + 1) for o, each in enumerate(both[1:])
    ]
    return [both[0]] + received, jnp.stack([sums[:, :width], sums[:, width:]])


def add_all(parts):
    total = parts[0].astype(F32)
    for part in parts[1:]:
        total = total + part.astype(F32)
    return total.astype(BF16)


def sum_first(values):
    return add_all([values[k] for k in range(values.shape[0])])


def everyone(values, axis):
    return [values[0]] + [exchange(values[k], axis, k) for k in range(1, lax.axis_size(axis))]


def spread(values, axes):
    return lax.all_to_all(values, axes, 0, 0, tiled=True)


def after(value, *others):
    return lax.optimization_barrier((value, others))[0]


def sum_pair(keep, other):
    return (keep.astype(F32) + other.astype(F32)).astype(BF16)


def sum_cores(keep, give):
    return sum_pair(keep, to_core(give))


def scatter(values):
    count = lax.axis_size(ACROSS)
    if count > FEW:
        values = spread(values, ACROSS)
        return [values[k] for k in range(count)]
    parts = [lax.dynamic_index_in_dim(values, across_index() ^ k, keepdims=False) for k in range(count)]
    return [exchange(part, ACROSS, k) if k else part for k, part in enumerate(parts)]


def gather_across(values):
    return jnp.stack([exchange(values, ACROSS, k) if k else values for k in range(lax.axis_size(ACROSS))])


def gather_plane(values):
    values = gather_across(values)
    return [values, to_core(values)]


def halve(values, axis):
    for bit in range(log2(lax.axis_size(axis))):
        values = values.reshape(-1, 2, *values.shape[1:])
        values = sum_pair(values[:, 0], exchange(values[:, 1], axis, 1 << bit))
    return values[0]


def both_cores(values):
    return [values, to_core(values)]


def padded(rows, parts):
    return -(-rows // (16 * parts)) * 16


def local(
    clips_in, cotangent, resets, videos,
    attend_gain_a, project_a, pooling_a, squeeze_a, offsets_a, output_a, mixer_gain_a, expand_a, reduce_a,
    attend_gain_b, project_b, pooling_b, squeeze_b, offsets_b, output_b, shortcut_b, mixer_gain_b, expand_b, reduce_b,
):
    seq, tensor, plane = lax.axis_size(FRAMES), lax.axis_size("tensor"), lax.axis_size(PLANE)
    plan = Plan(seq, tensor, clips_in.shape)
    width, wide = clips_in.shape[-1], cotangent.shape[-1]
    heads_a, heads_b = offsets_a.shape[0], offsets_b.shape[0]
    core = lax.axis_index("core")
    tokens, pooled, keys, memory = plan.tokens, plan.pooled, plan.keys, plan.memory
    order = jnp.asarray(plan.arrange(), BF16)
    home = ("tensor",) + FRAMES
    leaving = jnp.concatenate(
        [clips_in.reshape(plan.group, -1, width), cotangent.reshape(plan.group, -1, width)], axis=1
    )
    arrived = spread(swap(leaving), home)
    half = jnp.where(core == 0, expand_a, reduce_a)
    quarter = half.reshape(2, -1, half.shape[1])[lax.axis_index("near")]
    quarter, arrived = lax.optimization_barrier((quarter, arrived))
    mine = [exchange(quarter, "tensor", k) for k in range(1, tensor)]
    arrived = arrived.reshape(-1, width)
    pair = lambda w: [((pooled, 2 * w), BF16)] + [((memory // seq, 2 * w), BF16)] * plan.local_squeeze
    x, cot, n_a, q_a, *pair_a = call(
        "enter",
        functools.partial(enter_body, plan),
        [((tokens, width), BF16), ((pooled, wide), BF16), ((tokens, width), BF16), ((tokens, width), BF16),
         *pair(width)],
        [arrived, order, attend_gain_a, project_a, pooling_a, squeeze_a],
    )
    pairs_a = share_pairs(plan, pair_a, squeeze_a)
    hidden = [((tensor, width, expand_a.shape[1]), BF16), ((tensor, reduce_a.shape[0], width), BF16)]
    mine, pairs_a[1] = lax.optimization_barrier((mine, pairs_a[1]))
    mine = jnp.concatenate(mine, axis=0)
    weights = [mine, exchange(mine, "near", 1)]
    weights, cots, pairs_a = lax.optimization_barrier((weights, cot, pairs_a))
    weights = weights + [to_core(each) for each in weights]
    cots = [cot] + [exchange(cots, "tensor", k) for k in range(1, tensor)]
    or_a, m_a, l_a, probs_a = call(
        "first",
        functools.partial(first_body, plan, heads_a),
        [((tokens, width), BF16), ((tokens, width), F32), ((tokens, width), BF16), ((heads_a * tokens, keys), BF16)],
        [x, q_a, *pairs_a, offsets_a, output_a, mixer_gain_a],
        [resets, videos],
        [((8, 128), F32)],
    )
    m_a, cots = lax.optimization_barrier((m_a, cots))
    y_a, n_b, q_b, base, *pair_b = call(
        "between",
        functools.partial(between_body, plan),
        [((tokens, width), F32), ((tokens, width), BF16), ((pooled, wide), BF16), ((pooled, wide), F32), *pair(wide)],
        [m_a, l_a, expand_a, reduce_a, *weights, attend_gain_b, project_b, pooling_b, squeeze_b, shortcut_b],
        (),
        hidden,
    )
    pairs_b = share_pairs(plan, pair_b, squeeze_b)
    or_b, m_b, l_b, probs_b = call(
        "second",
        functools.partial(second_body, plan, heads_b),
        [((pooled, wide), BF16), ((pooled, wide), F32), ((pooled, wide), BF16), ((heads_b * pooled, keys), BF16)],
        [q_b, *pairs_b, offsets_b, output_b, mixer_gain_b, base],
        [resets, videos],
        [((8, 128), F32)],
    )
    rows_b = [exchange(l_b, "tensor", k) if k else l_b for k in range(tensor)]
    hidden_rows = (expand_b.shape[1] // LANES) * wide + (wide // LANES) * reduce_b.shape[0]
    half_plane = plane // 2
    hidden_each = padded(hidden_rows, plane)
    units = ((tensor * pooled, expand_b.shape[1]), BF16)
    *shares, hidden_b, grad_pre_b = call(
        "hidden",
        functools.partial(hidden_body, tensor),
        [((pooled, wide), BF16)] * tensor + [units, units],
        [expand_b, reduce_b, *rows_b, *cots],
    )
    sums = everyone(shares, "tensor")
    bias = lambda: [((plan.frames, 8, keys), F32)]
    key_grads = lambda w: (
        [((pooled, 2 * w), F32)] + [((pooled, 2 * w), BF16)] * (seq - 1) + [((memory, 2 * w), BF16)] * 2
    )
    dm_b, dmid_b, doutput_b, dq_b, dtable_b, *back = call(
        "second_back",
        functools.partial(second_back_body, plan, heads_b),
        [((pooled, wide), F32), ((1, wide), F32), ((wide, wide), BF16), ((pooled, wide), F32),
         ((8, 128), F32), *key_grads(wide)],
        [*sums, cot, m_b, mixer_gain_b, or_b, output_b, q_b, probs_b, *pairs_b],
        [resets, videos],
        bias(),
    )
    pieces, dsqueeze_given = return_pairs(plan, back, pairs_b, squeeze_b)
    share = width // tensor
    cross_each = padded((3 + 1) * wide // LANES * share + wide // LANES * (wide // tensor), plane)
    dy_a, dpool_b, dsqueeze_b, dgain_b, keep, give = call(
        "cross",
        functools.partial(cross_body, plan, cross_each),
        [((tokens, width), F32), ((3, 4, wide), F32), ((2, 4, wide), F32), ((1, width), F32)],
        [*pieces, dq_b, dm_b, doutput_b, n_b, y_a, attend_gain_b, project_b, pooling_b, squeeze_b, shortcut_b],
        stage=(2, half_plane, tensor, cross_each, LANES),
    )
    cross = (keep, give)
    hidden_b = after(hidden_b, dgain_b)
    *out_shares, keep, give = call(
        "hidden_rest",
        functools.partial(hidden_rest_body, tensor, hidden_each),
        [((pooled, wide), BF16)] * tensor,
        [reduce_b, hidden_b, grad_pre_b, *rows_b, *cots],
        stage=(2, half_plane, 1, hidden_each, LANES),
    )
    early = (keep, give)
    early, cross = sum_cores(*early), sum_cores(*cross)
    early = [part.reshape(half_plane, -1, LANES) for part in (early, cross)]
    early, dy_a = lax.optimization_barrier((jnp.concatenate(early, axis=1), dy_a))
    early = spread(early, ACROSS)
    first_each = padded(2 * width, plane)
    dmid_a, dm_a, doutput_a, dq_a, dtable_a, *back, keep, give = call(
        "first_back",
        functools.partial(first_back_body, plan, first_each, heads_a),
        [((1, width), F32), ((tokens, width), F32), ((width, width), BF16), ((tokens, width), F32), ((8, 128), F32),
         *key_grads(width)],
        [dy_a, m_a, l_a, mixer_gain_a, or_a, output_a, q_a, probs_a, expand_a, reduce_a, *weights,
         *pairs_a],
        [resets, videos],
        hidden + bias(),
        stage=(2, half_plane, tensor, first_each, LANES),
    )
    if dsqueeze_given is not None:
        dsqueeze_b = dsqueeze_given
    pieces, dsqueeze_given = return_pairs(plan, back, pairs_a, squeeze_a)
    out_sums = everyone(out_shares, "tensor")
    first = sum_cores(keep, give)
    tail_each, small_each = padded(4 * share, plane), padded(128, plane)
    grad_x, keep, give = call(
        "leave",
        functools.partial(leave_body, plan, tail_each, small_each),
        [((tokens, width), BF16)],
        [*pieces, dq_a, dm_a, doutput_a, n_a, x, attend_gain_a, project_a, pooling_a, squeeze_a, dmid_a, dtable_a,
         dgain_b, dpool_b, dsqueeze_b, dmid_b, dtable_b]
        + ([] if dsqueeze_given is None else [dsqueeze_given]),
        (),
        [((2, 4, width), F32), ((2, 4, width), F32), ((128, LANES), F32)],
        stage=(2, half_plane, 1, tensor * tail_each + small_each, LANES),
    )
    last = sum_cores(keep, give)
    last = jnp.concatenate([first.reshape(half_plane, -1, LANES), last[:, 0]], axis=1)
    last, early = lax.optimization_barrier((last, early))
    leaving, = call("exit", exit_body, [(arrived.shape, BF16)], [order, after(grad_x, last), m_b, *out_sums])
    last = spread(last, ACROSS)
    early = sum_first(early)
    cross = halve(early[hidden_each:].reshape(tensor, cross_each, LANES), "tensor")
    early = gather_across(jnp.concatenate([early[:hidden_each], cross], axis=0))
    last, cross, leaving = lax.optimization_barrier((last, cross, leaving))
    last = sum_first(last)
    first_rows = tensor * first_each
    first = last[:first_rows].reshape(tensor, first_each, LANES)
    small = jnp.broadcast_to(last[None, first_rows + tensor * tail_each :], (tensor, small_each, LANES))
    last = last[first_rows : first_rows + tensor * tail_each].reshape(tensor, tail_each, LANES)
    last = jnp.concatenate([first, last, small], axis=1)
    leaving = after(leaving, last)
    last = gather_across(halve(last, "tensor"))
    returned, early = lax.optimization_barrier((spread(leaving.reshape(plan.group, -1, width), home), early))
    returned, early = swap(returned), both_cores(early)
    x_rows = plan.frames * plan.rows * plan.cols
    grad_input = returned[:, :x_rows].reshape(clips_in.shape).astype(F32)
    result = returned[:, x_rows:].reshape(cotangent.shape).astype(F32)
    column = lambda rows, columns: ((rows, columns), F32)
    grad_expand_b, grad_reduce_b, grad_project_b, grad_shortcut_b, grad_output_b = call(
        "unpack_early",
        functools.partial(unpack_body, [(hidden_each, 2), (cross_each, 3)]),
        [
            (expand_b.shape, F32), (reduce_b.shape, F32),
            column(share, 3 * wide), column(share, wide), column(wide // tensor, wide),
        ],
        early,
        (),
        [((2, half_plane, hidden_each + cross_each, LANES), BF16)],
    )
    last, grad_expand_b, grad_input, result = lax.optimization_barrier((last, grad_expand_b, grad_input, result))
    last = both_cores(last)
    grad_expand_a, grad_reduce_a, grad_project_a, grad_output_a, *small = call(
        "unpack_last",
        functools.partial(unpack_body, [(first_each, 2), (tail_each, 2)]),
        [
            (expand_a.shape, F32), (reduce_a.shape, F32), column(share, 3 * width), column(share, width),
            ((width,), F32), (pooling_a.shape, F32), (squeeze_a.shape, F32), (offsets_a.shape, F32), ((width,), F32),
            ((width,), F32), (pooling_b.shape, F32), (squeeze_b.shape, F32), (offsets_b.shape, F32), ((wide,), F32),
        ],
        last,
        (),
        [((128, LANES), F32), ((2, half_plane, first_each + tail_each + small_each, LANES), BF16)],
    )
    return (
        result,
        grad_input,
        small[0],
        grad_project_a,
        small[1],
        small[2],
        small[3],
        grad_output_a,
        small[4],
        grad_expand_a,
        grad_reduce_a,
        small[5],
        grad_project_b,
        small[6],
        small[7],
        small[8],
        grad_output_b,
        grad_shortcut_b,
        small[9],
        grad_expand_b,
        grad_reduce_b,
    )


def solution(mesh):
    clip, seq, tensor = mesh.devices.shape
    split = Mesh(mesh.devices.reshape(clip // 2, 2, seq // 2, 2, tensor), EVERY)
    field = P(("chip", "core"), None, ("far", "near"), "tensor", None)
    up, down = P(None, "tensor"), P("tensor", None)
    block = (P(), P(), P(), P(), P(), P(), P(), up, down)
    block_b = (P(), P(), P(), P(), P(), P(), P(), P(), up, down)
    grads = (P(), down, P(), P(), P(), down, P(), up, down)
    grads_b = (P(), down, P(), P(), P(), down, down, P(), up, down)
    return jax.shard_map(
        local,
        mesh=split,
        in_specs=(field, field, P(), P()) + block + block_b,
        out_specs=(field, field) + grads + grads_b,
        check_vma=False,
    )
```

```python
import functools

import jax
import jax.numpy as jnp
import numpy as np
from jax import lax
from jax.experimental import pallas as pl
from jax.experimental.pallas import tpu as pltpu
from jax.sharding import Mesh
from jax.sharding import PartitionSpec as P

F32 = jnp.float32
BF16 = jnp.bfloat16
HIGHEST = lax.Precision.HIGHEST
EPSILON = 1e-06
MASKED = -1000000000.0
LOG_FOUR = 1.3862943611198906
SIZE = 96
LANES = 384
INTERPRET = False
PLANE = ("chip", "core", "far", "near")
EVERY = PLANE + ("tensor",)
ACROSS = ("chip", "far", "near")
FRAMES = ("far", "core")
FEW = 8
COSTS = {
    "enter": 3, "first": 4, "between": 6, "second": 7, "hidden": 4, "hidden_rest": 5, "second_back": 9, "cross": 8,
    "first_back": 10, "leave": 5, "exit": 2,
}


def wide_row(gain):
    return gain[...].reshape(1, gain.shape[0])


def log2(n):
    return n.bit_length() - 1


def mm(left, right):
    return jnp.dot(left, right, preferred_element_type=F32)


def mm_tl(left, right):
    return lax.dot_general(left, right, (((0,), (0,)), ((), ())), preferred_element_type=F32)


def mm_tr(left, right):
    return lax.dot_general(left, right, (((1,), (1,)), ((), ())), preferred_element_type=F32)


def norm(field):
    mean = jnp.mean(field, axis=-1, keepdims=True)
    centered = field - mean
    inverse = lax.rsqrt(jnp.mean(centered * centered, axis=-1, keepdims=True) + EPSILON)
    return centered * inverse, inverse


def norm_back(grad, gain, normed, inverse):
    scaled = grad * gain
    field = inverse * (
        scaled
        - jnp.mean(scaled, axis=-1, keepdims=True)
        - normed * jnp.mean(scaled * normed, axis=-1, keepdims=True)
    )
    return field, jnp.sum(grad * normed, axis=0, keepdims=True)


def gelu(values):
    return 0.5 * values * (1.0 + lax.erf(values * 0.7071067811865476))


def gelu_both(values):
    half = 0.5 * (1.0 + lax.erf(values * 0.7071067811865476))
    slope = half + values * jnp.exp(-0.5 * values * values) * 0.3989422804014327
    return values * half, slope


def blocks(values, count):
    rows = values.shape[0] // count
    return [values[i * rows : (i + 1) * rows] for i in range(count)]


def pool(values, weights):
    parts = blocks(values, 4)
    total = parts[0] * weights[0:1]
    for p in range(1, 4):
        total = total + parts[p] * weights[p : p + 1]
    return total


class Plan:
    def __init__(self, seq, tensor, shape):
        clips, frames, rows, cols, _ = shape
        self.seq, self.tensor = seq, tensor
        assert clips == tensor and frames % seq == 0 and rows % 2 == 0 and cols % 2 == 0
        self.all_frames = frames
        self.frames = frames // seq
        self.rows, self.cols = rows, cols
        self.group = seq * tensor
        self.cells = self.group * rows * cols // 4
        self.pooled = self.frames * self.cells
        self.tokens = 4 * self.pooled
        self.local_squeeze = self.frames % 4 == 0
        self.memory = frames // 4 * self.cells
        self.own = seq * self.pooled
        self.sources = seq + 2 * (seq if self.local_squeeze else 1)
        self.returned = seq + (2 * seq if self.local_squeeze else 0)
        self.keys = self.own + 2 * self.memory
        for n in (self.cells, self.pooled, self.memory, self.own, self.frames, seq):
            assert n == 1 << log2(n)

    def arrange(self):
        take = np.arange(self.tokens).reshape(
            self.group, self.frames, self.rows // 2, 2, self.cols // 2, 2
        )
        per = self.frames * self.rows * self.cols
        half = per // 4 * 2
        step = per + half
        x_rows = take // per * step + take % per
        x_rows = x_rows.transpose(3, 5, 1, 0, 2, 4).reshape(-1)
        cot = np.arange(self.pooled).reshape(self.group, self.frames, -1)
        low = cot // (per // 4) * step + per + cot % (per // 4) * 2
        low = low.transpose(1, 0, 2).reshape(-1)
        order = np.concatenate([x_rows, low, low + 1])
        return (order[:, None] == np.arange(self.group * step)[None, :]).astype(np.float32)


def clip_scalars(plan, resets, videos):
    s = lax.axis_index("far") * lax.axis_size("core") + lax.axis_index("core")
    chip = lax.axis_index("chip") * lax.axis_size("near") + lax.axis_index("near")
    g = chip * plan.tensor + lax.axis_index("tensor")
    before = jnp.maximum(g - 1, 0)
    earlier = jnp.maximum(g - 2, 0)
    first = (g >= 1) & (videos[g] == videos[before]) & (resets[g] == 0)
    second = first & (g >= 2) & (videos[before] == videos[earlier]) & (resets[before] == 0)
    return s, first.astype(jnp.int32), second.astype(jnp.int32)


def key_facts(plan, s, first, second):
    k = lax.broadcasted_iota(jnp.int32, (1, plan.keys), 1)
    own_time = ((s ^ (k >> log2(plan.pooled))) << log2(plan.frames)) + (
        (k & (plan.pooled - 1)) >> log2(plan.cells)
    )
    m = k - plan.own
    late = (m >> log2(plan.memory)) > 0
    g = (m & (plan.memory - 1)) >> log2(plan.cells)
    if plan.local_squeeze:
        each = log2(plan.frames // 4)
        squeezed = ((s ^ (g >> each)) << each) + (g & (plan.frames // 4 - 1))
    else:
        squeezed = (s >> log2(4 // plan.frames)) ^ g
    kind = jnp.where(m < 0, 0, jnp.where(late, 2, 1))
    time = jnp.where(m < 0, own_time, 4 * squeezed - plan.all_frames * kind)
    counts = jnp.where(kind == 0, 1, jnp.where(kind == 1, first, second))
    return time, counts


def offset_onehot(plan, s, time, frame):
    index = s * plan.frames + frame - time + plan.all_frames - 1
    rows = lax.broadcasted_iota(jnp.int32, (128, plan.keys), 0)
    return jnp.where(rows == index, 1.0, 0.0).astype(F32)


def head_mask(width, head):
    lane = lax.broadcasted_iota(jnp.int32, (1, width), 1)
    inside = (lane >= head * SIZE) & (lane < (head + 1) * SIZE)
    return jnp.where(inside, 1.0, 0.0).astype(F32)


def attend(plan, query, keys, values, offsets, heads, probs_ref, table_ref, scalars):
    s, first, second = scalars
    rows, width = query.shape
    places = rows // plan.pooled
    time, counts = key_facts(plan, s, first, second)
    biases = []
    table_ref[...] = jnp.zeros(table_ref.shape, F32)
    table_ref[:heads, : offsets.shape[1]] = offsets[...]
    table = table_ref[...]
    for f in range(plan.frames):
        onehot = offset_onehot(plan, s, time, f)
        bias = jnp.dot(table, onehot, precision=HIGHEST, preferred_element_type=F32)
        biases.append(jnp.where(counts > 0, bias, MASKED))
    total = query.astype(F32)
    for h in range(heads):
        mask = head_mask(width, h)
        scores = mm_tr(query * mask.astype(BF16), keys) * SIZE ** (-0.5)
        bias = jnp.concatenate(
            [jnp.broadcast_to(b[h : h + 1], (plan.cells, plan.keys)) for b in biases] * places, axis=0
        )
        scores = scores + bias
        scores = jnp.exp(scores - jnp.max(scores, axis=-1, keepdims=True))
        probs = scores * (1.0 / jnp.sum(scores, axis=-1, keepdims=True))
        probs = probs.astype(BF16)
        probs_ref[h * rows : (h + 1) * rows] = probs
        total = total + mm(probs, values) * mask
    return total


def attend_back(plan, grad, query, keys, values, probs_ref, heads, bias_ref, table_ref, scalars):
    s, first, second = scalars
    rows, width = query.shape
    places = rows // plan.pooled
    grad_r = grad.astype(BF16)
    grad_query = grad
    grad_keys = jnp.zeros((plan.keys, width), F32)
    grad_values = jnp.zeros((plan.keys, width), F32)
    bias_ref[...] = jnp.zeros(bias_ref.shape, F32)
    for h in range(heads):
        mask = head_mask(width, h)
        mask_r = mask.astype(BF16)
        grad_head = grad_r * mask_r
        query_head = query * mask_r
        probs_r = probs_ref[h * rows : (h + 1) * rows]
        probs = probs_r.astype(F32)
        grad_probs = mm_tr(grad_head, values)
        weighted = probs * grad_probs
        grad_scores = weighted - probs * jnp.sum(weighted, axis=-1, keepdims=True)
        for f in range(plan.frames):
            part = grad_scores[f * plan.cells : (f + 1) * plan.cells]
            for p in range(1, places):
                at = p * plan.pooled + f * plan.cells
                part = part + grad_scores[at : at + plan.cells]
            bias_ref[f, h : h + 1, :] = jnp.sum(part, axis=0, keepdims=True)
        grad_scores_r = grad_scores.astype(BF16)
        grad_query = grad_query + mm(grad_scores_r, keys) * (mask * SIZE ** (-0.5))
        grad_keys = grad_keys + mm_tl(grad_scores_r, query_head)
        grad_values = grad_values + mm_tl(probs_r, grad_head)
    time, _ = key_facts(plan, s, first, second)
    table = jnp.zeros((8, 128), F32)
    for f in range(plan.frames):
        onehot = offset_onehot(plan, s, time, f)
        table = table + lax.dot_general(
            bias_ref[f], onehot, (((1,), (1,)), ((), ())), precision=HIGHEST, preferred_element_type=F32
        )
    table_ref[...] = table
    return grad_query, grad_keys * SIZE ** (-0.5), grad_values


def load_pairs(refs, width):
    pairs = jnp.concatenate([ref[...] for ref in refs], axis=0)
    return pairs[:, :width], pairs[:, width:]


def pool_pair(plan, raw, pool_ref, squeeze_ref, pair_ref, memory_ref=None):
    width = raw.shape[1] // 2
    for i in range(2):
        pooled = pool(raw[:, i * width : (i + 1) * width], pool_ref[pool_ref.shape[0] - 2 + i])
        pair_ref[:, i * width : (i + 1) * width] = pooled.astype(BF16)
        if memory_ref is not None:
            weights = squeeze_ref[i]
            for g in range(plan.frames // 4):
                total = None
                for k in range(4):
                    at = (4 * g + k) * plan.cells
                    part = pooled[at : at + plan.cells] * weights[k : k + 1]
                    total = part if total is None else total + part
                at = g * plan.cells
                memory_ref[at : at + plan.cells, i * width : (i + 1) * width] = total.astype(BF16)


def store_rows(stage, each, z, start, values, base=0):
    core = lax.axis_index("core")
    half, at = stage.shape[1], 0
    while at < values.shape[0]:
        who, off = divmod(start + at, each)
        n = min(each - off, values.shape[0] - at)
        part = values[at : at + n].astype(BF16)
        rows = pl.ds(base + off if isinstance(base, int) else pl.multiple_of(base + off, 16), n)
        stage[(who // half) ^ core, who % half, z, rows, :] = part
        at += n


def store_columns(stage, each, tensor, start, values):
    rows = values.shape[0] // tensor
    t = lax.axis_index("tensor")
    for z in range(tensor):
        for c in range(values.shape[1] // LANES):
            part = values[z * rows : (z + 1) * rows, c * LANES : (c + 1) * LANES]
            store_rows(stage, each, z ^ t, start + c * rows, part)
    return start + values.shape[1] // LANES * rows


def send_stage(stage, keep, give, sems):
    copies = [pltpu.make_async_copy(stage.at[i], (keep, give)[i], sems.at[i]) for i in range(2)]
    for copy in copies:
        copy.start()
    for copy in copies:
        copy.wait()


def smooth_max(raw):
    parts = blocks(raw, 4)
    highest = jnp.maximum(jnp.maximum(parts[0], parts[1]), jnp.maximum(parts[2], parts[3]))
    total = jnp.exp(parts[0] - highest)
    for p in range(1, 4):
        total = total + jnp.exp(parts[p] - highest)
    return highest + jnp.log(total) - LOG_FOUR


def smooth_max_back(raw, grad):
    parts = blocks(raw, 4)
    highest = jnp.maximum(jnp.maximum(parts[0], parts[1]), jnp.maximum(parts[2], parts[3]))
    parts = [jnp.exp(part - highest) for part in parts]
    total = parts[0] + parts[1] + parts[2] + parts[3]
    scaled = grad / total
    return jnp.concatenate([part * scaled for part in parts], axis=0)


def call(name, body, outs, vmem, smem=(), scratch=(), stage=None):
    moved = COSTS.get(name, 4) * 3_000_000
    scratch = [pltpu.VMEM(shape, dtype) for shape, dtype in scratch]
    spaces = [pltpu.VMEM] * len(outs)
    if stage is not None:
        outs = outs + [(stage[1:], BF16)] * 2
        spaces += [pl.ANY] * 2
        scratch += [pltpu.VMEM(stage, BF16), pltpu.SemaphoreType.DMA((2,))]
    return pl.pallas_call(
        body,
        out_shape=[jax.ShapeDtypeStruct(shape, dtype) for shape, dtype in outs],
        in_specs=[pl.BlockSpec(memory_space=pltpu.SMEM)] * len(smem)
        + [pl.BlockSpec(memory_space=pltpu.VMEM)] * len(vmem),
        out_specs=[pl.BlockSpec(memory_space=space) for space in spaces],
        scratch_shapes=scratch,
        name=name,
        interpret=INTERPRET,
        cost_estimate=pl.CostEstimate(flops=0, bytes_accessed=moved, transcendentals=0),
        compiler_params=pltpu.CompilerParams(vmem_limit_bytes=56 << 20),
    )(*smem, *vmem)


def enter_body(plan, arrived, order, gain, project, pools, squeeze, x_ref, cot_ref, n_ref, q_ref, *pair):
    rows = mm(order[...], arrived[...])
    x = rows[: plan.tokens]
    x_ref[...] = x.astype(BF16)
    width = cot_ref.shape[1] // 2
    cot_ref[:, :width] = rows[plan.tokens : plan.tokens + plan.pooled].astype(BF16)
    cot_ref[:, width:] = rows[plan.tokens + plan.pooled :].astype(BF16)
    n = (norm(x)[0] * wide_row(gain)).astype(BF16)
    n_ref[...] = n
    raw = mm(n, project[...])
    q_ref[...] = raw[:, : x.shape[1]].astype(BF16)
    pool_pair(plan, raw[:, x.shape[1] :], pools, squeeze, *pair)


def pick_hidden(tensor, expand, reduce, weights, up_ref, down_ref):
    up_ref[0] = expand[...]
    down_ref[0] = reduce[...]
    core, near = lax.axis_index("core"), lax.axis_index("near")
    rows = weights[0].shape[0] // (tensor - 1)

    def put(first, second):
        for i, piece in enumerate(weights):
            at = pl.multiple_of(((i % 2) ^ near) * rows, 16)
            for k in range(1, tensor):
                part = piece[(k - 1) * rows : k * rows, :]
                (second if i // 2 else first)[k, pl.ds(at, rows), :] = part

    @pl.when(core == 0)
    def _():
        put(up_ref, down_ref)

    @pl.when(core != 0)
    def _():
        put(down_ref, up_ref)


def first_body(plan, heads, resets, videos, *refs):
    x, query = refs[:2]
    pairs, refs = refs[2 : 2 + plan.sources], refs[2 + plan.sources :]
    table, output, gain, or_ref, m_ref, l_ref, probs_ref, table_ref = refs
    scalars = clip_scalars(plan, resets, videos)
    keys, values = load_pairs(pairs, x.shape[1])
    mixed_r = attend(plan, query[...], keys, values, table, heads, probs_ref, table_ref, scalars).astype(BF16)
    or_ref[...] = mixed_r
    middle = x[...].astype(F32) + mm(mixed_r, output[...])
    m_ref[...] = middle
    l_ref[...] = (norm(middle)[0] * wide_row(gain)).astype(BF16)


def between_body(plan, m_ref, l_ref, expand, reduce, *refs):
    weights, refs = refs[:4], refs[4:]
    gain_b, project_b, pool_b, squeeze_b, shortcut_b, y_ref, nb_ref, qb_ref, base_ref = refs[:9]
    pair, up_ref, down_ref = refs[9:-2], refs[-2], refs[-1]
    pick_hidden(plan.tensor, expand, reduce, weights, up_ref, down_ref)
    l = l_ref[...]
    y = m_ref[...]
    for k in range(plan.tensor):
        hidden = gelu(mm(l, up_ref[k])).astype(BF16)
        y = y + mm(hidden, down_ref[k])
    y_ref[...] = y
    n = (norm(y)[0] * wide_row(gain_b)).astype(BF16)
    nb_ref[...] = n
    wide = base_ref.shape[1]
    raw = mm(n, project_b[...])
    qb_ref[...] = pool(raw[:, :wide], pool_b[0]).astype(BF16)
    pool_pair(plan, raw[:, wide:], pool_b, squeeze_b, *pair)
    base_ref[...] = smooth_max(mm(n, shortcut_b[...]))


def second_body(plan, heads, resets, videos, *refs):
    query, pairs, refs = refs[0], refs[1 : 1 + plan.sources], refs[1 + plan.sources :]
    table, output, gain, base, or_ref, m_ref, l_ref, probs_ref, table_ref = refs
    width = query.shape[1]
    scalars = clip_scalars(plan, resets, videos)
    keys, values = load_pairs(pairs, width)
    mixed_r = attend(plan, query[...], keys, values, table, heads, probs_ref, table_ref, scalars).astype(BF16)
    or_ref[...] = mixed_r
    middle = base[...] + mm(mixed_r, output[...])
    m_ref[...] = middle
    l_ref[...] = (norm(middle)[0] * wide_row(gain)).astype(BF16)


def hidden_body(tensor, up, down, *refs):
    rows, grads, refs = refs[:tensor], refs[tensor : 2 * tensor], refs[2 * tensor :]
    sends, (hidden_ref, grad_pre_ref) = refs[:tensor], refs[tensor:]
    l = jnp.concatenate([ref[...] for ref in rows], axis=0)
    grad = jnp.concatenate([ref[...] for ref in grads], axis=0)
    gate, slope = gelu_both(mm(l, up[...]))
    hidden_ref[...] = gate.astype(BF16)
    grad_pre = (slope * mm_tr(grad, down[...])).astype(BF16)
    grad_pre_ref[...] = grad_pre
    for ref, part in zip(sends, blocks(mm_tr(grad_pre, up[...]), tensor)):
        ref[...] = part.astype(BF16)


def hidden_rest_body(tensor, each, down, hidden_ref, grad_pre_ref, *refs):
    rows, grads, refs = refs[:tensor], refs[tensor : 2 * tensor], refs[2 * tensor :]
    sends, (keep, give, stage, sems) = refs[:tensor], refs[tensor:]
    hidden, grad_pre = hidden_ref[...], grad_pre_ref[...]
    l = jnp.concatenate([ref[...] for ref in rows], axis=0)
    grad = jnp.concatenate([ref[...] for ref in grads], axis=0)
    at = 0
    for whole in (mm_tl(l, grad_pre), mm_tl(hidden, grad)):
        for c in range(whole.shape[1] // LANES):
            part = whole[:, c * LANES : (c + 1) * LANES]
            store_rows(stage, each, 0, at, part)
            at += part.shape[0]
    for ref, part in zip(sends, blocks(mm(hidden, down[...]), tensor)):
        ref[...] = part.astype(BF16)
    send_stage(stage, keep, give, sems)


def sum_refs(refs):
    total = refs[0][...].astype(F32)
    for ref in refs[1:]:
        total = total + ref[...].astype(F32)
    return total


def second_back_body(plan, heads, resets, videos, *refs):
    refs = list(refs)
    sums, refs = refs[: plan.tensor], refs[plan.tensor :]
    cot, middle, gain, mixed, output, query, probs = refs[:7]
    pairs, refs = refs[7 : 7 + plan.sources], refs[7 + plan.sources :]
    dm_ref, dgain_ref = refs[:2]
    refs = refs[2:]
    normed, inverse = norm(middle[...])
    grad, dgain = norm_back(sum_refs(sums), wide_row(gain), normed, inverse)
    dgain_ref[...] = dgain
    grad = cot[...].astype(F32) + grad
    dm_ref[...] = grad
    store_back(plan, heads, resets, videos, grad, mixed, output, query, probs, pairs, *refs)


def store_back(plan, heads, resets, videos, grad, mixed, output, query, probs, pairs, doutput_ref, dq_ref, dtable_ref,
               *refs):
    width = query.shape[1]
    scalars = clip_scalars(plan, resets, videos)
    grad_r = grad.astype(BF16)
    doutput_ref[...] = mm_tl(mixed[...], grad_r).astype(BF16)
    grads, bias_ref = refs[:-1], refs[-1]
    keys, values = load_pairs(pairs, width)
    dq, dk, dv = attend_back(
        plan, mm_tr(grad_r, output[...]), query[...], keys, values, probs, heads, bias_ref, dtable_ref, scalars
    )
    dq_ref[...] = dq
    for i, part in enumerate((dk, dv)):
        lanes = slice(i * width, (i + 1) * width)
        at = 0
        for ref in grads:
            ref[:, lanes] = part[at : at + ref.shape[0]].astype(ref.dtype)
            at += ref.shape[0]


def pair_grads(plan, refs):
    own, received = refs[0], refs[1 : plan.seq]
    grad = own[...]
    for ref in received:
        grad = grad + ref[...].astype(F32)
    if not plan.local_squeeze:
        return grad, None
    memory = None
    size = plan.memory // plan.seq
    for i, ref in enumerate(refs[plan.seq :]):
        o = i % plan.seq
        part = ref[o * size : (o + 1) * size, :].astype(F32)
        memory = part if memory is None else memory + part
    return grad, memory


def unpool(plan, raw, grad, memory, pool_ref, squeeze_ref, dpool_ref, dsqueeze_ref, first):
    width = raw.shape[1] // 2
    result = []
    for i in range(2):
        weights = pool_ref[first + i]
        lanes = slice(i * width, (i + 1) * width)
        part = grad[:, lanes]
        source = raw[:, lanes]
        if plan.local_squeeze:
            pooled = pool(source, weights)
            ws = squeeze_ref[i]
            pieces = []
            sums = [None] * 4
            for g in range(plan.frames // 4):
                dm = memory[g * plan.cells : (g + 1) * plan.cells, lanes]
                for k in range(4):
                    at = (4 * g + k) * plan.cells
                    pieces.append(part[at : at + plan.cells] + dm * ws[k : k + 1])
                    total = jnp.sum(dm * pooled[at : at + plan.cells], axis=0, keepdims=True)
                    sums[k] = total if sums[k] is None else sums[k] + total
            part = jnp.concatenate(pieces, axis=0)
            for k in range(4):
                dsqueeze_ref[i, k : k + 1, :] = sums[k]
        result.append(unpool_one(source, part, weights, dpool_ref, first + i))
    return result


def unpool_one(source, part, weights, dpool_ref, place):
    pieces = []
    for p, piece in enumerate(blocks(source, 4)):
        dpool_ref[place, p : p + 1, :] = jnp.sum(part * piece, axis=0, keepdims=True)
        pieces.append((part * weights[p : p + 1]).astype(BF16))
    return jnp.concatenate(pieces, axis=0)


def cross_body(plan, each, *refs):
    pieces = plan.returned
    grads = refs[:pieces]
    (dq, dm, doutput_b, n_ref, y_ref, gain_b, project_b, pool_b, squeeze_b, shortcut_b,
     dy_ref, dpool_ref, dsqueeze_ref, dgain_ref, keep, give, stage, sems) = refs[pieces:]
    tensor = plan.tensor
    wide = dm.shape[1]
    n = n_ref[...]
    grad, memory = pair_grads(plan, grads)
    raw = mm(n, project_b[...])
    parts = [unpool_one(raw[:, :wide], dq[...], pool_b[0], dpool_ref, 0)]
    parts += unpool(plan, raw[:, wide:], grad, memory, pool_b, squeeze_b, dpool_ref, dsqueeze_ref, 1)
    at = 0
    grad_n = None
    for i, part in enumerate(parts):
        at = store_columns(stage, each, tensor, at, mm_tl(n, part))
        back = mm_tr(part, project_b[:, i * wide : (i + 1) * wide])
        grad_n = back if grad_n is None else grad_n + back
    grad_z = smooth_max_back(mm(n, shortcut_b[...]), dm[...]).astype(BF16)
    at = store_columns(stage, each, tensor, at, mm_tl(n, grad_z))
    store_columns(stage, each, tensor, at, doutput_b[...])
    grad_n = grad_n + mm_tr(grad_z, shortcut_b[...])
    normed, inverse = norm(y_ref[...])
    grad_y, dgain = norm_back(grad_n, wide_row(gain_b), normed, inverse)
    dgain_ref[...] = dgain
    dy_ref[...] = grad_y
    send_stage(stage, keep, give, sems)


def first_back_body(plan, each, heads, resets, videos, *refs):
    refs = list(refs)

    def take(n):
        taken = refs[:n]
        del refs[:n]
        return taken

    dy_ref, m_ref, l_ref, gain, mixed, output, query, probs, expand, reduce = take(10)
    weights = take(4)
    pairs = take(plan.sources)
    dgain_ref, dm_out = take(2)
    refs, (keep, give, up_ref, down_ref, bias_ref, stage, sems) = refs[:-7], refs[-7:]
    tensor = plan.tensor
    pick_hidden(tensor, expand, reduce, weights, up_ref, down_ref)
    grad_y = dy_ref[...]
    grad_r = grad_y.astype(BF16)
    l = l_ref[...]
    grad_l = None
    for k in range(tensor):
        gate, slope = gelu_both(mm(l, up_ref[k]))
        hidden = gate.astype(BF16)
        grad_pre = (slope * mm_tr(grad_r, down_ref[k])).astype(BF16)
        store_rows(stage, each, k, 0, mm_tl(l, grad_pre))
        store_rows(stage, each, k, l.shape[1], mm_tl(hidden, grad_r))
        back = mm_tr(grad_pre, up_ref[k])
        grad_l = back if grad_l is None else grad_l + back
    normed, inverse = norm(m_ref[...])
    grad, dgain = norm_back(grad_l, wide_row(gain), normed, inverse)
    dgain_ref[...] = dgain
    grad = grad_y + grad
    dm_out[...] = grad
    store_back(plan, heads, resets, videos, grad, mixed, output, query, probs, pairs, *refs, bias_ref)
    send_stage(stage, keep, give, sems)


def store_tail(stage, each, tensor, start, values):
    rows = values.shape[0] // tensor
    t = lax.axis_index("tensor")
    for z in range(tensor):
        for c in range(values.shape[1] // LANES):
            part = values[z * rows : (z + 1) * rows, c * LANES : (c + 1) * LANES]
            store_rows(stage, each, 0, start + c * rows, part, (z ^ t) * each)
    return start + values.shape[1] // LANES * rows


def load_rows(whole, each, start, count, base=0):
    half = whole.shape[1]
    parts, at = [], 0
    while at < count:
        who, off = divmod(start + at, each)
        n = min(each - off, count - at)
        parts.append(whole[who // half, who % half, base + off : base + off + n, :].astype(F32))
        at += n
    return parts


def across_index():
    index = 0
    for axis in ACROSS:
        index = index * lax.axis_size(axis) + lax.axis_index(axis)
    return index


def unpack_columns(whole, each, base, start, out):
    rows = out.shape[0]
    for c in range(out.shape[1] // LANES):
        at = 0
        for part in load_rows(whole, each, start + c * rows, rows, base):
            out[at : at + part.shape[0], c * LANES : (c + 1) * LANES] = part
            at += part.shape[0]
    return start + out.shape[1] // LANES * rows


def unpack_body(groups, *refs):
    core, across = lax.axis_index("core"), across_index()
    pieces, refs = refs[:2], refs[2:]
    count = sum(n for _, n in groups)
    outs, small, whole = refs[:count], refs[count:-1], refs[-1]
    sums, small = (small[-1], small[:-1]) if small else (None, small)
    for i, ref in enumerate(pieces):
        for k in range(ref.shape[0]):
            whole[i ^ core, k ^ across] = ref[k]
    base, first = 0, 0
    for each, n in groups:
        at = 0
        for out in outs[first : first + n]:
            at = unpack_columns(whole, each, base, at, out)
        base, first = base + each, first + n
    if sums is None:
        return
    at = 0
    for part in load_rows(whole, whole.shape[2] - base, 0, sums.shape[0], base):
        sums[at : at + part.shape[0]] = part
        at += part.shape[0]
    gain_a, pool_a, squeeze_a, table_a, mid_a, gain_b, pool_b, squeeze_b, table_b, mid_b = small
    for i, ref in enumerate((gain_a, mid_a, gain_b)):
        ref[...] = sums[i]
    for i in range(2):
        half = slice(i * LANES, (i + 1) * LANES)
        mid_b[half] = sums[3 + i]
        pool_a[i] = sums[8 + 4 * i : 12 + 4 * i, :]
        squeeze_a[i] = sums[16 + 4 * i : 20 + 4 * i, :]
        for j in range(3):
            pool_b[j, :, half] = sums[24 + 16 * i + 4 * j : 28 + 16 * i + 4 * j, :]
        for j in range(2):
            squeeze_b[j, :, half] = sums[56 + 8 * i + 4 * j : 60 + 8 * i + 4 * j, :]
    for ref, at in ((table_a, 72), (table_b, 80)):
        ref[...] = sums[at : at + ref.shape[0], : ref.shape[1]]


def leave_body(plan, each, small_each, *refs):
    refs = list(refs)
    pieces = plan.returned
    grads, refs = refs[:pieces], refs[pieces:]
    (dq, dm, doutput, n_ref, x_ref, gain, project, pools, squeeze,
     dgain_mid, dtable, dgain_b, dpool_b, dsqueeze_b, dmid_b, dtable_b) = refs[:16]
    refs = refs[16:]
    given = refs.pop(0) if not plan.local_squeeze else None
    grad_ref, keep, give, dpool_ref, dsqueeze_ref, sum_ref, stage, sems = refs
    tensor = plan.tensor
    width = x_ref.shape[1]
    n = n_ref[...]
    grad, memory = pair_grads(plan, grads)
    raw = mm(n, project[:, width:])
    parts = [dq[...].astype(BF16)]
    parts += unpool(plan, raw, grad, memory, pools, squeeze, dpool_ref, dsqueeze_ref, 0)
    at = 0
    grad_n = None
    for i, part in enumerate(parts):
        at = store_tail(stage, each, tensor, at, mm_tl(n, part))
        back = mm_tr(part, project[:, i * width : (i + 1) * width])
        grad_n = back if grad_n is None else grad_n + back
    store_tail(stage, each, tensor, at, doutput[...])
    normed, inverse = norm(x_ref[...].astype(F32))
    grad_x, dgain = norm_back(grad_n, wide_row(gain), normed, inverse)
    grad_ref[...] = (grad_x + dm[...]).astype(BF16)
    sum_ref[...] = jnp.zeros(sum_ref.shape, F32)
    squeeze_a = dsqueeze_ref if given is None else given
    sum_ref[0:1, :] = dgain
    sum_ref[1:2, :] = dgain_mid[...]
    sum_ref[2:3, :] = dgain_b[...]
    for i in range(2):
        half = slice(i * width, (i + 1) * width)
        sum_ref[3 + i : 4 + i, :] = dmid_b[:, half]
        sum_ref[8 + 4 * i : 12 + 4 * i, :] = dpool_ref[i]
        sum_ref[16 + 4 * i : 20 + 4 * i, :] = squeeze_a[i]
        for j in range(3):
            sum_ref[24 + 16 * i + 4 * j : 28 + 16 * i + 4 * j, :] = dpool_b[j, :, half]
        for j in range(2):
            sum_ref[56 + 8 * i + 4 * j : 60 + 8 * i + 4 * j, :] = dsqueeze_b[j, :, half]
    sum_ref[72:80, :128] = dtable[...]
    sum_ref[80:88, :128] = dtable_b[...]
    store_rows(stage, small_each, 0, 0, sum_ref[...], tensor * each)
    send_stage(stage, keep, give, sems)


def exit_body(order, grad_x, middle_b, *refs):
    outs, send_ref = refs[:-1], refs[-1]
    width = grad_x.shape[1]
    out = (middle_b[...] + sum_refs(outs)).astype(BF16)
    leaving = jnp.concatenate([grad_x[...], out[:, :width], out[:, width:]], axis=0)
    send_ref[...] = mm_tl(order[...], leaving).astype(BF16)


def exchange(values, axes, by):
    axes = (axes,) if isinstance(axes, str) else axes
    order = [axis for axis in EVERY if axis in axes]
    sizes = [lax.axis_size(axis) for axis in axes]
    into = [axes.index(axis) for axis in order]
    place = np.arange(np.prod(sizes)).reshape(sizes).transpose(into).reshape(-1)
    where = np.argsort(place)
    return lax.ppermute(values, tuple(order), [(i, int(where[p ^ by])) for i, p in enumerate(place)])


def to_core(values):
    return exchange(values, "core", 1)


def swap(values):
    cores, near = lax.axis_size("core"), lax.axis_size("near")
    assert cores == near
    pairs = [(i * near + j, j * near + i) for i in range(cores) for j in range(near)]
    return lax.ppermute(values, ("core", "near"), pairs)


def shift(values, by):
    chips, cores, far, near, tensor = (lax.axis_size(axis) for axis in EVERY)
    clips = chips * near * tensor

    def place(g, core, f):
        chip, n = divmod(g // tensor, near)
        return (((chip * cores + core) * far + f) * near + n) * tensor + g % tensor

    pairs = [
        (place(g, core, f), place(g + by, core, f))
        for g in range(clips)
        for core in range(cores)
        for f in range(far)
        if 0 <= g + by < clips
    ]
    return lax.ppermute(values, EVERY, pairs)


def relative_weights(plan, squeeze):
    s = lax.axis_index(FRAMES)
    order = jnp.arange(plan.all_frames)
    frame = ((s ^ (order // plan.frames)) * plan.frames + order % plan.frames) % 4
    pair = jnp.concatenate([squeeze[0], squeeze[1]], axis=-1)
    return pair[frame], frame


def share_pairs(plan, pair, squeeze):
    pairs = [pair[0]] + [exchange(pair[0], FRAMES, o) for o in range(1, plan.seq)]
    if plan.local_squeeze:
        memories = [shift(pair[1], by) for by in (1, 2)]
        return pairs + [exchange(each, FRAMES, o) if o else each for each in memories for o in range(plan.seq)]
    memory = squeeze_all(plan, pairs, squeeze)
    return pairs + [shift(memory, 1), shift(memory, 2)]


def by_frame(plan, pairs):
    together = jnp.concatenate([each.astype(F32) for each in pairs], axis=0)
    return together.reshape(plan.all_frames // 4, 4, plan.cells, -1)


def squeeze_all(plan, pairs, squeeze):
    weights = relative_weights(plan, squeeze)[0].reshape(plan.all_frames // 4, 4, 1, -1)
    total = jnp.sum(by_frame(plan, pairs) * weights, axis=1)
    return total.reshape(plan.memory, -1).astype(BF16)


def return_pairs(plan, grads, pairs, squeeze):
    own, others, memories = grads[0], grads[1 : plan.seq], grads[plan.seq :]
    memories = [shift(memories[0], -1), shift(memories[1], -2)]
    if plan.local_squeeze:
        received = [exchange(each, FRAMES, o + 1) for o, each in enumerate(others)]
        memories = [exchange(each, FRAMES, o) if o else each for each in memories for o in range(plan.seq)]
        return [own] + received + memories, None
    memory = memories[0].astype(F32) + memories[1].astype(F32)
    weights, frame = relative_weights(plan, squeeze)
    weights = weights.reshape(plan.all_frames // 4, 4, 1, -1)
    memory = memory.reshape(plan.all_frames // 4, 1, plan.cells, -1)
    both = by_frame(plan, [own, *others]) + memory * weights
    both = jnp.split(both.reshape(plan.own, -1), plan.seq, axis=0)
    sums = jnp.sum(by_frame(plan, pairs[: plan.seq]) * memory, axis=2).reshape(plan.all_frames, -1)
    onehot = (frame[None, :] == jnp.arange(4)[:, None]).astype(F32)
    sums = jnp.dot(onehot, sums, precision=HIGHEST)
    width = sums.shape[1] // 2
    received = [
        exchange(each.astype(BF16), FRAMES, o + 1) for o, each in enumerate(both[1:])
    ]
    return [both[0]] + received, jnp.stack([sums[:, :width], sums[:, width:]])


def add_all(parts):
    total = parts[0].astype(F32)
    for part in parts[1:]:
        total = total + part.astype(F32)
    return total.astype(BF16)


def sum_first(values):
    return add_all([values[k] for k in range(values.shape[0])])


def everyone(values, axis):
    return [values[0]] + [exchange(values[k], axis, k) for k in range(1, lax.axis_size(axis))]


def spread(values, axes):
    return lax.all_to_all(values, axes, 0, 0, tiled=True)


def after(value, *others):
    return lax.optimization_barrier((value, others))[0]


def sum_pair(keep, other):
    return (keep.astype(F32) + other.astype(F32)).astype(BF16)


def sum_cores(keep, give):
    return sum_pair(keep, to_core(give))


def scatter(values):
    count = lax.axis_size(ACROSS)
    if count > FEW:
        values = spread(values, ACROSS)
        return [values[k] for k in range(count)]
    parts = [lax.dynamic_index_in_dim(values, across_index() ^ k, keepdims=False) for k in range(count)]
    return [exchange(part, ACROSS, k) if k else part for k, part in enumerate(parts)]


def gather_across(values):
    return jnp.stack([exchange(values, ACROSS, k) if k else values for k in range(lax.axis_size(ACROSS))])


def gather_plane(values):
    values = gather_across(values)
    return [values, to_core(values)]


def halve(values, axis):
    for bit in range(log2(lax.axis_size(axis))):
        values = values.reshape(-1, 2, *values.shape[1:])
        values = sum_pair(values[:, 0], exchange(values[:, 1], axis, 1 << bit))
    return values[0]


def both_cores(values):
    return [values, to_core(values)]


def padded(rows, parts):
    return -(-rows // (16 * parts)) * 16


def local(
    clips_in, cotangent, resets, videos,
    attend_gain_a, project_a, pooling_a, squeeze_a, offsets_a, output_a, mixer_gain_a, expand_a, reduce_a,
    attend_gain_b, project_b, pooling_b, squeeze_b, offsets_b, output_b, shortcut_b, mixer_gain_b, expand_b, reduce_b,
):
    seq, tensor, plane = lax.axis_size(FRAMES), lax.axis_size("tensor"), lax.axis_size(PLANE)
    plan = Plan(seq, tensor, clips_in.shape)
    width, wide = clips_in.shape[-1], cotangent.shape[-1]
    heads_a, heads_b = offsets_a.shape[0], offsets_b.shape[0]
    core = lax.axis_index("core")
    tokens, pooled, keys, memory = plan.tokens, plan.pooled, plan.keys, plan.memory
    order = jnp.asarray(plan.arrange(), BF16)
    home = ("tensor",) + FRAMES
    leaving = jnp.concatenate(
        [clips_in.reshape(plan.group, -1, width), cotangent.reshape(plan.group, -1, width)], axis=1
    )
    arrived = spread(swap(leaving), home)
    half = jnp.where(core == 0, expand_a, reduce_a)
    quarter = half.reshape(2, -1, half.shape[1])[lax.axis_index("near")]
    quarter, arrived = lax.optimization_barrier((quarter, arrived))
    mine = [exchange(quarter, "tensor", k) for k in range(1, tensor)]
    arrived = arrived.reshape(-1, width)
    pair = lambda w: [((pooled, 2 * w), BF16)] + [((memory // seq, 2 * w), BF16)] * plan.local_squeeze
    x, cot, n_a, q_a, *pair_a = call(
        "enter",
        functools.partial(enter_body, plan),
        [((tokens, width), BF16), ((pooled, wide), BF16), ((tokens, width), BF16), ((tokens, width), BF16),
         *pair(width)],
        [arrived, order, attend_gain_a, project_a, pooling_a, squeeze_a],
    )
    pairs_a = share_pairs(plan, pair_a, squeeze_a)
    hidden = [((tensor, width, expand_a.shape[1]), BF16), ((tensor, reduce_a.shape[0], width), BF16)]
    mine, pairs_a[2] = lax.optimization_barrier((mine, pairs_a[2]))
    mine = jnp.concatenate(mine, axis=0)
    weights = [mine, exchange(mine, "near", 1)]
    weights, cots, pairs_a = lax.optimization_barrier((weights, cot, pairs_a))
    weights = weights + [to_core(each) for each in weights]
    cots = [cot] + [exchange(cots, "tensor", k) for k in range(1, tensor)]
    or_a, m_a, l_a, probs_a = call(
        "first",
        functools.partial(first_body, plan, heads_a),
        [((tokens, width), BF16), ((tokens, width), F32), ((tokens, width), BF16), ((heads_a * tokens, keys), BF16)],
        [x, q_a, *pairs_a, offsets_a, output_a, mixer_gain_a],
        [resets, videos],
        [((8, 128), F32)],
    )
    y_a, n_b, q_b, base, *pair_b = call(
        "between",
        functools.partial(between_body, plan),
        [((tokens, width), F32), ((tokens, width), BF16), ((pooled, wide), BF16), ((pooled, wide), F32), *pair(wide)],
        [m_a, l_a, expand_a, reduce_a, *weights, attend_gain_b, project_b, pooling_b, squeeze_b, shortcut_b],
        (),
        hidden,
    )
    pair_b, cots = lax.optimization_barrier((pair_b, cots))
    pairs_b = share_pairs(plan, pair_b, squeeze_b)
    or_b, m_b, l_b, probs_b = call(
        "second",
        functools.partial(second_body, plan, heads_b),
        [((pooled, wide), BF16), ((pooled, wide), F32), ((pooled, wide), BF16), ((heads_b * pooled, keys), BF16)],
        [q_b, *pairs_b, offsets_b, output_b, mixer_gain_b, base],
        [resets, videos],
        [((8, 128), F32)],
    )
    rows_b = [exchange(l_b, "tensor", k) if k else l_b for k in range(tensor)]
    hidden_rows = (expand_b.shape[1] // LANES) * wide + (wide // LANES) * reduce_b.shape[0]
    half_plane = plane // 2
    hidden_each = padded(hidden_rows, plane)
    units = ((tensor * pooled, expand_b.shape[1]), BF16)
    *shares, hidden_b, grad_pre_b = call(
        "hidden",
        functools.partial(hidden_body, tensor),
        [((pooled, wide), BF16)] * tensor + [units, units],
        [expand_b, reduce_b, *rows_b, *cots],
    )
    sums = everyone(shares, "tensor")
    bias = lambda: [((plan.frames, 8, keys), F32)]
    key_grads = lambda w: (
        [((pooled, 2 * w), F32)] + [((pooled, 2 * w), BF16)] * (seq - 1) + [((memory, 2 * w), BF16)] * 2
    )
    dm_b, dmid_b, doutput_b, dq_b, dtable_b, *back = call(
        "second_back",
        functools.partial(second_back_body, plan, heads_b),
        [((pooled, wide), F32), ((1, wide), F32), ((wide, wide), BF16), ((pooled, wide), F32),
         ((8, 128), F32), *key_grads(wide)],
        [*sums, cot, m_b, mixer_gain_b, or_b, output_b, q_b, probs_b, *pairs_b],
        [resets, videos],
        bias(),
    )
    pieces, dsqueeze_given = return_pairs(plan, back, pairs_b, squeeze_b)
    share = width // tensor
    cross_each = padded((3 + 1) * wide // LANES * share + wide // LANES * (wide // tensor), plane)
    dy_a, dpool_b, dsqueeze_b, dgain_b, keep, give = call(
        "cross",
        functools.partial(cross_body, plan, cross_each),
        [((tokens, width), F32), ((3, 4, wide), F32), ((2, 4, wide), F32), ((1, width), F32)],
        [*pieces, dq_b, dm_b, doutput_b, n_b, y_a, attend_gain_b, project_b, pooling_b, squeeze_b, shortcut_b],
        stage=(2, half_plane, tensor, cross_each, LANES),
    )
    cross = (keep, give)
    hidden_b = after(hidden_b, dgain_b)
    *out_shares, keep, give = call(
        "hidden_rest",
        functools.partial(hidden_rest_body, tensor, hidden_each),
        [((pooled, wide), BF16)] * tensor,
        [reduce_b, hidden_b, grad_pre_b, *rows_b, *cots],
        stage=(2, half_plane, 1, hidden_each, LANES),
    )
    early = (keep, give)
    early, cross = sum_cores(*early), sum_cores(*cross)
    early = [part.reshape(half_plane, -1, LANES) for part in (early, cross)]
    early, dy_a = lax.optimization_barrier((jnp.concatenate(early, axis=1), dy_a))
    early = spread(early, ACROSS)
    first_each = padded(2 * width, plane)
    dmid_a, dm_a, doutput_a, dq_a, dtable_a, *back, keep, give = call(
        "first_back",
        functools.partial(first_back_body, plan, first_each, heads_a),
        [((1, width), F32), ((tokens, width), F32), ((width, width), BF16), ((tokens, width), F32), ((8, 128), F32),
         *key_grads(width)],
        [dy_a, m_a, l_a, mixer_gain_a, or_a, output_a, q_a, probs_a, expand_a, reduce_a, *weights,
         *pairs_a],
        [resets, videos],
        hidden + bias(),
        stage=(2, half_plane, tensor, first_each, LANES),
    )
    if dsqueeze_given is not None:
        dsqueeze_b = dsqueeze_given
    pieces, dsqueeze_given = return_pairs(plan, back, pairs_a, squeeze_a)
    out_sums = everyone(out_shares, "tensor")
    first = sum_cores(keep, give)
    tail_each, small_each = padded(4 * share, plane), padded(128, plane)
    grad_x, keep, give = call(
        "leave",
        functools.partial(leave_body, plan, tail_each, small_each),
        [((tokens, width), BF16)],
        [*pieces, dq_a, dm_a, doutput_a, n_a, x, attend_gain_a, project_a, pooling_a, squeeze_a, dmid_a, dtable_a,
         dgain_b, dpool_b, dsqueeze_b, dmid_b, dtable_b]
        + ([] if dsqueeze_given is None else [dsqueeze_given]),
        (),
        [((2, 4, width), F32), ((2, 4, width), F32), ((128, LANES), F32)],
        stage=(2, half_plane, 1, tensor * tail_each + small_each, LANES),
    )
    last = sum_cores(keep, give)
    last = jnp.concatenate([first.reshape(half_plane, -1, LANES), last[:, 0]], axis=1)
    last, early = lax.optimization_barrier((last, early))
    leaving, = call("exit", exit_body, [(arrived.shape, BF16)], [order, after(grad_x, last), m_b, *out_sums])
    last = spread(last, ACROSS)
    early = sum_first(early)
    cross = halve(early[hidden_each:].reshape(tensor, cross_each, LANES), "tensor")
    early = gather_across(jnp.concatenate([early[:hidden_each], cross], axis=0))
    last, cross, leaving = lax.optimization_barrier((last, cross, leaving))
    last = sum_first(last)
    first_rows = tensor * first_each
    first = last[:first_rows].reshape(tensor, first_each, LANES)
    small = jnp.broadcast_to(last[None, first_rows + tensor * tail_each :], (tensor, small_each, LANES))
    last = last[first_rows : first_rows + tensor * tail_each].reshape(tensor, tail_each, LANES)
    last = jnp.concatenate([first, last, small], axis=1)
    leaving = after(leaving, last)
    last = gather_across(halve(last, "tensor"))
    returned, early = lax.optimization_barrier((spread(leaving.reshape(plan.group, -1, width), home), early))
    returned, early = swap(returned), both_cores(early)
    x_rows = plan.frames * plan.rows * plan.cols
    grad_input = returned[:, :x_rows].reshape(clips_in.shape).astype(F32)
    result = returned[:, x_rows:].reshape(cotangent.shape).astype(F32)
    column = lambda rows, columns: ((rows, columns), F32)
    grad_expand_b, grad_reduce_b, grad_project_b, grad_shortcut_b, grad_output_b = call(
        "unpack_early",
        functools.partial(unpack_body, [(hidden_each, 2), (cross_each, 3)]),
        [
            (expand_b.shape, F32), (reduce_b.shape, F32),
            column(share, 3 * wide), column(share, wide), column(wide // tensor, wide),
        ],
        early,
        (),
        [((2, half_plane, hidden_each + cross_each, LANES), BF16)],
    )
    last, grad_expand_b, grad_input, result = lax.optimization_barrier((last, grad_expand_b, grad_input, result))
    last = both_cores(last)
    grad_expand_a, grad_reduce_a, grad_project_a, grad_output_a, *small = call(
        "unpack_last",
        functools.partial(unpack_body, [(first_each, 2), (tail_each, 2)]),
        [
            (expand_a.shape, F32), (reduce_a.shape, F32), column(share, 3 * width), column(share, width),
            ((width,), F32), (pooling_a.shape, F32), (squeeze_a.shape, F32), (offsets_a.shape, F32), ((width,), F32),
            ((width,), F32), (pooling_b.shape, F32), (squeeze_b.shape, F32), (offsets_b.shape, F32), ((wide,), F32),
        ],
        last,
        (),
        [((128, LANES), F32), ((2, half_plane, first_each + tail_each + small_each, LANES), BF16)],
    )
    return (
        result,
        grad_input,
        small[0],
        grad_project_a,
        small[1],
        small[2],
        small[3],
        grad_output_a,
        small[4],
        grad_expand_a,
        grad_reduce_a,
        small[5],
        grad_project_b,
        small[6],
        small[7],
        small[8],
        grad_output_b,
        grad_shortcut_b,
        small[9],
        grad_expand_b,
        grad_reduce_b,
    )


def solution(mesh):
    clip, seq, tensor = mesh.devices.shape
    split = Mesh(mesh.devices.reshape(clip // 2, 2, seq // 2, 2, tensor), EVERY)
    field = P(("chip", "core"), None, ("far", "near"), "tensor", None)
    up, down = P(None, "tensor"), P("tensor", None)
    block = (P(), P(), P(), P(), P(), P(), P(), up, down)
    block_b = (P(), P(), P(), P(), P(), P(), P(), P(), up, down)
    grads = (P(), down, P(), P(), P(), down, P(), up, down)
    grads_b = (P(), down, P(), P(), P(), down, down, P(), up, down)
    return jax.shard_map(
        local,
        mesh=split,
        in_specs=(field, field, P(), P()) + block + block_b,
        out_specs=(field, field) + grads + grads_b,
        check_vma=False,
    )
```
